32 devices in a mesh: obs: 8 (over y, x, core), rows: 4 (over z).
Axes of the slice: x: 2, y: 2, z: 4, core: 2. Of those that a mesh axis runs over, the one named last changes fastest.
Arguments:
- state: float32 [8192, 256], P(('obs', 'rows')), may hold values from -6 to 6
- foot_tiles: int32 [192, 4], P('obs'), may hold values from 0 to 3
- foot_weight: float32 [192, 4, 256], P('obs'), may hold values from -0.25 to 0.25
- azimuth: float32 [768], P('obs'), may hold values from -3.140625 to 3.140625
- obs_value: float32 [768], replicated, may hold values from 0.5 to 2.5
- obs_var: float32 [768], replicated, may hold values from 0.3 to 3
- tile_bin: int32 [32, 768], P(('obs', 'rows')), may hold values from 0 to 14
- obs_bin: int32 [768, 768], P('obs'), may hold values from 0 to 14
- order: int32 [768], replicated, may hold values from 0 to 767, as said below
Outputs:
- analysis: float32 [8192, 256], P(('obs', 'rows'))
The draws below stay inside these ranges and needn't reach their ends.
Inputs may be any that keep to these rules, and one draw needn't show every extreme that they name: foot_tiles numbers a tile among the 4 tiles of the footprint's own observation group. `order`: a permutation of the observables; each aligned block of 128 entries is one batch, and every batch holds equally many observables of each observation group (the 96 observables of group g are g * 96 to g * 96 + 95).
All inputs are finite; a program needn't handle non-finite values.
Results may differ from the reference program's by a relative error of at most 0.0003.
Values sent between devices are 32-bit elements; how exact they have to be, the bound alone decides.
A program may use at most 64 MiB of HBM per device.

```python
import math
import jax
import jax.numpy as jnp
from jax import lax

MEMBERS = 256
BATCH = 128
BATCHES = 6
TILE = 256
FOOT = 4
RADIUS = 8
NROWS = 8192
NTILES = 32
TILES_GRP = 4
NOBS = 768
NFOOT = 192
FOOT_GRP = 24
OBS_GRP = 96


def cycle_bins(key, first_group, second_group, groups):
    apart = jnp.abs(first_group[:, None] - second_group[None, :])
    cycle = jnp.minimum(apart, groups - apart)
    extra = jax.random.randint(key, cycle.shape, 0, 3, dtype=jnp.int32)
    return (3 * cycle + extra).astype(jnp.int32)


def draw_tile_bin(key, part):
    groups = NOBS // OBS_GRP
    tile_group = jnp.arange(NTILES, dtype=jnp.int32) // TILES_GRP
    obs_group = jnp.arange(NOBS, dtype=jnp.int32) // OBS_GRP
    return cycle_bins(jax.random.fold_in(key, 11), tile_group, obs_group, groups)


def draw_obs_bin(key, part):
    groups = NOBS // OBS_GRP
    obs_group = jnp.arange(NOBS, dtype=jnp.int32) // OBS_GRP
    return cycle_bins(jax.random.fold_in(key, 23), obs_group, obs_group, groups)


def draw_order(key, part):
    groups = NOBS // OBS_GRP
    per_batch = OBS_GRP // BATCHES
    group_key, batch_key = jax.random.split(jax.random.fold_in(key, 37))
    within = jax.vmap(lambda single: jax.random.permutation(single, OBS_GRP))(jax.random.split(group_key, groups)).astype(jnp.int32)
    members = within + (jnp.arange(groups, dtype=jnp.int32) * OBS_GRP)[:, None]
    spread = members.reshape(groups, per_batch, BATCHES).transpose(2, 1, 0).reshape(BATCHES, BATCH)
    shuffle = jax.vmap(lambda single: jax.random.permutation(single, BATCH))(jax.random.split(batch_key, BATCHES)).astype(jnp.int32)
    mixed = jnp.take_along_axis(spread, shuffle, axis=1)
    return mixed.reshape(NOBS).astype(jnp.int32)


def plant(array, stream_key, low, largest):
    dims = array.shape
    place = [jax.random.randint(jax.random.fold_in(stream_key, axis), (), 0, dims[axis]) for axis in range(len(dims))]
    array = array.at[tuple(place)].set(low)
    longest = dims.index(max(dims))
    place[longest] = (place[longest] + 1) % dims[longest]
    return array.at[tuple(place)].set(largest)


def level_of(own_key, extent, cuts, least, top_value):
    loudness, own = 1.0, jax.random.fold_in(own_key, 6)
    for dim, blocks in cuts:
        heights = jnp.exp(jax.random.uniform(jax.random.fold_in(own, dim), (blocks,), jnp.float32, least / len(cuts), top_value / len(cuts)))
        loudness = loudness * jnp.repeat(heights, extent[dim] // blocks).reshape([-1 if axis == dim else 1 for axis in range(len(extent))])
    return loudness


def normal_values(stream_key, dims, scale, bound, cuts=(), kind=jnp.bfloat16):
    loudness = level_of(stream_key, dims, cuts, -0.22, 0.18) if cuts else 1.0
    result = jax.random.normal(stream_key, dims, jnp.float32) * scale * loudness
    return jnp.minimum(jnp.maximum(result, -bound), bound).astype(kind)


def setup_inputs(seed: int = 0) -> dict:
    keys = jax.random.split(jax.random.key(seed), 10)
    return {
        "state": normal_values(keys[0], (NROWS, MEMBERS), 1.0, 6.0, ((0, 32),), jnp.float32),
        "foot_tiles": plant(jax.random.randint(keys[1], (NFOOT, FOOT), 0, TILES_GRP), jax.random.fold_in(keys[1], 1), 0, TILES_GRP - 1).astype(jnp.int32),
        "foot_weight": normal_values(keys[2], (NFOOT, FOOT, TILE), (FOOT * TILE // 2) ** -0.5, 0.25, ((0, 8),), jnp.float32),
        "azimuth": jnp.clip(jax.random.uniform(keys[3], (NOBS,), jnp.float32, -3.140625, 3.140625), -3.140625, 3.140625),
        "obs_value": jnp.clip(jax.random.uniform(keys[4], (NOBS,), jnp.float32, 0.5, 2.5), 0.5, 2.5),
        "obs_var": jnp.clip(jnp.exp(jax.random.uniform(keys[5], (NOBS,), jnp.float32, math.log(0.3), math.log(3.0))), 0.3, 3.0),
        "tile_bin": draw_tile_bin(jax.random.fold_in(keys[9], 71), 0),
        "obs_bin": draw_obs_bin(jax.random.fold_in(keys[9], 71), 0),
        "order": draw_order(jax.random.fold_in(keys[9], 71), 0),
    }


HIGH = lax.Precision.HIGHEST

def model_function(east_wind, north_wind, angles):
    speed = jnp.sqrt(east_wind * east_wind + north_wind * north_wind + 1.0)
    cosine = (east_wind * jnp.cos(angles) + north_wind * jnp.sin(angles)) / speed
    return jnp.exp(0.6 * jnp.log(speed)) * (0.7 + 0.4 * cosine + 0.6 * cosine * cosine)

def taper_weight(bins):
    scaled = 1.0 - bins.astype(jnp.float32) / RADIUS
    return jnp.where(bins < RADIUS, scaled * scaled, jnp.zeros_like(scaled))

def batch_gains(batch_obs, values, variances):
    row_mean = lax.optimization_barrier(jnp.mean(batch_obs, axis=1))
    perturb = batch_obs - row_mean[:, None]
    innov = values - row_mean
    covariance = jnp.dot(perturb.astype(jnp.float32), perturb.T.astype(jnp.float32), precision=HIGH, preferred_element_type=jnp.float32) / (MEMBERS - 1) + jnp.diag(variances)
    factor = jnp.linalg.cholesky(covariance)
    middle = jax.scipy.linalg.solve_triangular(factor, innov, lower=True)
    solved = jax.scipy.linalg.solve_triangular(factor, middle, lower=True, trans=1)
    eye_matrix = jnp.eye(BATCH, dtype=jnp.float32)
    shifted = factor + jnp.diag(jnp.sqrt(variances))
    inverse = jax.scipy.linalg.solve_triangular(shifted, eye_matrix, lower=True)
    gain_matrix = jax.scipy.linalg.solve_triangular(factor, inverse, lower=True, trans=1)
    return (perturb, solved, gain_matrix)

def localised(ensemble, weights, rows_per, perturb, solved, gain_matrix):
    row_mean = lax.optimization_barrier(jnp.mean(ensemble, axis=1, keepdims=True))
    deviation = ensemble - row_mean
    product = jnp.dot(deviation.astype(jnp.float32), perturb.T.astype(jnp.float32), precision=HIGH, preferred_element_type=jnp.float32) / (MEMBERS - 1)
    product = (product.reshape(-1, rows_per, BATCH) * weights[:, None, :]).reshape(product.shape)
    row_mean = row_mean + jnp.dot(product.astype(jnp.float32), solved[:, None].astype(jnp.float32), precision=HIGH, preferred_element_type=jnp.float32)
    mixed = jnp.dot(product.astype(jnp.float32), gain_matrix.astype(jnp.float32), precision=HIGH, preferred_element_type=jnp.float32)
    deviation = deviation - jnp.dot(mixed.astype(jnp.float32), perturb.astype(jnp.float32), precision=HIGH, preferred_element_type=jnp.float32)
    return row_mean + deviation

def reference(state, foot_tiles, foot_weight, azimuth, obs_value, obs_var, tile_bin, obs_bin, order):
    half_tile = TILE // 2
    tiles = state.reshape(NTILES, 2, half_tile, MEMBERS)
    group_start = jnp.arange(NFOOT, dtype=jnp.int32) // FOOT_GRP * TILES_GRP
    global_tiles = (foot_tiles + group_start[:, None]).astype(jnp.int32)

    def footprint(inputs):
        listed, weights = inputs
        picked_tiles = tiles[listed]
        return jnp.einsum('thc,thcm->hm', weights.reshape(FOOT, 2, half_tile), picked_tiles, precision=HIGH)
    wind_sums = lax.map(footprint, (global_tiles, foot_weight))
    angles = azimuth.reshape(NFOOT, 4)
    observed = model_function(wind_sums[:, 0, None, :], wind_sums[:, 1, None, :], angles[:, :, None]).reshape(NOBS, MEMBERS)

    def batch_step(carry, batch_num):
        ensemble, observed = carry
        picked = lax.dynamic_slice_in_dim(order, batch_num * BATCH, BATCH).astype(jnp.int32)
        perturb, solved, gain_matrix = batch_gains(observed[picked], obs_value[picked], obs_var[picked])
        ensemble = localised(ensemble, taper_weight(tile_bin[:, picked]), TILE, perturb, solved, gain_matrix)
        observed = localised(observed, taper_weight(obs_bin[:, picked]), 1, perturb, solved, gain_matrix)
        return ((ensemble, observed), None)
    (ensemble, observed), unused = lax.scan(batch_step, (state, observed), jnp.arange(BATCHES, dtype=jnp.int32))
    return ensemble
```

```python
import functools

import jax
import jax.numpy as jnp
from jax import lax
from jax.experimental import pallas as pl
from jax.experimental.pallas import tpu as pltpu
from jax.sharding import PartitionSpec as P

MEMBERS = 256
BATCH = 128
TILE = 256
RADIUS = 8
SUB = 8
STAGES = 8
F32 = jnp.float32
BF16 = jnp.bfloat16


HIGH = lax.Precision.HIGHEST
MESH = pl.DeviceIdType.MESH
VMEM = pl.BlockSpec(memory_space=pltpu.VMEM)


def model_function(east_wind, north_wind, cosines, sines):
    speed = jnp.sqrt(east_wind * east_wind + north_wind * north_wind + 1.0)
    cosine = (east_wind * cosines + north_wind * sines) / speed
    return jnp.exp(0.6 * jnp.log(speed)) * (0.7 + 0.4 * cosine + 0.6 * cosine * cosine)


def taper_weight(bins):
    scaled = 1.0 - bins.astype(F32) / RADIUS
    return jnp.where(bins < RADIUS, scaled * scaled, jnp.zeros_like(scaled))


def halves(value):
    high = value.astype(BF16)
    return high, (value - high.astype(F32)).astype(BF16)


def dot3(left, right, dims):
    (left_hi, left_lo), (right_hi, right_lo) = left, right
    (left_dim,), (right_dim,) = dims
    return lax.dot_general(
        jnp.concatenate([left_hi, left_lo, left_hi], left_dim),
        jnp.concatenate([right_hi, right_hi, right_lo], right_dim),
        (dims, ((), ())),
        preferred_element_type=F32,
    )


NN = ((1,), (0,))
NT = ((1,), (1,))
TN = ((0,), (0,))


def total(terms):
    while len(terms) > 1:
        terms = [a + b for a, b in zip(terms[::2], terms[1::2])]
    return terms[0]


def factor(panel, roots, upper, stage):
    blocks, half = BATCH // SUB, BATCH // 2
    lane = lax.broadcasted_iota(jnp.int32, (SUB, BATCH), 1)
    sub = lax.broadcasted_iota(jnp.int32, (SUB, BATCH), 0)
    left, right = pl.ds(0, BATCH), pl.ds(BATCH, BATCH)

    def across(value, column):
        lanes = jnp.full((SUB, BATCH), column, jnp.int32)
        return jnp.take_along_axis(value, lanes, axis=1, mode="promise_in_bounds")

    def down(value, row):
        return jnp.broadcast_to(value[row : row + 1, :], (SUB, BATCH))

    def rows(i):
        return pl.ds(SUB * i, SUB)

    for b in range(blocks):
        base = SUB * b
        end = blocks if base >= half else blocks // 2
        inside = jnp.logical_and(lane >= base, lane < base + SUB)
        start = panel[rows(b), left]
        given = panel[rows(b), right]
        root = roots[rows(b), :]
        cols = [across(start, base + k) for k in range(SUB)]
        for i in range(b + 1, end):
            value = panel[rows(i), left]
            for k in range(SUB):
                stage[i % STAGES, k] = across(value, base + k)
        solved = jnp.where(inside, (lane == sub + base).astype(F32), start)
        forward, scale, diagonal, steps = solved, None, None, []
        for k in range(0, SUB, 2):
            one, two = sub == k, sub == k + 1
            pair, below = jnp.logical_or(one, two), sub > k + 1
            u, v = cols[k], cols[k + 1]
            a, e, c = down(u, k), down(u, k + 1), down(v, k + 1)
            det = a * c - e * e
            inv_det_root, inv_root = lax.rsqrt(det), lax.rsqrt(a)
            inv = inv_det_root * inv_det_root
            p = jnp.where(one, -c, jnp.where(two, e, c * u - e * v))
            q = jnp.where(one, e, jnp.where(two, -a, a * v - e * u))
            for m in range(k + 2, SUB):
                cols[m] = jnp.where(pair, 0.0, cols[m]) - (p * down(u, m) + q * down(v, m)) * inv
            full_p, full_q = p * inv, q * inv
            solved = jnp.where(pair, 0.0, solved) - (full_p * down(solved, k) + full_q * down(solved, k + 1))
            ratio = e * (inv_root * inv_root)
            part_p = jnp.where(below, full_p, jnp.where(two, ratio, 0.0))
            part_q = jnp.where(below, full_q, 0.0)
            forward = forward - (part_p * down(forward, k) + part_q * down(forward, k + 1))
            second_scale = inv_det_root * (a * inv_root)
            diag_one, diag_two = a * inv_root, det * inv_det_root * inv_root
            if k == 0:
                scale, diagonal = jnp.where(one, inv_root, second_scale), jnp.where(one, diag_one, diag_two)
            else:
                scale = jnp.where(one, inv_root, jnp.where(two, second_scale, scale))
                diagonal = jnp.where(one, diag_one, jnp.where(two, diag_two, diagonal))
            steps.append((k, full_p, full_q, pair, u * inv_root, (v - u * ratio) * second_scale, one, two, below))
        forward = forward * scale
        lower = jnp.where(lane <= sub + base, forward, 0.0)
        panel[rows(b), left] = lower
        if base < half:
            upper[rows(b), :] = jnp.where(lane < half, lower, forward)
        gain = 1.0 / (diagonal + root)
        own = given
        for k, _, _, _, low, next_low, one, two, below in steps:
            first = down(own, k) * down(gain, k)
            second = (down(own, k + 1) - down(low, k + 1) * first) * down(gain, k + 1)
            rest = own - (low * first + next_low * second)
            own = jnp.where(below, rest, jnp.where(one, first, jnp.where(two, second, own)))
        panel[rows(b), right] = own
        if b + 1 < end:
            spread = given - root * own
            for k, full_p, full_q, pair, *_ in steps:
                spread = jnp.where(pair, 0.0, spread) - (full_p * down(spread, k) + full_q * down(spread, k + 1))
            for i in range(b + 1, end):
                columns = [stage[i % STAGES, k] for k in range(SUB)]
                value = jnp.where(inside, 0.0, panel[rows(i), left])
                panel[rows(i), left] = value - total([columns[k] * down(solved, k) for k in range(SUB)])
                panel[rows(i), right] = panel[rows(i), right] - total([columns[k] * down(spread, k) for k in range(SUB)])
        elif end < blocks:
            far = pl.ds(half, half)
            outer = halves(upper[...])
            wide = lax.broadcasted_iota(jnp.int32, (half, BATCH), 1)
            change = dot3(outer, outer, TN)[half:, :]
            panel[far, left] = jnp.where(wide < half, 0.0, panel[far, left]) - change
            change = dot3(outer, halves(panel[:half, right]), TN)[half:, :]
            panel[far, right] = panel[far, right] - change


def filter_kernel(
    group_size, state_ref, obs_ref, taper_ref, tile_ref, given_ref, order_ref, order_row_ref, out_ref, held, weights, picked_given,
    panel, roots, upper, stage,
):
    nobs = obs_ref.shape[0]
    batches = nobs // BATCH
    tiles_dev = tile_ref.shape[0]
    index = lax.broadcasted_iota(jnp.int32, (BATCH, nobs), 1)
    dot = functools.partial(jnp.dot, preferred_element_type=F32)

    lane = lax.broadcasted_iota(jnp.int32, (BATCH, BATCH), 1)
    before = lane < lax.broadcasted_iota(jnp.int32, (BATCH, BATCH), 0)

    def pick(select, value):
        high, rest = halves(value)
        low = (value - high.astype(F32) - rest.astype(F32)).astype(BF16)
        return dot(select, high) + (dot(select, rest) + dot(select, low))

    def arrange(num, carry):
        rows = pl.ds(pl.multiple_of(num * BATCH, BATCH), BATCH)
        wanted = order_ref[rows, :]
        select = (wanted == index).astype(F32).astype(BF16)
        picked_given[rows, :] = pick(select, given_ref[...])
        group = wanted // group_size
        same = jnp.logical_and(before, group == order_row_ref[:, rows] // group_size)
        earlier = jnp.sum(same.astype(F32), axis=1, keepdims=True).astype(jnp.int32)
        place = group * (group_size // batches) + earlier
        select = (place == lane).astype(F32).astype(BF16)
        held[rows, :] = pick(select, obs_ref[rows, :])
        weights[rows, :] = dot(select, taper_ref[rows, :].astype(BF16))
        return carry

    lax.fori_loop(0, batches, arrange, 0)
    out_ref[...] = state_ref[...]
    eye = lax.broadcasted_iota(jnp.int32, (BATCH, BATCH), 0) == lax.broadcasted_iota(
        jnp.int32, (BATCH, BATCH), 1
    )

    def batch_step(num, carry):
        rows = pl.ds(pl.multiple_of(num * BATCH, BATCH), BATCH)
        batch_obs = held[rows, :]
        row_mean = jnp.mean(batch_obs, axis=1, keepdims=True)
        perturb = batch_obs - row_mean
        given = picked_given[rows, :]
        innov = given[:, 0:1] - row_mean
        variance = given[:, 1:2]
        roots[...] = jnp.broadcast_to(jnp.sqrt(variance), (BATCH, BATCH))
        split = halves(perturb)
        scaled = halves(perturb * (1.0 / (MEMBERS - 1)))
        panel[:, :BATCH] = dot3(split, scaled, NT) + jnp.where(eye, variance, 0.0)
        panel[:, BATCH:] = eye.astype(F32)
        factor(panel, roots, upper, stage)
        first = halves(panel[:, :BATCH])
        second = panel[:, BATCH:]
        middle = dot3(first, halves(jnp.broadcast_to(innov, (BATCH, MEMBERS))), NN) - dot3(
            halves(second), split, NN
        )
        change = halves(dot3(first, halves(middle), TN))

        def update(ref, place, weight):
            value = ref[place, :]
            product = dot3(halves(value), scaled, NT) * weight
            ref[place, :] = value + dot3(halves(product), change, NN)

        def update_obs(other, inner):
            place = pl.ds(pl.multiple_of(other * BATCH, BATCH), BATCH)
            update(held, place, weights[place, rows])
            return inner

        lax.fori_loop(num + 1, batches, update_obs, 0)
        for tile in range(tiles_dev):
            update(out_ref, pl.ds(tile * TILE, TILE), tile_ref[tile : tile + 1, rows])
        return carry

    lax.fori_loop(0, batches, batch_step, 0)


def filter_all(state, every_obs, taper, tile_taper, given, order, group_size):
    nobs = every_obs.shape[0]
    return pl.pallas_call(
        functools.partial(filter_kernel, group_size),
        out_shape=jax.ShapeDtypeStruct(state.shape, F32),
        in_specs=[VMEM] * 7,
        out_specs=VMEM,
        scratch_shapes=[
            pltpu.VMEM((nobs, MEMBERS), F32),
            pltpu.VMEM((nobs, nobs), F32),
            pltpu.VMEM((nobs, given.shape[1]), F32),
            pltpu.VMEM((BATCH, 2 * BATCH), F32),
            pltpu.VMEM((BATCH, BATCH), F32),
            pltpu.VMEM((BATCH // 2, BATCH), F32),
            pltpu.VMEM((STAGES, SUB, SUB, BATCH), F32),
        ],
        compiler_params=pltpu.CompilerParams(vmem_limit_bytes=48 * 1024 * 1024),
    )(state, every_obs, taper, tile_taper, given, order[:, None], order[None, :])


def exchange_kernel(
    groups, layers, state_ref, tiles_ref, weight_ref, cos_ref, sin_ref, order_ref, bins_ref, tile_bin_ref,
    obs_out, taper_out, tile_out, own_sums, sums, own_obs, own_taper,
    sum_send, sum_recv, obs_send, obs_recv, taper_send, taper_recv,
):
    me, layer = lax.axis_index("obs"), lax.axis_index("rows")
    feet, batches, per = tiles_ref.shape[0], own_obs.shape[0], own_obs.shape[1]
    count, nobs = bins_ref.shape
    tiles_dev, half = tile_bin_ref.shape[0], TILE // 2
    barrier = pltpu.get_barrier_semaphore()
    for k in range(1, groups):
        pl.semaphore_signal(barrier, inc=1, device_id={"obs": lax.rem(me + k, groups)}, device_id_type=MESH)
    for k in range(1, layers):
        pl.semaphore_signal(barrier, inc=1, device_id={"rows": lax.rem(layer + k, layers)}, device_id_type=MESH)

    partial = [jnp.zeros((feet, MEMBERS), F32) for _ in range(2)]
    for tile in range(tiles_dev):
        number = layer * tiles_dev + tile
        factor = jnp.zeros((feet, TILE), F32)
        for t in range(tiles_ref.shape[1]):
            factor = factor + jnp.where(tiles_ref[:, t : t + 1] == number, weight_ref[:, t, :], 0.0)
        for h in range(2):
            partial[h] = partial[h] + jnp.dot(
                factor[:, h * half : (h + 1) * half],
                state_ref[pl.ds(tile * TILE + h * half, half), :],
                precision=HIGH,
                preferred_element_type=F32,
            )
    for h in range(2):
        own_sums[h] = partial[h]
    pl.semaphore_wait(barrier, groups + layers - 2)

    sum_copies = []
    for k in range(1, layers):
        copy = pltpu.make_async_remote_copy(
            own_sums, sums.at[k], sum_send.at[k], sum_recv.at[k],
            device_id={"rows": lax.rem(layer + k, layers)}, device_id_type=MESH,
        )
        copy.start()
        sum_copies.append(copy)

    order = order_ref[...]
    base = me * count
    steps = lax.broadcasted_iota(jnp.int32, (count, nobs), 1).astype(F32)
    member = jnp.logical_and(order >= base, order < base + count).astype(F32)
    local = lax.broadcasted_iota(jnp.int32, (count, 1), 0)
    column = lax.broadcasted_iota(jnp.int32, (count, count), 1)

    def ranks(ids):
        at = jnp.sum(jnp.where(order == base + ids, steps, 0.0), axis=1, keepdims=True)
        rank = jnp.sum(jnp.where(steps < at, member, 0.0), axis=1, keepdims=True)
        return (rank.astype(jnp.int32) == column).astype(F32)

    sorter = (lax.broadcasted_iota(jnp.int32, (nobs, nobs), 0) == order).astype(F32).astype(BF16)
    ordered = jnp.dot(taper_weight(bins_ref[...]).astype(BF16), sorter, preferred_element_type=F32)
    ordered = lax.dot_general(
        ranks(local).astype(BF16), ordered.astype(BF16), (TN, ((), ())), preferred_element_type=F32
    )
    for b in range(batches):
        own_taper[b] = ordered[b * per : (b + 1) * per, :]
        taper_out[b, me] = ordered[b * per : (b + 1) * per, :]
    cuts = [(b, 1) for b in range(1, batches)]
    taper_copies = []
    for k in range(1, groups):
        for c, (first, length) in enumerate(cuts):
            wide = pl.ds(0, (first + length - 1) * BATCH)
            copy = pltpu.make_async_remote_copy(
                own_taper.at[pl.ds(first, length), :, wide],
                taper_out.at[pl.ds(first, length), me, :, wide],
                taper_send.at[k, c], taper_recv.at[k, c],
                device_id={"obs": lax.rem(me + k, groups)}, device_id_type=MESH,
            )
            copy.start()
            taper_copies.append(copy)

    tile_out[...] = jnp.dot(taper_weight(tile_bin_ref[...]).astype(BF16), sorter, preferred_element_type=F32)
    chooser = ranks(local % feet * 4 + local // feet)
    for copy in sum_copies:
        copy.wait()
    winds = [own_sums[h] for h in range(2)]
    for k in range(1, layers):
        winds = [winds[h] + sums[k, h] for h in range(2)]
    observed = jnp.concatenate(
        [
            model_function(winds[0], winds[1], cos_ref[:, k : k + 1], sin_ref[:, k : k + 1])
            for k in range(cos_ref.shape[1])
        ],
        0,
    )
    observed = lax.dot_general(chooser, observed, (TN, ((), ())), precision=HIGH, preferred_element_type=F32)
    for b in range(batches):
        own_obs[b] = observed[b * per : (b + 1) * per, :]
        obs_out[b, me] = observed[b * per : (b + 1) * per, :]
    obs_copies = []
    for k in range(1, groups):
        copy = pltpu.make_async_remote_copy(
            own_obs, obs_out.at[:, me], obs_send.at[k], obs_recv.at[k],
            device_id={"obs": lax.rem(me + k, groups)}, device_id_type=MESH,
        )
        copy.start()
        obs_copies.append(copy)
    for copy in taper_copies + obs_copies:
        copy.wait()


def exchange(state, foot_tiles, foot_weight, cosines, sines, order_row, obs_bin, tile_bin):
    groups, layers = lax.axis_size("obs"), lax.axis_size("rows")
    count, nobs = obs_bin.shape
    batches, feet = nobs // BATCH, foot_tiles.shape[0]
    per = count // batches
    dma = pltpu.SemaphoreType.DMA
    return pl.pallas_call(
        functools.partial(exchange_kernel, groups, layers),
        out_shape=(
            jax.ShapeDtypeStruct((batches, groups, per, MEMBERS), F32),
            jax.ShapeDtypeStruct((batches, groups, per, nobs), F32),
            jax.ShapeDtypeStruct(tile_bin.shape, F32),
        ),
        in_specs=[VMEM] * 8,
        out_specs=(VMEM, VMEM, VMEM),
        scratch_shapes=[
            pltpu.VMEM((2, feet, MEMBERS), F32),
            pltpu.VMEM((layers, 2, feet, MEMBERS), F32),
            pltpu.VMEM((batches, per, MEMBERS), F32),
            pltpu.VMEM((batches, per, nobs), F32),
            dma((layers,)), dma((layers,)), dma((groups,)), dma((groups,)), dma((groups, batches)), dma((groups, batches)),
        ],
        compiler_params=pltpu.CompilerParams(
            collective_id=0, has_side_effects=True, vmem_limit_bytes=48 * 1024 * 1024
        ),
    )(state, foot_tiles, foot_weight, cosines, sines, order_row, obs_bin, tile_bin)


def shards(state, foot_tiles, foot_weight, azimuth, obs_value, obs_var, tile_bin, obs_bin, order):
    angles = azimuth.reshape(foot_tiles.shape[0], -1)
    every_obs, taper, tile_taper = exchange(
        state, foot_tiles, foot_weight, jnp.cos(angles), jnp.sin(angles), order[None, :], obs_bin, tile_bin
    )
    nobs = order.shape[0]
    given = jnp.stack([obs_value, obs_var], axis=1)
    return filter_all(
        state, every_obs.reshape(nobs, MEMBERS), taper.reshape(nobs, nobs), tile_taper, given, order, obs_bin.shape[0]
    )


def solution(mesh):
    return jax.shard_map(
        shards,
        mesh=mesh,
        in_specs=(
            P(("obs", "rows"), None),
            P("obs", None),
            P("obs", None, None),
            P("obs"),
            P(),
            P(),
            P(("obs", "rows"), None),
            P("obs", None),
            P(),
        ),
        out_specs=P(("obs", "rows"), None),
        check_vma=False,
    )
```

```python
import functools

import jax
import jax.numpy as jnp
from jax import lax
from jax.experimental import pallas as pl
from jax.experimental.pallas import tpu as pltpu
from jax.sharding import PartitionSpec as P

MEMBERS = 256
BATCH = 128
TILE = 256
RADIUS = 8
SUB = 8
STAGES = 8
F32 = jnp.float32
BF16 = jnp.bfloat16


HIGH = lax.Precision.HIGHEST
MESH = pl.DeviceIdType.MESH
VMEM = pl.BlockSpec(memory_space=pltpu.VMEM)
ANY = pl.BlockSpec(memory_space=pl.ANY)


def model_function(east_wind, north_wind, cosines, sines):
    speed = jnp.sqrt(east_wind * east_wind + north_wind * north_wind + 1.0)
    cosine = (east_wind * cosines + north_wind * sines) / speed
    return jnp.exp(0.6 * jnp.log(speed)) * (0.7 + 0.4 * cosine + 0.6 * cosine * cosine)


def taper_weight(bins):
    scaled = 1.0 - bins.astype(F32) / RADIUS
    return jnp.where(bins < RADIUS, scaled * scaled, jnp.zeros_like(scaled))


def halves(value):
    high = value.astype(BF16)
    return high, (value - high.astype(F32)).astype(BF16)


def dot3(left, right, dims):
    (left_hi, left_lo), (right_hi, right_lo) = left, right
    (left_dim,), (right_dim,) = dims
    return lax.dot_general(
        jnp.concatenate([left_hi, left_lo, left_hi], left_dim),
        jnp.concatenate([right_hi, right_hi, right_lo], right_dim),
        (dims, ((), ())),
        preferred_element_type=F32,
    )


NN = ((1,), (0,))
NT = ((1,), (1,))
TN = ((0,), (0,))


def total(terms):
    while len(terms) > 1:
        terms = [a + b for a, b in zip(terms[::2], terms[1::2])]
    return terms[0]


def factor(panel, roots, upper, stage):
    blocks, half = BATCH // SUB, BATCH // 2
    lane = lax.broadcasted_iota(jnp.int32, (SUB, BATCH), 1)
    sub = lax.broadcasted_iota(jnp.int32, (SUB, BATCH), 0)
    left, right = pl.ds(0, BATCH), pl.ds(BATCH, BATCH)

    def across(value, column):
        lanes = jnp.full((SUB, BATCH), column, jnp.int32)
        return jnp.take_along_axis(value, lanes, axis=1, mode="promise_in_bounds")

    def down(value, row):
        return jnp.broadcast_to(value[row : row + 1, :], (SUB, BATCH))

    def rows(i):
        return pl.ds(SUB * i, SUB)

    for b in range(blocks):
        base = SUB * b
        end = blocks if base >= half else blocks // 2
        inside = jnp.logical_and(lane >= base, lane < base + SUB)
        start = panel[rows(b), left]
        given = panel[rows(b), right]
        root = roots[rows(b), :]
        cols = [across(start, base + k) for k in range(SUB)]
        for i in range(b + 1, end):
            value = panel[rows(i), left]
            for k in range(SUB):
                stage[i % STAGES, k] = across(value, base + k)
        solved = jnp.where(inside, (lane == sub + base).astype(F32), start)
        forward, scale, diagonal, steps = solved, None, None, []
        for k in range(0, SUB, 2):
            one, two = sub == k, sub == k + 1
            pair, below = jnp.logical_or(one, two), sub > k + 1
            u, v = cols[k], cols[k + 1]
            a, e, c = down(u, k), down(u, k + 1), down(v, k + 1)
            det = a * c - e * e
            inv_det_root, inv_root = lax.rsqrt(det), lax.rsqrt(a)
            inv = inv_det_root * inv_det_root
            p = jnp.where(one, -c, jnp.where(two, e, c * u - e * v))
            q = jnp.where(one, e, jnp.where(two, -a, a * v - e * u))
            for m in range(k + 2, SUB):
                cols[m] = jnp.where(pair, 0.0, cols[m]) - (p * down(u, m) + q * down(v, m)) * inv
            full_p, full_q = p * inv, q * inv
            solved = jnp.where(pair, 0.0, solved) - (full_p * down(solved, k) + full_q * down(solved, k + 1))
            ratio = e * (inv_root * inv_root)
            part_p = jnp.where(below, full_p, jnp.where(two, ratio, 0.0))
            part_q = jnp.where(below, full_q, 0.0)
            forward = forward - (part_p * down(forward, k) + part_q * down(forward, k + 1))
            second_scale = inv_det_root * (a * inv_root)
            diag_one, diag_two = a * inv_root, det * inv_det_root * inv_root
            if k == 0:
                scale, diagonal = jnp.where(one, inv_root, second_scale), jnp.where(one, diag_one, diag_two)
            else:
                scale = jnp.where(one, inv_root, jnp.where(two, second_scale, scale))
                diagonal = jnp.where(one, diag_one, jnp.where(two, diag_two, diagonal))
            steps.append((k, full_p, full_q, pair, u * inv_root, (v - u * ratio) * second_scale, one, two, below))
        forward = forward * scale
        lower = jnp.where(lane <= sub + base, forward, 0.0)
        panel[rows(b), left] = lower
        if base < half:
            upper[rows(b), :] = jnp.where(lane < half, lower, forward)
        gain = 1.0 / (diagonal + root)
        own = given
        for k, _, _, _, low, next_low, one, two, below in steps:
            first = down(own, k) * down(gain, k)
            second = (down(own, k + 1) - down(low, k + 1) * first) * down(gain, k + 1)
            rest = own - (low * first + next_low * second)
            own = jnp.where(below, rest, jnp.where(one, first, jnp.where(two, second, own)))
        panel[rows(b), right] = own
        if b + 1 < end:
            spread = given - root * own
            for k, full_p, full_q, pair, *_ in steps:
                spread = jnp.where(pair, 0.0, spread) - (full_p * down(spread, k) + full_q * down(spread, k + 1))
            for i in range(b + 1, end):
                columns = [stage[i % STAGES, k] for k in range(SUB)]
                value = jnp.where(inside, 0.0, panel[rows(i), left])
                panel[rows(i), left] = value - total([columns[k] * down(solved, k) for k in range(SUB)])
                panel[rows(i), right] = panel[rows(i), right] - total([columns[k] * down(spread, k) for k in range(SUB)])
        elif end < blocks:
            far = pl.ds(half, half)
            outer = halves(upper[...])
            wide = lax.broadcasted_iota(jnp.int32, (half, BATCH), 1)
            change = dot3(outer, outer, TN)[half:, :]
            panel[far, left] = jnp.where(wide < half, 0.0, panel[far, left]) - change
            change = dot3(outer, halves(panel[:half, right]), TN)[half:, :]
            panel[far, right] = panel[far, right] - change


def pick(select, value):
    high, rest = halves(value)
    low = (value - high.astype(F32) - rest.astype(F32)).astype(BF16)
    dot = functools.partial(jnp.dot, preferred_element_type=F32)
    return dot(select, high) + (dot(select, rest) + dot(select, low))


def lookup(pieces, index):
    inner, outer = index % BATCH, index // BATCH
    found = jnp.zeros(index.shape, pieces[0].dtype)
    for q, piece in enumerate(pieces):
        piece = jnp.broadcast_to(piece, index.shape)
        piece = jnp.take_along_axis(piece, inner, axis=1, mode="promise_in_bounds")
        found = jnp.where(outer == q, piece, found)
    return found


def iota(shape, dim):
    return lax.broadcasted_iota(jnp.int32, shape, dim)


def column_of(row):
    size = row.shape[1]
    eye = iota((size, size), 0) == iota((size, size), 1)
    return jnp.sum(jnp.where(eye, row, jnp.zeros_like(row)), axis=1, keepdims=True)


def filter_kernel(
    groups, layers, state_hbm, tiles_hbm, weight_hbm, azimuth_hbm, value_hbm, var_hbm, tile_bin_hbm, bins_hbm,
    order_hbm, out_ref,
    tiles, weight, azimuth, values, variances, tile_bin, bins, order,
    own_sums, sums, own_obs, every_obs, own_taper, every_taper,
    held, weights, selects, value_cols, root_cols, var_rows, tile_weights, gathered,
    panel, upper, stage, scaled_all, change_all,
    load_sem, sum_send, sum_recv, obs_send, obs_recv, taper_send, taper_recv,
):
    me, layer = lax.axis_index("obs"), lax.axis_index("rows")
    feet = weight.shape[0]
    batches, per = own_obs.shape[0], own_obs.shape[1]
    count, nobs = bins.shape
    tiles_dev, half = tile_bin.shape[0], TILE // 2
    padded = var_rows.shape[0]

    pairs = [
        (order_hbm, order), (value_hbm, values), (var_hbm, variances), (azimuth_hbm, azimuth), (tiles_hbm, tiles),
        (tile_bin_hbm, tile_bin), (state_hbm, out_ref), (weight_hbm, weight), (bins_hbm, bins),
    ]
    loads = [pltpu.make_async_copy(source, target, load_sem.at[i]) for i, (source, target) in enumerate(pairs)]
    for load in loads:
        load.start()
    barrier = pltpu.get_barrier_semaphore()
    for k in range(1, groups):
        pl.semaphore_signal(barrier, inc=1, device_id={"obs": lax.rem(me + k, groups)}, device_id_type=MESH)
    for k in range(1, layers):
        pl.semaphore_signal(barrier, inc=1, device_id={"rows": lax.rem(layer + k, layers)}, device_id_type=MESH)
    for load in loads[:8]:
        load.wait()

    partial = [jnp.zeros((feet, MEMBERS), F32) for _ in range(2)]
    listed = [column_of(tiles[t : t + 1, :].astype(F32)).astype(jnp.int32) for t in range(tiles.shape[0])]
    for tile in range(tiles_dev):
        number = layer * tiles_dev + tile
        chosen = jnp.zeros((feet, TILE), F32)
        for t in range(tiles.shape[0]):
            chosen = chosen + jnp.where(listed[t] == number, weight[:, t, :], 0.0)
        for h in range(2):
            partial[h] = partial[h] + jnp.dot(
                chosen[:, h * half : (h + 1) * half],
                out_ref[pl.ds(tile * TILE + h * half, half), :],
                precision=HIGH,
                preferred_element_type=F32,
            )
    for h in range(2):
        own_sums[h] = partial[h]
    loads[8].wait()
    pl.semaphore_wait(barrier, groups + layers - 2)

    def sum_copy(k):
        return pltpu.make_async_remote_copy(
            own_sums, sums.at[k], sum_send.at[k], sum_recv.at[k],
            device_id={"rows": lax.rem(layer + k, layers)}, device_id_type=MESH,
        )

    def obs_copy(k, b):
        return pltpu.make_async_remote_copy(
            own_obs.at[b], every_obs.at[b, me], obs_send.at[k, b], obs_recv.at[k, b],
            device_id={"obs": lax.rem(me + k, groups)}, device_id_type=MESH,
        )

    def taper_copy(k, b):
        wide = pl.ds(0, b * BATCH)
        return pltpu.make_async_remote_copy(
            own_taper.at[b, :, wide], every_taper.at[b, me, :, wide], taper_send.at[k, b], taper_recv.at[k, b],
            device_id={"obs": lax.rem(me + k, groups)}, device_id_type=MESH,
        )

    def peers(action):
        def one(k, carry):
            action(k)
            return carry

        lax.fori_loop(1, groups, one, 0)

    for k in range(1, layers):
        sum_copy(k).start()

    order_rows = [order[pl.ds(BATCH * q, BATCH)].reshape(1, BATCH) for q in range(batches)]
    base = me * count
    order_wide = jnp.concatenate(order_rows, 1)
    steps = iota((count, nobs), 1).astype(F32)
    member = jnp.logical_and(order_wide >= base, order_wide < base + count).astype(F32)
    local = iota((count, 1), 0)
    at = jnp.sum(jnp.where(order_wide == base + local, steps, 0.0), axis=1, keepdims=True)
    rank = jnp.sum(jnp.where(steps < at, member, 0.0), axis=1, keepdims=True)
    square = (count, count)
    rank_row = jnp.sum(jnp.where(iota(square, 0) == iota(square, 1), rank, 0.0), axis=0, keepdims=True)
    chooser = (iota(square, 0).astype(F32) == rank_row).astype(F32)
    ranked = jnp.dot(
        chooser.astype(BF16), taper_weight(bins[...]).astype(BF16), preferred_element_type=F32
    )
    for n in range(batches - 1):
        rest = count - (n + 1) * per
        index = jnp.broadcast_to(order_rows[n], (rest, BATCH))
        block = lookup([ranked[count - rest :, q * BATCH : (q + 1) * BATCH] for q in range(batches)], index)
        for b in range(n + 1, batches):
            own_taper[b, :, n * BATCH : (n + 1) * BATCH] = block[(b - n - 1) * per : (b - n) * per, :]
    for b in range(1, batches):
        every_taper[b, me, :, : b * BATCH] = own_taper[b, :, : b * BATCH]
    early = min(4, batches)
    for b in range(1, early):
        peers(lambda k: taper_copy(k, b).start())

    foot_of = (iota((count, feet), 0) // (count // feet) == iota((count, feet), 1)).astype(F32)
    spread_feet = jnp.dot(chooser.astype(BF16), foot_of.astype(BF16), preferred_element_type=F32).astype(BF16)
    angles = azimuth[...].reshape(1, count)
    cosines = jnp.sum(chooser * jnp.cos(angles), axis=1, keepdims=True)
    sines = jnp.sum(chooser * jnp.sin(angles), axis=1, keepdims=True)

    blank = [jnp.zeros((padded - batches, BATCH), jnp.int32)] if padded > batches else []
    orders = jnp.concatenate(order_rows + blank, 0)
    value_rows = lookup([values[pl.ds(BATCH * q, BATCH)].reshape(1, BATCH) for q in range(batches)], orders)
    variance_rows = lookup([variances[pl.ds(BATCH * q, BATCH)].reshape(1, BATCH) for q in range(batches)], orders)
    var_rows[...] = variance_rows
    for tile in range(tiles_dev):
        tapers = taper_weight(tile_bin[tile : tile + 1, :])
        tile_weights[tile] = lookup([tapers[:, q * BATCH : (q + 1) * BATCH] for q in range(batches)], orders)
    before = (iota((BATCH, BATCH), 0) < iota((BATCH, BATCH), 1)).astype(F32).astype(BF16)
    places = []
    for b in range(batches):
        group = order_rows[b] // count
        same = (iota((groups, BATCH), 0) == group).astype(F32)
        earlier = jnp.dot(same.astype(BF16), before, preferred_element_type=F32)
        places.append(group.astype(F32) * per + jnp.sum(same * earlier, axis=0, keepdims=True))
    empty = [jnp.zeros((padded - batches, BATCH), F32)] if padded > batches else []
    columns = jnp.transpose(jnp.concatenate(places + empty + [value_rows, jnp.sqrt(variance_rows)], 0))
    for b in range(batches):
        place = columns[:, b : b + 1]
        selects[b] = (place == iota((BATCH, BATCH), 1).astype(F32)).astype(F32).astype(BF16)
        value_cols[b] = columns[:, padded + b : padded + b + 1]
        root_cols[b] = jnp.broadcast_to(columns[:, 2 * padded + b : 2 * padded + b + 1], (BATCH, BATCH))

    for k in range(1, layers):
        sum_copy(k).wait_recv()
    winds = [own_sums[h] for h in range(2)]
    for k in range(1, layers):
        winds = [winds[h] + sums[k, h] for h in range(2)]
    winds = pick(spread_feet, jnp.concatenate(winds, 1))
    observed = model_function(winds[:, :MEMBERS], winds[:, MEMBERS:], cosines, sines)
    for b in range(batches):
        own_obs[b] = observed[b * per : (b + 1) * per, :]
        every_obs[b, me] = observed[b * per : (b + 1) * per, :]
    for b in range(batches):
        if b >= early:
            peers(lambda k: taper_copy(k, b).start())
        peers(lambda k: obs_copy(k, b).start())

    def prepare(b):
        rows = pl.ds(b * BATCH, BATCH)
        peers(lambda k: obs_copy(k, b).wait_recv())
        if b:
            peers(lambda k: taper_copy(k, b).wait_recv())
        if per % SUB == 0:
            obs = every_obs[b].reshape(BATCH, MEMBERS)
            taper = every_taper[b].reshape(BATCH, nobs)
        else:
            for g in range(groups):
                gathered[g * per : (g + 1) * per, :MEMBERS] = every_obs[b, g]
                gathered[g * per : (g + 1) * per, MEMBERS:] = every_taper[b, g]
            obs, taper = gathered[:, :MEMBERS], gathered[:, MEMBERS:]
        select = selects[b]
        held[rows, :] = pick(select, obs)
        if b:
            known = taper[:, : b * BATCH].astype(BF16)
            weights[rows, : b * BATCH] = jnp.dot(select, known, preferred_element_type=F32)

    def update(ref, place, weight, m):
        value = ref[place, :]
        scaled = (scaled_all[m, :, :MEMBERS], scaled_all[m, :, MEMBERS:])
        change = (change_all[m, :, :MEMBERS], change_all[m, :, MEMBERS:])
        product = dot3(halves(value), scaled, NT) * weight
        ref[place, :] = value + dot3(halves(product), change, NN)

    def update_obs(b, m):
        place = pl.ds(pl.multiple_of(b * BATCH, BATCH), BATCH)
        update(held, place, weights[place, pl.ds(pl.multiple_of(m * BATCH, BATCH), BATCH)], m)

    eye = iota((BATCH, BATCH), 0) == iota((BATCH, BATCH), 1)
    prepare(0)

    def batch_step(num, carry):
        rows = pl.ds(pl.multiple_of(num * BATCH, BATCH), BATCH)
        batch_obs = held[rows, :]
        row_mean = jnp.mean(batch_obs, axis=1, keepdims=True)
        perturb = batch_obs - row_mean
        innov = value_cols[num] - row_mean
        split = halves(perturb)
        scaled = halves(perturb * (1.0 / (MEMBERS - 1)))
        panel[:, :BATCH] = dot3(split, scaled, NT) + jnp.where(eye, var_rows[pl.ds(num, 1), :], 0.0)
        panel[:, BATCH:] = eye.astype(F32)
        factor(panel, root_cols.at[num], upper, stage)
        first = panel[:, :BATCH]
        inverses = halves(jnp.concatenate([first, -panel[:, BATCH:]], 1))
        known = halves(jnp.concatenate([jnp.broadcast_to(innov, (BATCH, MEMBERS)), perturb], 0))
        middle = dot3(inverses, known, NN)
        change = dot3(halves(first), halves(middle), TN)
        scaled_all[num] = jnp.concatenate(scaled, 1)
        change_all[num] = jnp.concatenate(halves(change), 1)

        @pl.when(num == 0)
        def _():
            prepare(1)

        @pl.when(num + 1 < batches)
        def _():
            update_obs(num + 1, num)

        for b in range(2, batches):

            @pl.when(num == b - 2)
            def _():
                prepare(b)

        @pl.when(num + 2 < batches)
        def _():
            def pending(m, inner):
                update_obs(num + 2, m)
                return inner

            lax.fori_loop(0, num + 1, pending, 0)

        for tile in range(tiles_dev):
            update(out_ref, pl.ds(tile * TILE, TILE), tile_weights[tile, pl.ds(num, 1), :], num)
        return carry

    lax.fori_loop(0, batches, batch_step, 0)
    for k in range(1, layers):
        sum_copy(k).wait_send()
    for b in range(batches):
        peers(lambda k: obs_copy(k, b).wait_send())
        if b:
            peers(lambda k: taper_copy(k, b).wait_send())


def shards(state, foot_tiles, foot_weight, azimuth, obs_value, obs_var, tile_bin, obs_bin, order):
    groups, layers = lax.axis_size("obs"), lax.axis_size("rows")
    count, nobs = obs_bin.shape
    batches, feet, tiles_dev = nobs // BATCH, foot_tiles.shape[0], tile_bin.shape[0]
    per, padded = count // batches, (nobs // BATCH + SUB - 1) // SUB * SUB
    dma, vmem = pltpu.SemaphoreType.DMA, pltpu.VMEM
    return pl.pallas_call(
        functools.partial(filter_kernel, groups, layers),
        out_shape=jax.ShapeDtypeStruct(state.shape, F32),
        in_specs=[ANY] * 9,
        out_specs=VMEM,
        scratch_shapes=[
            vmem(foot_tiles.shape[::-1], jnp.int32), vmem(foot_weight.shape, F32), vmem((count,), F32),
            vmem((nobs,), F32), vmem((nobs,), F32), vmem(tile_bin.shape, jnp.int32), vmem(obs_bin.shape, jnp.int32),
            vmem((nobs,), jnp.int32),
            vmem((2, feet, MEMBERS), F32), vmem((layers, 2, feet, MEMBERS), F32),
            vmem((batches, per, MEMBERS), F32), vmem((batches, groups, per, MEMBERS), F32),
            vmem((batches, per, nobs), F32), vmem((batches, groups, per, nobs), F32),
            vmem((nobs, MEMBERS), F32), vmem((nobs, nobs), F32), vmem((batches, BATCH, BATCH), BF16),
            vmem((batches, BATCH, 1), F32), vmem((batches, BATCH, BATCH), F32), vmem((padded, BATCH), F32),
            vmem((tiles_dev, padded, BATCH), F32), vmem((BATCH, MEMBERS + nobs), F32),
            vmem((BATCH, 2 * BATCH), F32), vmem((BATCH // 2, BATCH), F32), vmem((STAGES, SUB, SUB, BATCH), F32),
            vmem((batches, BATCH, 2 * MEMBERS), BF16), vmem((batches, BATCH, 2 * MEMBERS), BF16),
            dma((9,)), dma((layers,)), dma((layers,)), dma((groups, batches)), dma((groups, batches)),
            dma((groups, batches)), dma((groups, batches)),
        ],
        compiler_params=pltpu.CompilerParams(
            collective_id=0, has_side_effects=True, vmem_limit_bytes=48 * 1024 * 1024
        ),
    )(state, foot_tiles.T, foot_weight, azimuth, obs_value, obs_var, tile_bin, obs_bin, order)


def solution(mesh):
    return jax.shard_map(
        shards,
        mesh=mesh,
        in_specs=(
            P(("obs", "rows"), None),
            P("obs", None),
            P("obs", None, None),
            P("obs"),
            P(),
            P(),
            P(("obs", "rows"), None),
            P("obs", None),
            P(),
        ),
        out_specs=P(("obs", "rows"), None),
        check_vma=False,
    )
```

```python
import functools

import jax
import jax.numpy as jnp
from jax import lax
from jax.experimental import pallas as pl
from jax.experimental.pallas import tpu as pltpu
from jax.sharding import PartitionSpec as P

MEMBERS = 256
BATCH = 128
TILE = 256
RADIUS = 8
SUB = 8
STAGES = 8
F32 = jnp.float32
BF16 = jnp.bfloat16


HIGH = lax.Precision.HIGHEST
MESH = pl.DeviceIdType.MESH
VMEM = pl.BlockSpec(memory_space=pltpu.VMEM)
ANY = pl.BlockSpec(memory_space=pl.ANY)


def model_function(east_wind, north_wind, cosines, sines):
    speed = jnp.sqrt(east_wind * east_wind + north_wind * north_wind + 1.0)
    cosine = (east_wind * cosines + north_wind * sines) / speed
    return jnp.exp(0.6 * jnp.log(speed)) * (0.7 + 0.4 * cosine + 0.6 * cosine * cosine)


def taper_weight(bins):
    scaled = 1.0 - bins.astype(F32) / RADIUS
    return jnp.where(bins < RADIUS, scaled * scaled, jnp.zeros_like(scaled))


def halves(value):
    high = value.astype(BF16)
    return high, (value - high.astype(F32)).astype(BF16)


def dot3(left, right, dims):
    (left_hi, left_lo), (right_hi, right_lo) = left, right
    (left_dim,), (right_dim,) = dims
    return lax.dot_general(
        jnp.concatenate([left_hi, left_lo, left_hi], left_dim),
        jnp.concatenate([right_hi, right_hi, right_lo], right_dim),
        (dims, ((), ())),
        preferred_element_type=F32,
    )


NN = ((1,), (0,))
NT = ((1,), (1,))
TN = ((0,), (0,))


def total(terms):
    while len(terms) > 1:
        terms = [a + b for a, b in zip(terms[::2], terms[1::2])]
    return terms[0]


def factor(panel, roots, upper, stage):
    blocks, half = BATCH // SUB, BATCH // 2
    lane = lax.broadcasted_iota(jnp.int32, (SUB, BATCH), 1)
    sub = lax.broadcasted_iota(jnp.int32, (SUB, BATCH), 0)
    left, right = pl.ds(0, BATCH), pl.ds(BATCH, BATCH)

    def across(value, column):
        lanes = jnp.full((SUB, BATCH), column, jnp.int32)
        return jnp.take_along_axis(value, lanes, axis=1, mode="promise_in_bounds")

    def down(value, row):
        return jnp.broadcast_to(value[row : row + 1, :], (SUB, BATCH))

    def rows(i):
        return pl.ds(SUB * i, SUB)

    for b in range(blocks):
        base = SUB * b
        end = blocks if base >= half else blocks // 2
        inside = jnp.logical_and(lane >= base, lane < base + SUB)
        start = panel[rows(b), left]
        given = panel[rows(b), right]
        root = roots[rows(b), :]
        cols = [across(start, base + k) for k in range(SUB)]
        for i in range(b + 1, end):
            value = panel[rows(i), left]
            for k in range(SUB):
                stage[i % STAGES, k] = across(value, base + k)
        solved = jnp.where(inside, (lane == sub + base).astype(F32), start)
        forward, scale, diagonal, steps = solved, None, None, []
        for k in range(0, SUB, 2):
            one, two = sub == k, sub == k + 1
            pair, below = jnp.logical_or(one, two), sub > k + 1
            u, v = cols[k], cols[k + 1]
            a, e, c = down(u, k), down(u, k + 1), down(v, k + 1)
            det = a * c - e * e
            inv_det_root, inv_root = lax.rsqrt(det), lax.rsqrt(a)
            inv = inv_det_root * inv_det_root
            p = jnp.where(one, -c, jnp.where(two, e, c * u - e * v))
            q = jnp.where(one, e, jnp.where(two, -a, a * v - e * u))
            for m in range(k + 2, SUB):
                cols[m] = jnp.where(pair, 0.0, cols[m]) - (p * down(u, m) + q * down(v, m)) * inv
            full_p, full_q = p * inv, q * inv
            solved = jnp.where(pair, 0.0, solved) - (full_p * down(solved, k) + full_q * down(solved, k + 1))
            ratio = e * (inv_root * inv_root)
            part_p = jnp.where(below, full_p, jnp.where(two, ratio, 0.0))
            part_q = jnp.where(below, full_q, 0.0)
            forward = forward - (part_p * down(forward, k) + part_q * down(forward, k + 1))
            second_scale = inv_det_root * (a * inv_root)
            diag_one, diag_two = a * inv_root, det * inv_det_root * inv_root
            if k == 0:
                scale, diagonal = jnp.where(one, inv_root, second_scale), jnp.where(one, diag_one, diag_two)
            else:
                scale = jnp.where(one, inv_root, jnp.where(two, second_scale, scale))
                diagonal = jnp.where(one, diag_one, jnp.where(two, diag_two, diagonal))
            steps.append((k, full_p, full_q, pair, u * inv_root, (v - u * ratio) * second_scale, one, two, below))
        forward = forward * scale
        lower = jnp.where(lane <= sub + base, forward, 0.0)
        panel[rows(b), left] = lower
        if base < half:
            upper[rows(b), :] = jnp.where(lane < half, lower, forward)
        gain = 1.0 / (diagonal + root)
        own = given
        for k, _, _, _, low, next_low, one, two, below in steps:
            first = down(own, k) * down(gain, k)
            second = (down(own, k + 1) - down(low, k + 1) * first) * down(gain, k + 1)
            rest = own - (low * first + next_low * second)
            own = jnp.where(below, rest, jnp.where(one, first, jnp.where(two, second, own)))
        panel[rows(b), right] = own
        if b + 1 < end:
            spread = given - root * own
            for k, full_p, full_q, pair, *_ in steps:
                spread = jnp.where(pair, 0.0, spread) - (full_p * down(spread, k) + full_q * down(spread, k + 1))
            for i in range(b + 1, end):
                columns = [stage[i % STAGES, k] for k in range(SUB)]
                value = jnp.where(inside, 0.0, panel[rows(i), left])
                panel[rows(i), left] = value - total([columns[k] * down(solved, k) for k in range(SUB)])
                panel[rows(i), right] = panel[rows(i), right] - total([columns[k] * down(spread, k) for k in range(SUB)])
        elif end < blocks:
            far = pl.ds(half, half)
            outer = halves(upper[...])
            wide = lax.broadcasted_iota(jnp.int32, (half, BATCH), 1)
            change = dot3(outer, outer, TN)[half:, :]
            panel[far, left] = jnp.where(wide < half, 0.0, panel[far, left]) - change
            change = dot3(outer, halves(panel[:half, right]), TN)[half:, :]
            panel[far, right] = panel[far, right] - change


def pick(select, value):
    high, rest = halves(value)
    low = (value - high.astype(F32) - rest.astype(F32)).astype(BF16)
    dot = functools.partial(jnp.dot, preferred_element_type=F32)
    return dot(select, high) + (dot(select, rest) + dot(select, low))


def lookup(pieces, index):
    inner, outer = index % BATCH, index // BATCH
    found = jnp.zeros(index.shape, pieces[0].dtype)
    for q, piece in enumerate(pieces):
        piece = jnp.broadcast_to(piece, index.shape)
        piece = jnp.take_along_axis(piece, inner, axis=1, mode="promise_in_bounds")
        found = jnp.where(outer == q, piece, found)
    return found


def iota(shape, dim):
    return lax.broadcasted_iota(jnp.int32, shape, dim)


def column_of(row):
    size = row.shape[1]
    eye = iota((size, size), 0) == iota((size, size), 1)
    return jnp.sum(jnp.where(eye, row, jnp.zeros_like(row)), axis=1, keepdims=True)


def filter_kernel(
    groups, layers, state_hbm, tiles_hbm, weight_hbm, azimuth_hbm, value_hbm, var_hbm, tile_bin_hbm, bins_hbm,
    order_hbm, out_ref,
    tiles, weight, azimuth, values, variances, tile_bin, bins, order,
    own_sums, sums, own_obs, every_obs, own_taper, every_taper,
    held, weights, selects, value_cols, root_cols, var_rows, tile_weights, gathered,
    panel, upper, stage, scaled_all, change_all,
    load_sem, sum_send, sum_recv, obs_send, obs_recv, taper_send, taper_recv,
):
    me, layer = lax.axis_index("obs"), lax.axis_index("rows")
    feet = weight.shape[0]
    batches, per = own_obs.shape[0], own_obs.shape[1]
    count, nobs = bins.shape
    tiles_dev, half = tile_bin.shape[0], TILE // 2
    padded = var_rows.shape[0]

    pairs = [
        (order_hbm, order), (value_hbm, values), (var_hbm, variances), (azimuth_hbm, azimuth), (tiles_hbm, tiles),
        (tile_bin_hbm, tile_bin), (state_hbm, out_ref), (weight_hbm, weight), (bins_hbm, bins),
    ]
    loads = [pltpu.make_async_copy(source, target, load_sem.at[i]) for i, (source, target) in enumerate(pairs)]
    for load in loads:
        load.start()
    barrier = pltpu.get_barrier_semaphore()
    for k in range(1, groups):
        pl.semaphore_signal(barrier, inc=1, device_id={"obs": lax.rem(me + k, groups)}, device_id_type=MESH)
    for k in range(1, layers):
        pl.semaphore_signal(barrier, inc=1, device_id={"rows": lax.rem(layer + k, layers)}, device_id_type=MESH)
    for load in loads[:8]:
        load.wait()

    partial = [jnp.zeros((feet, MEMBERS), F32) for _ in range(2)]
    listed = [column_of(tiles[t : t + 1, :].astype(F32)).astype(jnp.int32) for t in range(tiles.shape[0])]
    for tile in range(tiles_dev):
        number = layer * tiles_dev + tile
        chosen = jnp.zeros((feet, TILE), F32)
        for t in range(tiles.shape[0]):
            chosen = chosen + jnp.where(listed[t] == number, weight[:, t, :], 0.0)
        for h in range(2):
            partial[h] = partial[h] + jnp.dot(
                chosen[:, h * half : (h + 1) * half],
                out_ref[pl.ds(tile * TILE + h * half, half), :],
                precision=HIGH,
                preferred_element_type=F32,
            )
    for h in range(2):
        own_sums[h] = partial[h]
    loads[8].wait()
    pl.semaphore_wait(barrier, groups + layers - 2)

    def sum_copy(k):
        return pltpu.make_async_remote_copy(
            own_sums, sums.at[k], sum_send.at[k], sum_recv.at[k],
            device_id={"rows": lax.rem(layer + k, layers)}, device_id_type=MESH,
        )

    def obs_copy(k, b):
        return pltpu.make_async_remote_copy(
            own_obs.at[b], every_obs.at[b, me], obs_send.at[k, b], obs_recv.at[k, b],
            device_id={"obs": lax.rem(me + k, groups)}, device_id_type=MESH,
        )

    def taper_copy(k, b):
        wide = pl.ds(0, b * BATCH)
        return pltpu.make_async_remote_copy(
            own_taper.at[b, :, wide], every_taper.at[b, me, :, wide], taper_send.at[k, b], taper_recv.at[k, b],
            device_id={"obs": lax.rem(me + k, groups)}, device_id_type=MESH,
        )

    def peers(action):
        def one(k, carry):
            action(k)
            return carry

        lax.fori_loop(1, groups, one, 0)

    for k in range(1, layers):
        sum_copy(k).start()

    order_rows = [order[pl.ds(BATCH * q, BATCH)].reshape(1, BATCH) for q in range(batches)]
    base = me * count
    order_wide = jnp.concatenate(order_rows, 1)
    steps = iota((count, nobs), 1).astype(F32)
    member = jnp.logical_and(order_wide >= base, order_wide < base + count).astype(F32)
    local = iota((count, 1), 0)
    at = jnp.sum(jnp.where(order_wide == base + local, steps, 0.0), axis=1, keepdims=True)
    rank = jnp.sum(jnp.where(steps < at, member, 0.0), axis=1, keepdims=True)
    square = (count, count)
    rank_row = jnp.sum(jnp.where(iota(square, 0) == iota(square, 1), rank, 0.0), axis=0, keepdims=True)
    chooser = (iota(square, 0).astype(F32) == rank_row).astype(F32)
    ranked = jnp.dot(
        chooser.astype(BF16), taper_weight(bins[...]).astype(BF16), preferred_element_type=F32
    )
    for n in range(batches - 1):
        rest = count - (n + 1) * per
        index = jnp.broadcast_to(order_rows[n], (rest, BATCH))
        block = lookup([ranked[count - rest :, q * BATCH : (q + 1) * BATCH] for q in range(batches)], index)
        for b in range(n + 1, batches):
            own_taper[b, :, n * BATCH : (n + 1) * BATCH] = block[(b - n - 1) * per : (b - n) * per, :]
    for b in range(1, batches):
        every_taper[b, me, :, : b * BATCH] = own_taper[b, :, : b * BATCH]
    early = min(4, batches)
    for b in range(1, early):
        peers(lambda k: taper_copy(k, b).start())

    foot_of = (iota((count, feet), 0) // (count // feet) == iota((count, feet), 1)).astype(F32)
    spread_feet = jnp.dot(chooser.astype(BF16), foot_of.astype(BF16), preferred_element_type=F32).astype(BF16)
    angles = azimuth[...].reshape(1, count)
    cosines = jnp.sum(chooser * jnp.cos(angles), axis=1, keepdims=True)
    sines = jnp.sum(chooser * jnp.sin(angles), axis=1, keepdims=True)

    blank = [jnp.zeros((padded - batches, BATCH), jnp.int32)] if padded > batches else []
    orders = jnp.concatenate(order_rows + blank, 0)
    value_rows = lookup([values[pl.ds(BATCH * q, BATCH)].reshape(1, BATCH) for q in range(batches)], orders)
    variance_rows = lookup([variances[pl.ds(BATCH * q, BATCH)].reshape(1, BATCH) for q in range(batches)], orders)
    var_rows[...] = variance_rows
    for tile in range(tiles_dev):
        tapers = taper_weight(tile_bin[tile : tile + 1, :])
        tile_weights[tile] = lookup([tapers[:, q * BATCH : (q + 1) * BATCH] for q in range(batches)], orders)
    before = (iota((BATCH, BATCH), 0) < iota((BATCH, BATCH), 1)).astype(F32).astype(BF16)
    places = []
    for b in range(batches):
        group = order_rows[b] // count
        same = (iota((groups, BATCH), 0) == group).astype(F32)
        earlier = jnp.dot(same.astype(BF16), before, preferred_element_type=F32)
        places.append(group.astype(F32) * per + jnp.sum(same * earlier, axis=0, keepdims=True))
    empty = [jnp.zeros((padded - batches, BATCH), F32)] if padded > batches else []
    columns = jnp.transpose(jnp.concatenate(places + empty + [value_rows, jnp.sqrt(variance_rows)], 0))
    for b in range(batches):
        place = columns[:, b : b + 1]
        selects[b] = (place == iota((BATCH, BATCH), 1).astype(F32)).astype(F32).astype(BF16)
        value_cols[b] = columns[:, padded + b : padded + b + 1]
        root_cols[b] = jnp.broadcast_to(columns[:, 2 * padded + b : 2 * padded + b + 1], (BATCH, BATCH))

    for k in range(1, layers):
        sum_copy(k).wait_recv()
    winds = [own_sums[h] for h in range(2)]
    for k in range(1, layers):
        winds = [winds[h] + sums[k, h] for h in range(2)]
    winds = pick(spread_feet, jnp.concatenate(winds, 1))
    observed = model_function(winds[:, :MEMBERS], winds[:, MEMBERS:], cosines, sines)
    for b in range(batches):
        own_obs[b] = observed[b * per : (b + 1) * per, :]
        every_obs[b, me] = observed[b * per : (b + 1) * per, :]
    for b in range(batches):
        if b >= early:
            peers(lambda k: taper_copy(k, b).start())
        peers(lambda k: obs_copy(k, b).start())

    def prepare(b):
        rows = pl.ds(b * BATCH, BATCH)
        peers(lambda k: obs_copy(k, b).wait_recv())
        if b:
            peers(lambda k: taper_copy(k, b).wait_recv())
        if per % SUB == 0:
            obs = every_obs[b].reshape(BATCH, MEMBERS)
            taper = every_taper[b].reshape(BATCH, nobs)
        else:
            for g in range(groups):
                gathered[g * per : (g + 1) * per, :MEMBERS] = every_obs[b, g]
                gathered[g * per : (g + 1) * per, MEMBERS:] = every_taper[b, g]
            obs, taper = gathered[:, :MEMBERS], gathered[:, MEMBERS:]
        select = selects[b]
        held[rows, :] = pick(select, obs)
        if b:
            known = taper[:, : b * BATCH].astype(BF16)
            weights[rows, : b * BATCH] = jnp.dot(select, known, preferred_element_type=F32)

    def update(ref, place, weight, m):
        value = ref[place, :]
        scaled = (scaled_all[m, :, :MEMBERS], scaled_all[m, :, MEMBERS:])
        change = (change_all[m, :, :MEMBERS], change_all[m, :, MEMBERS:])
        product = dot3(halves(value), scaled, NT) * weight
        ref[place, :] = value + dot3(halves(product), change, NN)

    def update_obs(b, m):
        place = pl.ds(pl.multiple_of(b * BATCH, BATCH), BATCH)
        update(held, place, weights[place, pl.ds(pl.multiple_of(m * BATCH, BATCH), BATCH)], m)

    eye = iota((BATCH, BATCH), 0) == iota((BATCH, BATCH), 1)
    prepare(0)

    def batch_step(num, carry):
        rows = pl.ds(pl.multiple_of(num * BATCH, BATCH), BATCH)
        batch_obs = held[rows, :]
        row_mean = jnp.mean(batch_obs, axis=1, keepdims=True)
        perturb = batch_obs - row_mean
        innov = value_cols[num] - row_mean
        split = halves(perturb)
        scaled = halves(perturb * (1.0 / (MEMBERS - 1)))
        panel[:, :BATCH] = dot3(split, scaled, NT) + jnp.where(eye, var_rows[pl.ds(num, 1), :], 0.0)
        panel[:, BATCH:] = eye.astype(F32)
        factor(panel, root_cols.at[num], upper, stage)
        first = panel[:, :BATCH]
        inverses = halves(jnp.concatenate([first, -panel[:, BATCH:]], 1))
        known = halves(jnp.concatenate([jnp.broadcast_to(innov, (BATCH, MEMBERS)), perturb], 0))
        middle = dot3(inverses, known, NN)
        change = dot3(halves(first), halves(middle), TN)
        scaled_all[num] = jnp.concatenate(scaled, 1)
        change_all[num] = jnp.concatenate(halves(change), 1)

        @pl.when(num == 0)
        def _():
            prepare(1)

        @pl.when(num + 1 < batches)
        def _():
            update_obs(num + 1, num)

        for b in range(2, batches):

            @pl.when(num == b - 2)
            def _():
                prepare(b)

        @pl.when(num + 2 < batches)
        def _():
            def pending(m, inner):
                update_obs(num + 2, m)
                return inner

            lax.fori_loop(0, num + 1, pending, 0)

        for tile in range(tiles_dev):
            update(out_ref, pl.ds(tile * TILE, TILE), tile_weights[tile, pl.ds(num, 1), :], num)
        return carry

    lax.fori_loop(0, batches, batch_step, 0)
    for k in range(1, layers):
        sum_copy(k).wait_send()
    for b in range(batches):
        peers(lambda k: obs_copy(k, b).wait_send())
        if b:
            peers(lambda k: taper_copy(k, b).wait_send())


def shards(state, foot_tiles, foot_weight, azimuth, obs_value, obs_var, tile_bin, obs_bin, order):
    groups, layers = lax.axis_size("obs"), lax.axis_size("rows")
    count, nobs = obs_bin.shape
    batches, feet, tiles_dev = nobs // BATCH, foot_tiles.shape[0], tile_bin.shape[0]
    per, padded = count // batches, (nobs // BATCH + SUB - 1) // SUB * SUB
    dma, vmem = pltpu.SemaphoreType.DMA, pltpu.VMEM
    return pl.pallas_call(
        functools.partial(filter_kernel, groups, layers),
        out_shape=jax.ShapeDtypeStruct(state.shape, F32),
        in_specs=[ANY] * 9,
        out_specs=VMEM,
        scratch_shapes=[
            vmem(foot_tiles.shape[::-1], jnp.int32), vmem(foot_weight.shape, F32), vmem((count,), F32),
            vmem((nobs,), F32), vmem((nobs,), F32), vmem(tile_bin.shape, jnp.int32), vmem(obs_bin.shape, jnp.int32),
            vmem((nobs,), jnp.int32),
            vmem((2, feet, MEMBERS), F32), vmem((layers, 2, feet, MEMBERS), F32),
            vmem((batches, per, MEMBERS), F32), vmem((batches, groups, per, MEMBERS), F32),
            vmem((batches, per, nobs), F32), vmem((batches, groups, per, nobs), F32),
            vmem((nobs, MEMBERS), F32), vmem((nobs, nobs), F32), vmem((batches, BATCH, BATCH), BF16),
            vmem((batches, BATCH, 1), F32), vmem((batches, BATCH, BATCH), F32), vmem((padded, BATCH), F32),
            vmem((tiles_dev, padded, BATCH), F32), vmem((BATCH, MEMBERS + nobs), F32),
            vmem((BATCH, 2 * BATCH), F32), vmem((BATCH // 2, BATCH), F32), vmem((STAGES, SUB, SUB, BATCH), F32),
            vmem((batches, BATCH, 2 * MEMBERS), BF16), vmem((batches, BATCH, 2 * MEMBERS), BF16),
            dma((9,)), dma((layers,)), dma((layers,)), dma((groups, batches)), dma((groups, batches)),
            dma((groups, batches)), dma((groups, batches)),
        ],
        compiler_params=pltpu.CompilerParams(
            collective_id=0, has_side_effects=True, vmem_limit_bytes=67043328
        ),
    )(state, foot_tiles.T, foot_weight, azimuth, obs_value, obs_var, tile_bin, obs_bin, order)


def solution(mesh):
    return jax.shard_map(
        shards,
        mesh=mesh,
        in_specs=(
            P(("obs", "rows"), None),
            P("obs", None),
            P("obs", None, None),
            P("obs"),
            P(),
            P(),
            P(("obs", "rows"), None),
            P("obs", None),
            P(),
        ),
        out_specs=P(("obs", "rows"), None),
        check_vma=False,
    )
```

```python
import functools

import jax
import jax.numpy as jnp
from jax import lax
from jax.experimental import pallas as pl
from jax.experimental.pallas import tpu as pltpu
from jax.sharding import PartitionSpec as P

MEMBERS = 256
BATCH = 128
TILE = 256
RADIUS = 8
SUB = 8
STAGES = 8
SPAN = 16
LAGGED = 3
F32 = jnp.float32
BF16 = jnp.bfloat16


HIGH = lax.Precision.HIGHEST
MESH = pl.DeviceIdType.MESH
VMEM = pl.BlockSpec(memory_space=pltpu.VMEM)
ANY = pl.BlockSpec(memory_space=pl.ANY)


def model_function(east_wind, north_wind, cosines, sines):
    speed = jnp.sqrt(east_wind * east_wind + north_wind * north_wind + 1.0)
    cosine = (east_wind * cosines + north_wind * sines) / speed
    return jnp.exp(0.6 * jnp.log(speed)) * (0.7 + 0.4 * cosine + 0.6 * cosine * cosine)


def taper_weight(bins):
    scaled = 1.0 - bins.astype(F32) / RADIUS
    return jnp.where(bins < RADIUS, scaled * scaled, jnp.zeros_like(scaled))


def halves(value):
    high = value.astype(BF16)
    return high, (value - high.astype(F32)).astype(BF16)


def dot3(left, right, dims):
    (left_hi, left_lo), (right_hi, right_lo) = left, right
    (left_dim,), (right_dim,) = dims
    return lax.dot_general(
        jnp.concatenate([left_hi, left_lo, left_hi], left_dim),
        jnp.concatenate([right_hi, right_hi, right_lo], right_dim),
        (dims, ((), ())),
        preferred_element_type=F32,
    )


NN = ((1,), (0,))
NT = ((1,), (1,))
TN = ((0,), (0,))


def total(terms):
    while len(terms) > 1:
        terms = [a + b for a, b in zip(terms[::2], terms[1::2])]
    return terms[0]


def factor(panel, roots, upper, stage, fill):
    blocks, group = BATCH // SUB, upper.shape[0] // SUB
    lane = lax.broadcasted_iota(jnp.int32, (SUB, BATCH), 1)
    sub = lax.broadcasted_iota(jnp.int32, (SUB, BATCH), 0)
    left, right = pl.ds(0, BATCH), pl.ds(BATCH, BATCH)

    def across(value, column):
        lanes = jnp.full((SUB, BATCH), column, jnp.int32)
        return jnp.take_along_axis(value, lanes, axis=1, mode="promise_in_bounds")

    def down(value, row):
        return jnp.broadcast_to(value[row : row + 1, :], (SUB, BATCH))

    def rows(i):
        return pl.ds(SUB * i, SUB)

    for b in range(blocks):
        base = SUB * b
        end = (b // group + 1) * group
        border = SUB * end
        inside = jnp.logical_and(lane >= base, lane < base + SUB)
        start = panel[rows(b), left]
        given = panel[rows(b), right]
        root = roots[rows(b), :]
        cols = [across(start, base + k) for k in range(SUB)]
        for i in range(b + 1, end):
            value = panel[rows(i), left]
            for k in range(SUB):
                stage[i % STAGES, k] = across(value, base + k)
        solved = jnp.where(inside, (lane == sub + base).astype(F32), start)
        forward, scale, diagonal, steps = solved, None, None, []
        for k in range(0, SUB, 2):
            one, two = sub == k, sub == k + 1
            pair, below = jnp.logical_or(one, two), sub > k + 1
            u, v = cols[k], cols[k + 1]
            a, e, c = down(u, k), down(u, k + 1), down(v, k + 1)
            det = a * c - e * e
            inv_det_root, inv_root = lax.rsqrt(det), lax.rsqrt(a)
            inv = inv_det_root * inv_det_root
            p = jnp.where(one, -c, jnp.where(two, e, c * u - e * v))
            q = jnp.where(one, e, jnp.where(two, -a, a * v - e * u))
            for m in range(k + 2, SUB):
                cols[m] = jnp.where(pair, 0.0, cols[m]) - (p * down(u, m) + q * down(v, m)) * inv
            full_p, full_q = p * inv, q * inv
            solved = jnp.where(pair, 0.0, solved) - (full_p * down(solved, k) + full_q * down(solved, k + 1))
            ratio = e * (inv_root * inv_root)
            part_p = jnp.where(below, full_p, jnp.where(two, ratio, 0.0))
            part_q = jnp.where(below, full_q, 0.0)
            forward = forward - (part_p * down(forward, k) + part_q * down(forward, k + 1))
            second_scale = inv_det_root * (a * inv_root)
            diag_one, diag_two = a * inv_root, det * inv_det_root * inv_root
            if k == 0:
                scale, diagonal = jnp.where(one, inv_root, second_scale), jnp.where(one, diag_one, diag_two)
            else:
                scale = jnp.where(one, inv_root, jnp.where(two, second_scale, scale))
                diagonal = jnp.where(one, diag_one, jnp.where(two, diag_two, diagonal))
            steps.append((k, full_p, full_q, pair, u * inv_root, (v - u * ratio) * second_scale, one, two, below))
        forward = forward * scale
        lower = jnp.where(lane <= sub + base, forward, 0.0)
        panel[rows(b), left] = lower
        if end < blocks:
            upper[rows(b % group), :] = jnp.where(lane < border, lower, forward)
        gain = 1.0 / (diagonal + root)
        own = given
        for k, _, _, _, low, next_low, one, two, below in steps:
            first = down(own, k) * down(gain, k)
            second = (down(own, k + 1) - down(low, k + 1) * first) * down(gain, k + 1)
            rest = own - (low * first + next_low * second)
            own = jnp.where(below, rest, jnp.where(one, first, jnp.where(two, second, own)))
        panel[rows(b), right] = own
        if b + 1 < end:
            spread = given - root * own
            for k, full_p, full_q, pair, *_ in steps:
                spread = jnp.where(pair, 0.0, spread) - (full_p * down(spread, k) + full_q * down(spread, k + 1))
            for i in range(b + 1, end):
                columns = [stage[i % STAGES, k] for k in range(SUB)]
                value = jnp.where(inside, 0.0, panel[rows(i), left])
                panel[rows(i), left] = value - total([columns[k] * down(solved, k) for k in range(SUB)])
                panel[rows(i), right] = panel[rows(i), right] - total([columns[k] * down(spread, k) for k in range(SUB)])
        elif end < blocks:
            inner, far = pl.ds(border - SUB * group, SUB * group), pl.ds(border, BATCH - border)
            outer = halves(upper[...])
            wide = iota((BATCH - border, BATCH), 1)
            joined = jnp.logical_and(wide >= border - SUB * group, wide < border)
            change = dot3(outer, outer, TN)[border:, :]
            panel[far, left] = jnp.where(joined, 0.0, panel[far, left]) - change
            change = dot3(outer, halves(panel[inner, right]), TN)[border:, :]
            panel[far, right] = panel[far, right] - change
        fill(b)


def pick(select, value):
    high, rest = halves(value)
    low = (value - high.astype(F32) - rest.astype(F32)).astype(BF16)
    dot = functools.partial(jnp.dot, preferred_element_type=F32)
    return dot(select, high) + (dot(select, rest) + dot(select, low))


def lookup(pieces, index):
    inner, outer = index % BATCH, index // BATCH
    found = jnp.zeros(index.shape, pieces[0].dtype)
    for q, piece in enumerate(pieces):
        piece = jnp.broadcast_to(piece, index.shape)
        piece = jnp.take_along_axis(piece, inner, axis=1, mode="promise_in_bounds")
        found = jnp.where(outer == q, piece, found)
    return found


def iota(shape, dim):
    return lax.broadcasted_iota(jnp.int32, shape, dim)


def column_of(row):
    size = row.shape[1]
    eye = iota((size, size), 0) == iota((size, size), 1)
    return jnp.sum(jnp.where(eye, row, jnp.zeros_like(row)), axis=1, keepdims=True)


def filter_kernel(
    groups, layers, state_hbm, tiles_hbm, weight_hbm, azimuth_hbm, value_hbm, var_hbm, tile_bin_hbm, bins_hbm,
    order_hbm, out_ref,
    tiles, weight, azimuth, values, variances, tile_bin, bins, order,
    own_sums, sums, own_obs, every_obs, own_taper, every_taper,
    held, weights, selects, value_cols, root_cols, var_rows, tile_weights, gathered,
    panel, upper, stage, scaled_all, change_all,
    load_sem, sum_send, sum_recv, obs_send, obs_recv, taper_send, taper_recv,
):
    me, layer = lax.axis_index("obs"), lax.axis_index("rows")
    feet = weight.shape[0]
    batches, per = own_obs.shape[0], own_obs.shape[1]
    count, nobs = bins.shape
    tiles_dev, half = tile_bin.shape[0], TILE // 2
    padded = var_rows.shape[0]

    pairs = [
        (order_hbm, order), (value_hbm, values), (var_hbm, variances), (azimuth_hbm, azimuth), (tiles_hbm, tiles),
        (tile_bin_hbm, tile_bin), (state_hbm, out_ref), (weight_hbm, weight), (bins_hbm, bins),
    ]
    loads = [pltpu.make_async_copy(source, target, load_sem.at[i]) for i, (source, target) in enumerate(pairs)]
    for load in loads:
        load.start()
    barrier = pltpu.get_barrier_semaphore()
    for k in range(1, groups):
        pl.semaphore_signal(barrier, inc=1, device_id={"obs": lax.rem(me + k, groups)}, device_id_type=MESH)
    for k in range(1, layers):
        pl.semaphore_signal(barrier, inc=1, device_id={"rows": lax.rem(layer + k, layers)}, device_id_type=MESH)
    for load in loads[:8]:
        load.wait()

    partial = [jnp.zeros((feet, MEMBERS), F32) for _ in range(2)]
    listed = [column_of(tiles[t : t + 1, :].astype(F32)).astype(jnp.int32) for t in range(tiles.shape[0])]
    for tile in range(tiles_dev):
        number = layer * tiles_dev + tile
        chosen = jnp.zeros((feet, TILE), F32)
        for t in range(tiles.shape[0]):
            chosen = chosen + jnp.where(listed[t] == number, weight[:, t, :], 0.0)
        for h in range(2):
            partial[h] = partial[h] + jnp.dot(
                chosen[:, h * half : (h + 1) * half],
                out_ref[pl.ds(tile * TILE + h * half, half), :],
                precision=HIGH,
                preferred_element_type=F32,
            )
    for h in range(2):
        own_sums[h] = partial[h]
    loads[8].wait()
    pl.semaphore_wait(barrier, groups + layers - 2)

    def sum_copy(k):
        return pltpu.make_async_remote_copy(
            own_sums, sums.at[k], sum_send.at[k], sum_recv.at[k],
            device_id={"rows": lax.rem(layer + k, layers)}, device_id_type=MESH,
        )

    def obs_copy(k, b):
        return pltpu.make_async_remote_copy(
            own_obs.at[b], every_obs.at[b, me], obs_send.at[k, b], obs_recv.at[k, b],
            device_id={"obs": lax.rem(me + k, groups)}, device_id_type=MESH,
        )

    def taper_copy(k, b):
        wide = pl.ds(0, b * BATCH)
        return pltpu.make_async_remote_copy(
            own_taper.at[b, :, wide], every_taper.at[b, me, :, wide], taper_send.at[k, b], taper_recv.at[k, b],
            device_id={"obs": lax.rem(me + k, groups)}, device_id_type=MESH,
        )

    def peers(action):
        def one(k, carry):
            action(k)
            return carry

        lax.fori_loop(1, groups, one, 0)

    for k in range(1, layers):
        sum_copy(k).start()

    order_rows = [order[pl.ds(BATCH * q, BATCH)].reshape(1, BATCH) for q in range(batches)]
    base = me * count
    order_wide = jnp.concatenate(order_rows, 1)
    steps = iota((count, nobs), 1).astype(F32)
    member = jnp.logical_and(order_wide >= base, order_wide < base + count).astype(F32)
    local = iota((count, 1), 0)
    at = jnp.sum(jnp.where(order_wide == base + local, steps, 0.0), axis=1, keepdims=True)
    rank = jnp.sum(jnp.where(steps < at, member, 0.0), axis=1, keepdims=True)
    square = (count, count)
    rank_row = jnp.sum(jnp.where(iota(square, 0) == iota(square, 1), rank, 0.0), axis=0, keepdims=True)
    chooser = (iota(square, 0).astype(F32) == rank_row).astype(F32)
    ranked = jnp.dot(
        chooser.astype(BF16), taper_weight(bins[...]).astype(BF16), preferred_element_type=F32
    )
    for n in range(batches - 1):
        rest = count - (n + 1) * per
        index = jnp.broadcast_to(order_rows[n], (rest, BATCH))
        block = lookup([ranked[count - rest :, q * BATCH : (q + 1) * BATCH] for q in range(batches)], index)
        for b in range(n + 1, batches):
            own_taper[b, :, n * BATCH : (n + 1) * BATCH] = block[(b - n - 1) * per : (b - n) * per, :]
    for b in range(1, batches):
        every_taper[b, me, :, : b * BATCH] = own_taper[b, :, : b * BATCH]
    early = min(4, batches)
    for b in range(1, early):
        peers(lambda k: taper_copy(k, b).start())

    foot_of = (iota((count, feet), 0) // (count // feet) == iota((count, feet), 1)).astype(F32)
    spread_feet = jnp.dot(chooser.astype(BF16), foot_of.astype(BF16), preferred_element_type=F32).astype(BF16)
    angles = azimuth[...].reshape(1, count)
    cosines = jnp.sum(chooser * jnp.cos(angles), axis=1, keepdims=True)
    sines = jnp.sum(chooser * jnp.sin(angles), axis=1, keepdims=True)

    blank = [jnp.zeros((padded - batches, BATCH), jnp.int32)] if padded > batches else []
    orders = jnp.concatenate(order_rows + blank, 0)
    value_rows = lookup([values[pl.ds(BATCH * q, BATCH)].reshape(1, BATCH) for q in range(batches)], orders)
    variance_rows = lookup([variances[pl.ds(BATCH * q, BATCH)].reshape(1, BATCH) for q in range(batches)], orders)
    var_rows[...] = variance_rows
    for tile in range(tiles_dev):
        tapers = taper_weight(tile_bin[tile : tile + 1, :])
        tile_weights[tile] = lookup([tapers[:, q * BATCH : (q + 1) * BATCH] for q in range(batches)], orders)
    before = (iota((BATCH, BATCH), 0) < iota((BATCH, BATCH), 1)).astype(F32).astype(BF16)
    places = []
    for b in range(batches):
        group = order_rows[b] // count
        same = (iota((groups, BATCH), 0) == group).astype(F32)
        earlier = jnp.dot(same.astype(BF16), before, preferred_element_type=F32)
        places.append(group.astype(F32) * per + jnp.sum(same * earlier, axis=0, keepdims=True))
    empty = [jnp.zeros((padded - batches, BATCH), F32)] if padded > batches else []
    columns = jnp.transpose(jnp.concatenate(places + empty + [value_rows, jnp.sqrt(variance_rows)], 0))
    for b in range(batches):
        place = columns[:, b : b + 1]
        selects[b] = (place == iota((BATCH, BATCH), 1).astype(F32)).astype(F32).astype(BF16)
        value_cols[b] = columns[:, padded + b : padded + b + 1]
        root_cols[b] = jnp.broadcast_to(columns[:, 2 * padded + b : 2 * padded + b + 1], (BATCH, BATCH))

    for k in range(1, layers):
        sum_copy(k).wait_recv()
    winds = [own_sums[h] for h in range(2)]
    for k in range(1, layers):
        winds = [winds[h] + sums[k, h] for h in range(2)]
    winds = pick(spread_feet, jnp.concatenate(winds, 1))
    observed = model_function(winds[:, :MEMBERS], winds[:, MEMBERS:], cosines, sines)
    for b in range(batches):
        own_obs[b] = observed[b * per : (b + 1) * per, :]
        every_obs[b, me] = observed[b * per : (b + 1) * per, :]
    for b in range(batches):
        if b >= early:
            peers(lambda k: taper_copy(k, b).start())
        peers(lambda k: obs_copy(k, b).start())

    def arrive(b):
        peers(lambda k: obs_copy(k, b).wait_recv())
        if b:
            peers(lambda k: taper_copy(k, b).wait_recv())

    def prepare(b):
        rows = pl.ds(b * BATCH, BATCH)
        if per % SUB == 0:
            obs = every_obs[b].reshape(BATCH, MEMBERS)
            taper = every_taper[b].reshape(BATCH, nobs)
        else:
            for g in range(groups):
                gathered[g * per : (g + 1) * per, :MEMBERS] = every_obs[b, g]
                gathered[g * per : (g + 1) * per, MEMBERS:] = every_taper[b, g]
            obs, taper = gathered[:, :MEMBERS], gathered[:, MEMBERS:]
        select = selects[b]
        held[rows, :] = pick(select, obs)
        if b:
            known = taper[:, : b * BATCH].astype(BF16)
            weights[rows, : b * BATCH] = jnp.dot(select, known, preferred_element_type=F32)

    def update(ref, first, weight, m):
        place = pl.ds(first, BATCH)
        product = []

        def measure():
            scaled = (scaled_all[m, :, :MEMBERS], scaled_all[m, :, MEMBERS:])
            product.append(halves(dot3(halves(ref[place, :]), scaled, NT) * weight()))

        def apply():
            change = (change_all[m, :, :MEMBERS], change_all[m, :, MEMBERS:])
            ref[place, :] = ref[place, :] + dot3(product[0], change, NN)

        return [measure, apply]

    def update_obs(b, m):
        return update(held, b * BATCH, lambda: weights[pl.ds(b * BATCH, BATCH), pl.ds(m * BATCH, BATCH)], m)

    def update_state(m):
        work = []
        for first in range(0, tiles_dev * TILE, BATCH):
            work += update(out_ref, first, lambda tile=first // TILE: tile_weights[tile, pl.ds(m, 1), :], m)
        return work

    eye = iota((BATCH, BATCH), 0) == iota((BATCH, BATCH), 1)

    def gains(n, work):
        batch_obs = held[pl.ds(n * BATCH, BATCH), :]
        row_mean = jnp.mean(batch_obs, axis=1, keepdims=True)
        perturb = batch_obs - row_mean
        innov = value_cols[n] - row_mean
        split = halves(perturb)
        scaled = halves(perturb * (1.0 / (MEMBERS - 1)))
        panel[:, :BATCH] = dot3(split, scaled, NT) + jnp.where(eye, var_rows[pl.ds(n, 1), :], 0.0)
        panel[:, BATCH:] = eye.astype(F32)
        queue, slots = list(work), BATCH // SUB

        def fill(b):
            for _ in range(-(-len(queue) // (slots - b))):
                queue.pop(0)()

        factor(panel, root_cols.at[n], upper, stage, fill)
        first = panel[:, :BATCH]
        inverses = halves(jnp.concatenate([first, -panel[:, BATCH:]], 1))
        known = halves(jnp.concatenate([jnp.broadcast_to(innov, (BATCH, MEMBERS)), perturb], 0))
        middle = dot3(inverses, known, NN)
        change = dot3(halves(first), halves(middle), TN)
        scaled_all[n] = jnp.concatenate(scaled, 1)
        change_all[n] = jnp.concatenate(halves(change), 1)

    def run(work):
        for step in work:
            step()

    applied = [0] * batches
    arrive(0)
    prepare(0)
    for n in range(batches):
        work = []
        if n:
            for b in [2, 3] if n == 1 else [n + 2]:
                if b < batches:
                    arrive(b)
                    work.append(functools.partial(prepare, b))
        room = LAGGED
        for b in range(n + 1, min(n + 3, batches)):
            while applied[b] < n and (b == n + 1 or room > 0):
                work += update_obs(b, applied[b])
                applied[b] += 1
                room -= 1
        if n:
            work += update_state(n - 1)
        gains(n, work)
        if n == 0 and batches > 1:
            arrive(1)
            prepare(1)
        if n + 1 < batches:
            run(update_obs(n + 1, n))
            applied[n + 1] = n + 1
    run(update_state(batches - 1))
    for k in range(1, layers):
        sum_copy(k).wait_send()
    for b in range(batches):
        peers(lambda k: obs_copy(k, b).wait_send())
        if b:
            peers(lambda k: taper_copy(k, b).wait_send())


def shards(state, foot_tiles, foot_weight, azimuth, obs_value, obs_var, tile_bin, obs_bin, order):
    groups, layers = lax.axis_size("obs"), lax.axis_size("rows")
    count, nobs = obs_bin.shape
    batches, feet, tiles_dev = nobs // BATCH, foot_tiles.shape[0], tile_bin.shape[0]
    per, padded = count // batches, (nobs // BATCH + SUB - 1) // SUB * SUB
    dma, vmem = pltpu.SemaphoreType.DMA, pltpu.VMEM
    return pl.pallas_call(
        functools.partial(filter_kernel, groups, layers),
        out_shape=jax.ShapeDtypeStruct(state.shape, F32),
        in_specs=[ANY] * 9,
        out_specs=VMEM,
        scratch_shapes=[
            vmem(foot_tiles.shape[::-1], jnp.int32), vmem(foot_weight.shape, F32), vmem((count,), F32),
            vmem((nobs,), F32), vmem((nobs,), F32), vmem(tile_bin.shape, jnp.int32), vmem(obs_bin.shape, jnp.int32),
            vmem((nobs,), jnp.int32),
            vmem((2, feet, MEMBERS), F32), vmem((layers, 2, feet, MEMBERS), F32),
            vmem((batches, per, MEMBERS), F32), vmem((batches, groups, per, MEMBERS), F32),
            vmem((batches, per, nobs), F32), vmem((batches, groups, per, nobs), F32),
            vmem((nobs, MEMBERS), F32), vmem((nobs, nobs), F32), vmem((batches, BATCH, BATCH), BF16),
            vmem((batches, BATCH, 1), F32), vmem((batches, BATCH, BATCH), F32), vmem((padded, BATCH), F32),
            vmem((tiles_dev, padded, BATCH), F32), vmem((BATCH, MEMBERS + nobs), F32),
            vmem((BATCH, 2 * BATCH), F32), vmem((SPAN, BATCH), F32), vmem((STAGES, SUB, SUB, BATCH), F32),
            vmem((batches, BATCH, 2 * MEMBERS), BF16), vmem((batches, BATCH, 2 * MEMBERS), BF16),
            dma((9,)), dma((layers,)), dma((layers,)), dma((groups, batches)), dma((groups, batches)),
            dma((groups, batches)), dma((groups, batches)),
        ],
        compiler_params=pltpu.CompilerParams(
            collective_id=0, has_side_effects=True, vmem_limit_bytes=67043328
        ),
    )(state, foot_tiles.T, foot_weight, azimuth, obs_value, obs_var, tile_bin, obs_bin, order)


def solution(mesh):
    return jax.shard_map(
        shards,
        mesh=mesh,
        in_specs=(
            P(("obs", "rows"), None),
            P("obs", None),
            P("obs", None, None),
            P("obs"),
            P(),
            P(),
            P(("obs", "rows"), None),
            P("obs", None),
            P(),
        ),
        out_specs=P(("obs", "rows"), None),
        check_vma=False,
    )
```

```python
import functools

import jax
import jax.numpy as jnp
from jax import lax
from jax.experimental import pallas as pl
from jax.experimental.pallas import tpu as pltpu
from jax.sharding import PartitionSpec as P

MEMBERS = 256
BATCH = 128
TILE = 256
RADIUS = 8
SUB = 8
STAGES = 8
SPAN = 16
F32 = jnp.float32
BF16 = jnp.bfloat16


HIGH = lax.Precision.HIGHEST
MESH = pl.DeviceIdType.MESH
VMEM = pl.BlockSpec(memory_space=pltpu.VMEM)
ANY = pl.BlockSpec(memory_space=pl.ANY)


def model_function(east_wind, north_wind, cosines, sines):
    speed = jnp.sqrt(east_wind * east_wind + north_wind * north_wind + 1.0)
    cosine = (east_wind * cosines + north_wind * sines) / speed
    return jnp.exp(0.6 * jnp.log(speed)) * (0.7 + 0.4 * cosine + 0.6 * cosine * cosine)


def taper_weight(bins):
    scaled = 1.0 - bins.astype(F32) / RADIUS
    return jnp.where(bins < RADIUS, scaled * scaled, jnp.zeros_like(scaled))


def halves(value):
    high = value.astype(BF16)
    return high, (value - high.astype(F32)).astype(BF16)


def dot3(left, right, dims):
    (left_hi, left_lo), (right_hi, right_lo) = left, right
    (left_dim,), (right_dim,) = dims
    return lax.dot_general(
        jnp.concatenate([left_hi, left_lo, left_hi], left_dim),
        jnp.concatenate([right_hi, right_hi, right_lo], right_dim),
        (dims, ((), ())),
        preferred_element_type=F32,
    )


NN = ((1,), (0,))
NT = ((1,), (1,))
TN = ((0,), (0,))


def total(terms):
    while len(terms) > 1:
        terms = [a + b for a, b in zip(terms[::2], terms[1::2])]
    return terms[0]


def factor(panel, roots, upper, stage, fill):
    blocks, group = BATCH // SUB, upper.shape[0] // SUB
    lane = lax.broadcasted_iota(jnp.int32, (SUB, BATCH), 1)
    sub = lax.broadcasted_iota(jnp.int32, (SUB, BATCH), 0)
    left, right = pl.ds(0, BATCH), pl.ds(BATCH, BATCH)

    def across(value, column):
        lanes = jnp.full((SUB, BATCH), column, jnp.int32)
        return jnp.take_along_axis(value, lanes, axis=1, mode="promise_in_bounds")

    def down(value, row):
        return jnp.broadcast_to(value[row : row + 1, :], (SUB, BATCH))

    def rows(i):
        return pl.ds(SUB * i, SUB)

    for b in range(blocks):
        base = SUB * b
        end = (b // group + 1) * group
        border = SUB * end
        inside = jnp.logical_and(lane >= base, lane < base + SUB)
        start = panel[rows(b), left]
        given = panel[rows(b), right]
        root = roots[rows(b), :]
        cols = [across(start, base + k) for k in range(SUB)]
        for i in range(b + 1, end):
            value = panel[rows(i), left]
            for k in range(SUB):
                stage[i % STAGES, k] = across(value, base + k)
        solved = jnp.where(inside, (lane == sub + base).astype(F32), start)
        forward, scale, diagonal, steps = solved, None, None, []
        for k in range(0, SUB, 2):
            one, two = sub == k, sub == k + 1
            pair, below = jnp.logical_or(one, two), sub > k + 1
            u, v = cols[k], cols[k + 1]
            a, e, c = down(u, k), down(u, k + 1), down(v, k + 1)
            det = a * c - e * e
            inv_det_root, inv_root = lax.rsqrt(det), lax.rsqrt(a)
            inv = inv_det_root * inv_det_root
            p = jnp.where(one, -c, jnp.where(two, e, c * u - e * v))
            q = jnp.where(one, e, jnp.where(two, -a, a * v - e * u))
            for m in range(k + 2, SUB):
                cols[m] = jnp.where(pair, 0.0, cols[m]) - (p * down(u, m) + q * down(v, m)) * inv
            full_p, full_q = p * inv, q * inv
            solved = jnp.where(pair, 0.0, solved) - (full_p * down(solved, k) + full_q * down(solved, k + 1))
            ratio = e * (inv_root * inv_root)
            part_p = jnp.where(below, full_p, jnp.where(two, ratio, 0.0))
            part_q = jnp.where(below, full_q, 0.0)
            forward = forward - (part_p * down(forward, k) + part_q * down(forward, k + 1))
            second_scale = inv_det_root * (a * inv_root)
            diag_one, diag_two = a * inv_root, det * inv_det_root * inv_root
            if k == 0:
                scale, diagonal = jnp.where(one, inv_root, second_scale), jnp.where(one, diag_one, diag_two)
            else:
                scale = jnp.where(one, inv_root, jnp.where(two, second_scale, scale))
                diagonal = jnp.where(one, diag_one, jnp.where(two, diag_two, diagonal))
            steps.append((k, full_p, full_q, pair, u * inv_root, (v - u * ratio) * second_scale, one, two, below))
        forward = forward * scale
        lower = jnp.where(lane <= sub + base, forward, 0.0)
        panel[rows(b), left] = lower
        if end < blocks:
            upper[rows(b % group), :] = jnp.where(lane < border, lower, forward)
        gain = 1.0 / (diagonal + root)
        own = given
        for k, _, _, _, low, next_low, one, two, below in steps:
            first = down(own, k) * down(gain, k)
            second = (down(own, k + 1) - down(low, k + 1) * first) * down(gain, k + 1)
            rest = own - (low * first + next_low * second)
            own = jnp.where(below, rest, jnp.where(one, first, jnp.where(two, second, own)))
        panel[rows(b), right] = own
        if b + 1 < end:
            spread = given - root * own
            for k, full_p, full_q, pair, *_ in steps:
                spread = jnp.where(pair, 0.0, spread) - (full_p * down(spread, k) + full_q * down(spread, k + 1))
            for i in range(b + 1, end):
                columns = [stage[i % STAGES, k] for k in range(SUB)]
                value = jnp.where(inside, 0.0, panel[rows(i), left])
                panel[rows(i), left] = value - total([columns[k] * down(solved, k) for k in range(SUB)])
                panel[rows(i), right] = panel[rows(i), right] - total([columns[k] * down(spread, k) for k in range(SUB)])
        elif end < blocks:
            inner, far = pl.ds(border - SUB * group, SUB * group), pl.ds(border, BATCH - border)
            outer = halves(upper[...])
            wide = iota((BATCH - border, BATCH), 1)
            joined = jnp.logical_and(wide >= border - SUB * group, wide < border)
            change = dot3(outer, outer, TN)[border:, :]
            panel[far, left] = jnp.where(joined, 0.0, panel[far, left]) - change
            change = dot3(outer, halves(panel[inner, right]), TN)[border:, :]
            panel[far, right] = panel[far, right] - change
        fill(b)


def pick(select, value):
    high, rest = halves(value)
    low = (value - high.astype(F32) - rest.astype(F32)).astype(BF16)
    dot = functools.partial(jnp.dot, preferred_element_type=F32)
    return dot(select, high) + (dot(select, rest) + dot(select, low))


def lookup(pieces, index):
    inner, outer = index % BATCH, index // BATCH
    found = jnp.zeros(index.shape, pieces[0].dtype)
    for q, piece in enumerate(pieces):
        piece = jnp.broadcast_to(piece, index.shape)
        piece = jnp.take_along_axis(piece, inner, axis=1, mode="promise_in_bounds")
        found = jnp.where(outer == q, piece, found)
    return found


def iota(shape, dim):
    return lax.broadcasted_iota(jnp.int32, shape, dim)


def column_of(row):
    size = row.shape[1]
    eye = iota((size, size), 0) == iota((size, size), 1)
    return jnp.sum(jnp.where(eye, row, jnp.zeros_like(row)), axis=1, keepdims=True)


def filter_kernel(
    groups, layers, state_hbm, tiles_hbm, weight_hbm, azimuth_hbm, value_hbm, var_hbm, tile_bin_hbm, bins_hbm,
    order_hbm, out_ref,
    tiles, weight, azimuth, values, variances, tile_bin, bins, order,
    own_sums, sums, own_obs, every_obs, own_taper, every_taper,
    held, weights, selects, value_cols, root_cols, var_rows, tile_weights, gathered,
    panel, upper, stage, scaled_all, change_all,
    load_sem, sum_send, sum_recv, obs_send, obs_recv, taper_send, taper_recv,
):
    me, layer = lax.axis_index("obs"), lax.axis_index("rows")
    feet = weight.shape[0]
    batches, per = own_obs.shape[0], own_obs.shape[1]
    count, nobs = bins.shape
    tiles_dev, half = tile_bin.shape[0], TILE // 2
    padded = var_rows.shape[0]

    pairs = [
        (order_hbm, order), (value_hbm, values), (var_hbm, variances), (azimuth_hbm, azimuth), (tiles_hbm, tiles),
        (tile_bin_hbm, tile_bin), (state_hbm, out_ref), (weight_hbm, weight), (bins_hbm, bins),
    ]
    loads = [pltpu.make_async_copy(source, target, load_sem.at[i]) for i, (source, target) in enumerate(pairs)]
    for load in loads:
        load.start()
    barrier = pltpu.get_barrier_semaphore()
    for k in range(1, groups):
        pl.semaphore_signal(barrier, inc=1, device_id={"obs": lax.rem(me + k, groups)}, device_id_type=MESH)
    for k in range(1, layers):
        pl.semaphore_signal(barrier, inc=1, device_id={"rows": lax.rem(layer + k, layers)}, device_id_type=MESH)
    for load in loads[:8]:
        load.wait()

    partial = [jnp.zeros((feet, MEMBERS), F32) for _ in range(2)]
    listed = [column_of(tiles[t : t + 1, :].astype(F32)).astype(jnp.int32) for t in range(tiles.shape[0])]
    for tile in range(tiles_dev):
        number = layer * tiles_dev + tile
        chosen = jnp.zeros((feet, TILE), F32)
        for t in range(tiles.shape[0]):
            chosen = chosen + jnp.where(listed[t] == number, weight[:, t, :], 0.0)
        for h in range(2):
            partial[h] = partial[h] + jnp.dot(
                chosen[:, h * half : (h + 1) * half],
                out_ref[pl.ds(tile * TILE + h * half, half), :],
                precision=HIGH,
                preferred_element_type=F32,
            )
    for h in range(2):
        own_sums[h] = partial[h]
    loads[8].wait()
    pl.semaphore_wait(barrier, groups + layers - 2)

    def sum_copy(k):
        return pltpu.make_async_remote_copy(
            own_sums, sums.at[k], sum_send.at[k], sum_recv.at[k],
            device_id={"rows": lax.rem(layer + k, layers)}, device_id_type=MESH,
        )

    def obs_copy(k, b):
        return pltpu.make_async_remote_copy(
            own_obs.at[b], every_obs.at[b, me], obs_send.at[b], obs_recv.at[b],
            device_id={"obs": lax.rem(me + k, groups)}, device_id_type=MESH,
        )

    def taper_copy(k, b):
        wide = pl.ds(0, b * BATCH)
        return pltpu.make_async_remote_copy(
            own_taper.at[b, :, wide], every_taper.at[b, me, :, wide], taper_send.at[b], taper_recv.at[b],
            device_id={"obs": lax.rem(me + k, groups)}, device_id_type=MESH,
        )

    def all_copies(b):
        others, right = pl.ds(0, groups - 1), {"obs": lax.rem(me + 1, groups)}
        copies = [
            pltpu.make_async_remote_copy(
                every_obs.at[b, others], every_obs.at[b, others], obs_send.at[b], obs_recv.at[b],
                device_id=right, device_id_type=MESH,
            )
        ]
        if b:
            part = every_taper.at[b, others, :, pl.ds(0, b * BATCH)]
            copies.append(
                pltpu.make_async_remote_copy(
                    part, part, taper_send.at[b], taper_recv.at[b], device_id=right, device_id_type=MESH,
                )
            )
        return copies

    def peers(action):
        def one(k, carry):
            action(k)
            return carry

        lax.fori_loop(1, groups, one, 0)

    for k in range(1, layers):
        sum_copy(k).start()

    order_rows = [order[pl.ds(BATCH * q, BATCH)].reshape(1, BATCH) for q in range(batches)]
    base = me * count
    order_wide = jnp.concatenate(order_rows, 1)
    steps = iota((count, nobs), 1).astype(F32)
    member = jnp.logical_and(order_wide >= base, order_wide < base + count).astype(F32)
    local = iota((count, 1), 0)
    at = jnp.sum(jnp.where(order_wide == base + local, steps, 0.0), axis=1, keepdims=True)
    rank = jnp.sum(jnp.where(steps < at, member, 0.0), axis=1, keepdims=True)
    square = (count, count)
    rank_row = jnp.sum(jnp.where(iota(square, 0) == iota(square, 1), rank, 0.0), axis=0, keepdims=True)
    chooser = (iota(square, 0).astype(F32) == rank_row).astype(F32)
    ranked = jnp.dot(
        chooser.astype(BF16), taper_weight(bins[...]).astype(BF16), preferred_element_type=F32
    )
    for n in range(batches - 1):
        rest = count - (n + 1) * per
        index = jnp.broadcast_to(order_rows[n], (rest, BATCH))
        block = lookup([ranked[count - rest :, q * BATCH : (q + 1) * BATCH] for q in range(batches)], index)
        for b in range(n + 1, batches):
            own_taper[b, :, n * BATCH : (n + 1) * BATCH] = block[(b - n - 1) * per : (b - n) * per, :]
    for b in range(1, batches):
        every_taper[b, me, :, : b * BATCH] = own_taper[b, :, : b * BATCH]
    early = min(4, batches)
    for b in range(1, early):
        peers(lambda k: taper_copy(k, b).start())

    foot_of = (iota((count, feet), 0) // (count // feet) == iota((count, feet), 1)).astype(F32)
    spread_feet = jnp.dot(chooser.astype(BF16), foot_of.astype(BF16), preferred_element_type=F32).astype(BF16)
    angles = azimuth[...].reshape(1, count)
    cosines = jnp.sum(chooser * jnp.cos(angles), axis=1, keepdims=True)
    sines = jnp.sum(chooser * jnp.sin(angles), axis=1, keepdims=True)

    blank = [jnp.zeros((padded - batches, BATCH), jnp.int32)] if padded > batches else []
    orders = jnp.concatenate(order_rows + blank, 0)
    value_rows = lookup([values[pl.ds(BATCH * q, BATCH)].reshape(1, BATCH) for q in range(batches)], orders)
    variance_rows = lookup([variances[pl.ds(BATCH * q, BATCH)].reshape(1, BATCH) for q in range(batches)], orders)
    var_rows[...] = variance_rows
    for tile in range(tiles_dev):
        tapers = taper_weight(tile_bin[tile : tile + 1, :])
        tile_weights[tile] = lookup([tapers[:, q * BATCH : (q + 1) * BATCH] for q in range(batches)], orders)
    before = (iota((BATCH, BATCH), 0) < iota((BATCH, BATCH), 1)).astype(F32).astype(BF16)
    places = []
    for b in range(batches):
        group = order_rows[b] // count
        same = (iota((groups, BATCH), 0) == group).astype(F32)
        earlier = jnp.dot(same.astype(BF16), before, preferred_element_type=F32)
        places.append(group.astype(F32) * per + jnp.sum(same * earlier, axis=0, keepdims=True))
    empty = [jnp.zeros((padded - batches, BATCH), F32)] if padded > batches else []
    columns = jnp.transpose(jnp.concatenate(places + empty + [value_rows, jnp.sqrt(variance_rows)], 0))
    for b in range(batches):
        place = columns[:, b : b + 1]
        selects[b] = (place == iota((BATCH, BATCH), 1).astype(F32)).astype(F32).astype(BF16)
        value_cols[b] = columns[:, padded + b : padded + b + 1]
        root_cols[b] = jnp.broadcast_to(columns[:, 2 * padded + b : 2 * padded + b + 1], (BATCH, BATCH))

    for k in range(1, layers):
        sum_copy(k).wait_recv()
    winds = [own_sums[h] for h in range(2)]
    for k in range(1, layers):
        winds = [winds[h] + sums[k, h] for h in range(2)]
    winds = pick(spread_feet, jnp.concatenate(winds, 1))
    observed = model_function(winds[:, :MEMBERS], winds[:, MEMBERS:], cosines, sines)
    for b in range(batches):
        own_obs[b] = observed[b * per : (b + 1) * per, :]
        every_obs[b, me] = observed[b * per : (b + 1) * per, :]
    for b in range(batches):
        if b >= early:
            peers(lambda k: taper_copy(k, b).start())
        peers(lambda k: obs_copy(k, b).start())

    def arrive(b):
        for copy in all_copies(b):
            copy.wait_recv()

    def prepare(b):
        rows = pl.ds(b * BATCH, BATCH)
        if per % SUB == 0:
            obs = every_obs[b].reshape(BATCH, MEMBERS)
            taper = every_taper[b].reshape(BATCH, nobs)
        else:
            for g in range(groups):
                gathered[g * per : (g + 1) * per, :MEMBERS] = every_obs[b, g]
                gathered[g * per : (g + 1) * per, MEMBERS:] = every_taper[b, g]
            obs, taper = gathered[:, :MEMBERS], gathered[:, MEMBERS:]
        select = selects[b]
        held[rows, :] = pick(select, obs)
        if b:
            known = taper[:, : b * BATCH].astype(BF16)
            weights[rows, : b * BATCH] = jnp.dot(select, known, preferred_element_type=F32)

    def members_of(place):
        kind, number = place
        return (held, number * BATCH, BATCH) if kind == "obs" else (out_ref, number * TILE, TILE)

    def weight_of(place, m):
        kind, number = place
        if kind == "obs":
            return weights[pl.ds(number * BATCH, BATCH), pl.ds(m * BATCH, BATCH)]
        return jnp.broadcast_to(tile_weights[number, pl.ds(m, 1), :], (TILE, BATCH))

    def load(places):
        values = []
        for place in places:
            ref, first, size = members_of(place)
            values.append(ref[pl.ds(first, size), :])
        return jnp.concatenate(values, 0)

    def store(places, value):
        done = 0
        for place in places:
            ref, first, size = members_of(place)
            ref[pl.ds(first, size), :] = value[done : done + size, :]
            done += size

    def measure(places, scaled, m):
        product = dot3(halves(load(places)), scaled, NT)
        return product * jnp.concatenate([weight_of(place, m) for place in places], 0)

    def lagged(places, m):
        product = []

        def first():
            scaled = (scaled_all[m, :, :MEMBERS], scaled_all[m, :, MEMBERS:])
            product.append(halves(measure(places, scaled, m)))

        def second():
            change = (change_all[m, :, :MEMBERS], change_all[m, :, MEMBERS:])
            store(places, load(places) + dot3(product[0], change, NN))

        return [first, second]

    eye = iota((BATCH, BATCH), 0) == iota((BATCH, BATCH), 1)
    states = [("state", tile) for tile in range(tiles_dev)]

    def gains(n, work, ahead):
        batch_obs = held[pl.ds(n * BATCH, BATCH), :]
        row_mean = jnp.mean(batch_obs, axis=1, keepdims=True)
        perturb = batch_obs - row_mean
        innov = value_cols[n] - row_mean
        split = halves(perturb)
        scaled = halves(perturb * (1.0 / (MEMBERS - 1)))
        panel[:, :BATCH] = dot3(split, scaled, NT) + jnp.where(eye, var_rows[pl.ds(n, 1), :], 0.0)
        panel[:, BATCH:] = eye.astype(F32)
        scaled_all[n] = jnp.concatenate(scaled, 1)
        queue, slots, products = list(work), BATCH // SUB, []
        if ahead and (n or ahead == states):
            queue.append(lambda: products.append(halves(measure(ahead, scaled, n))))

        def fill(b):
            for _ in range(-(-len(queue) // (slots - b))):
                queue.pop(0)()

        factor(panel, root_cols.at[n], upper, stage, fill)
        first = panel[:, :BATCH]
        inverses = halves(jnp.concatenate([first, -panel[:, BATCH:]], 1))
        known = halves(jnp.concatenate([jnp.broadcast_to(innov, (BATCH, MEMBERS)), perturb], 0))
        middle = halves(dot3(inverses, known, NN))
        first = halves(first)
        if n == 0 and ahead != states:
            arrive(1)
            prepare(1)
            products.append(halves(measure(ahead, scaled, n)))
        rotated = halves(dot3(products[0], first, NT))
        store(ahead, load(ahead) + dot3(rotated, middle, NN))

        def change():
            change_all[n] = jnp.concatenate(halves(dot3(first, middle, TN)), 1)

        return change

    applied = [0] * batches
    arrive(0)
    prepare(0)
    change = None
    for n in range(batches):
        work = [change] if n else []
        if n:
            for b in [2, 3] if n == 1 else [n + 2]:
                if b < batches:
                    arrive(b)
                    work.append(functools.partial(prepare, b))
            seen = [b for b in range(n + 1, min(n + 3, batches))]
            for m in range(n):
                places = [("obs", b) for b in seen if applied[b] <= m]
                if m == n - 1:
                    places = places + states
                if places:
                    work += lagged(places, m)
            for b in seen:
                applied[b] = n
        ahead = [("obs", n + 1)] if n + 1 < batches else states
        change = gains(n, work, ahead)
        if n + 1 < batches:
            applied[n + 1] = n + 1
    for k in range(1, layers):
        sum_copy(k).wait_send()
    for b in range(batches):
        for copy in all_copies(b):
            copy.wait_send()


def shards(state, foot_tiles, foot_weight, azimuth, obs_value, obs_var, tile_bin, obs_bin, order):
    groups, layers = lax.axis_size("obs"), lax.axis_size("rows")
    count, nobs = obs_bin.shape
    batches, feet, tiles_dev = nobs // BATCH, foot_tiles.shape[0], tile_bin.shape[0]
    per, padded = count // batches, (nobs // BATCH + SUB - 1) // SUB * SUB
    dma, vmem = pltpu.SemaphoreType.DMA, pltpu.VMEM
    return pl.pallas_call(
        functools.partial(filter_kernel, groups, layers),
        out_shape=jax.ShapeDtypeStruct(state.shape, F32),
        in_specs=[ANY] * 9,
        out_specs=VMEM,
        scratch_shapes=[
            vmem(foot_tiles.shape[::-1], jnp.int32), vmem(foot_weight.shape, F32), vmem((count,), F32),
            vmem((nobs,), F32), vmem((nobs,), F32), vmem(tile_bin.shape, jnp.int32), vmem(obs_bin.shape, jnp.int32),
            vmem((nobs,), jnp.int32),
            vmem((2, feet, MEMBERS), F32), vmem((layers, 2, feet, MEMBERS), F32),
            vmem((batches, per, MEMBERS), F32), vmem((batches, groups, per, MEMBERS), F32),
            vmem((batches, per, nobs), F32), vmem((batches, groups, per, nobs), F32),
            vmem((nobs, MEMBERS), F32), vmem((nobs, nobs), F32), vmem((batches, BATCH, BATCH), BF16),
            vmem((batches, BATCH, 1), F32), vmem((batches, BATCH, BATCH), F32), vmem((padded, BATCH), F32),
            vmem((tiles_dev, padded, BATCH), F32), vmem((BATCH, MEMBERS + nobs), F32),
            vmem((BATCH, 2 * BATCH), F32), vmem((SPAN, BATCH), F32), vmem((STAGES, SUB, SUB, BATCH), F32),
            vmem((batches, BATCH, 2 * MEMBERS), BF16), vmem((batches, BATCH, 2 * MEMBERS), BF16),
            dma((9,)), dma((layers,)), dma((layers,)), dma((batches,)), dma((batches,)), dma((batches,)), dma((batches,)),
        ],
        compiler_params=pltpu.CompilerParams(
            collective_id=0, has_side_effects=True, vmem_limit_bytes=67043328
        ),
    )(state, foot_tiles.T, foot_weight, azimuth, obs_value, obs_var, tile_bin, obs_bin, order)


def solution(mesh):
    return jax.shard_map(
        shards,
        mesh=mesh,
        in_specs=(
            P(("obs", "rows"), None),
            P("obs", None),
            P("obs", None, None),
            P("obs"),
            P(),
            P(),
            P(("obs", "rows"), None),
            P("obs", None),
            P(),
        ),
        out_specs=P(("obs", "rows"), None),
        check_vma=False,
    )
```

```python
import functools

import jax
import jax.numpy as jnp
from jax import lax
from jax.experimental import pallas as pl
from jax.experimental.pallas import tpu as pltpu
from jax.sharding import PartitionSpec as P

MEMBERS = 256
BATCH = 128
TILE = 256
RADIUS = 8
SUB = 8
STAGES = 8
SPAN = 16
F32 = jnp.float32
BF16 = jnp.bfloat16


HIGH = lax.Precision.HIGHEST
MESH = pl.DeviceIdType.MESH
VMEM = pl.BlockSpec(memory_space=pltpu.VMEM)
ANY = pl.BlockSpec(memory_space=pl.ANY)


def model_function(east_wind, north_wind, cosines, sines):
    speed = jnp.sqrt(east_wind * east_wind + north_wind * north_wind + 1.0)
    cosine = (east_wind * cosines + north_wind * sines) / speed
    return jnp.exp(0.6 * jnp.log(speed)) * (0.7 + 0.4 * cosine + 0.6 * cosine * cosine)


def taper_weight(bins):
    scaled = 1.0 - bins.astype(F32) / RADIUS
    return jnp.where(bins < RADIUS, scaled * scaled, jnp.zeros_like(scaled))


def halves(value):
    high = value.astype(BF16)
    return high, (value - high.astype(F32)).astype(BF16)


def dot3(left, right, dims):
    (left_hi, left_lo), (right_hi, right_lo) = left, right
    (left_dim,), (right_dim,) = dims
    return lax.dot_general(
        jnp.concatenate([left_hi, left_lo, left_hi], left_dim),
        jnp.concatenate([right_hi, right_hi, right_lo], right_dim),
        (dims, ((), ())),
        preferred_element_type=F32,
    )


NN = ((1,), (0,))
NT = ((1,), (1,))
TN = ((0,), (0,))


def total(terms):
    while len(terms) > 1:
        terms = [a + b for a, b in zip(terms[::2], terms[1::2])]
    return terms[0]


def factor(panel, roots, upper, stage, fill):
    blocks, group = BATCH // SUB, upper.shape[0] // SUB
    lane = lax.broadcasted_iota(jnp.int32, (SUB, BATCH), 1)
    sub = lax.broadcasted_iota(jnp.int32, (SUB, BATCH), 0)
    left, right = pl.ds(0, BATCH), pl.ds(BATCH, BATCH)

    def across(value, column):
        lanes = jnp.full((SUB, BATCH), column, jnp.int32)
        return jnp.take_along_axis(value, lanes, axis=1, mode="promise_in_bounds")

    def down(value, row):
        return jnp.broadcast_to(value[row : row + 1, :], (SUB, BATCH))

    def rows(i):
        return pl.ds(SUB * i, SUB)

    for b in range(blocks):
        base = SUB * b
        end = (b // group + 1) * group
        border = SUB * end
        inside = jnp.logical_and(lane >= base, lane < base + SUB)
        start = panel[rows(b), left]
        given = panel[rows(b), right]
        root = roots[rows(b), :]
        cols = [across(start, base + k) for k in range(SUB)]
        for i in range(b + 1, end):
            value = panel[rows(i), left]
            for k in range(SUB):
                stage[i % STAGES, k] = across(value, base + k)
        solved = jnp.where(inside, (lane == sub + base).astype(F32), start)
        forward, scale, diagonal, steps = solved, None, None, []
        for k in range(0, SUB, 2):
            one, two = sub == k, sub == k + 1
            pair, below = jnp.logical_or(one, two), sub > k + 1
            u, v = cols[k], cols[k + 1]
            a, e, c = down(u, k), down(u, k + 1), down(v, k + 1)
            det = a * c - e * e
            inv_det_root, inv_root = lax.rsqrt(det), lax.rsqrt(a)
            inv = inv_det_root * inv_det_root
            p = jnp.where(one, -c, jnp.where(two, e, c * u - e * v))
            q = jnp.where(one, e, jnp.where(two, -a, a * v - e * u))
            for m in range(k + 2, SUB):
                cols[m] = jnp.where(pair, 0.0, cols[m]) - (p * down(u, m) + q * down(v, m)) * inv
            full_p, full_q = p * inv, q * inv
            solved = jnp.where(pair, 0.0, solved) - (full_p * down(solved, k) + full_q * down(solved, k + 1))
            ratio = e * (inv_root * inv_root)
            part_p = jnp.where(below, full_p, jnp.where(two, ratio, 0.0))
            part_q = jnp.where(below, full_q, 0.0)
            forward = forward - (part_p * down(forward, k) + part_q * down(forward, k + 1))
            second_scale = inv_det_root * (a * inv_root)
            diag_one, diag_two = a * inv_root, det * inv_det_root * inv_root
            if k == 0:
                scale, diagonal = jnp.where(one, inv_root, second_scale), jnp.where(one, diag_one, diag_two)
            else:
                scale = jnp.where(one, inv_root, jnp.where(two, second_scale, scale))
                diagonal = jnp.where(one, diag_one, jnp.where(two, diag_two, diagonal))
            steps.append((k, full_p, full_q, pair, u * inv_root, (v - u * ratio) * second_scale, one, two, below))
        forward = forward * scale
        lower = jnp.where(lane <= sub + base, forward, 0.0)
        panel[rows(b), left] = lower
        if end < blocks:
            upper[rows(b % group), :] = jnp.where(lane < border, lower, forward)
        gain = 1.0 / (diagonal + root)
        own = given
        for k, _, _, _, low, next_low, one, two, below in steps:
            first = down(own, k) * down(gain, k)
            second = (down(own, k + 1) - down(low, k + 1) * first) * down(gain, k + 1)
            rest = own - (low * first + next_low * second)
            own = jnp.where(below, rest, jnp.where(one, first, jnp.where(two, second, own)))
        panel[rows(b), right] = own
        if b + 1 < end:
            spread = given - root * own
            for k, full_p, full_q, pair, *_ in steps:
                spread = jnp.where(pair, 0.0, spread) - (full_p * down(spread, k) + full_q * down(spread, k + 1))
            for i in range(b + 1, end):
                columns = [stage[i % STAGES, k] for k in range(SUB)]
                value = jnp.where(inside, 0.0, panel[rows(i), left])
                panel[rows(i), left] = value - total([columns[k] * down(solved, k) for k in range(SUB)])
                panel[rows(i), right] = panel[rows(i), right] - total([columns[k] * down(spread, k) for k in range(SUB)])
        elif end < blocks:
            inner, far = pl.ds(border - SUB * group, SUB * group), pl.ds(border, BATCH - border)
            outer = halves(upper[...])
            wide = iota((BATCH - border, BATCH), 1)
            joined = jnp.logical_and(wide >= border - SUB * group, wide < border)
            change = dot3(outer, outer, TN)[border:, :]
            panel[far, left] = jnp.where(joined, 0.0, panel[far, left]) - change
            change = dot3(outer, halves(panel[inner, right]), TN)[border:, :]
            panel[far, right] = panel[far, right] - change
        fill(b)


def pick(select, value):
    high, rest = halves(value)
    low = (value - high.astype(F32) - rest.astype(F32)).astype(BF16)
    dot = functools.partial(jnp.dot, preferred_element_type=F32)
    return dot(select, high) + (dot(select, rest) + dot(select, low))


def lookup(pieces, index):
    inner, outer = index % BATCH, index // BATCH
    found = jnp.zeros(index.shape, pieces[0].dtype)
    for q, piece in enumerate(pieces):
        piece = jnp.broadcast_to(piece, index.shape)
        piece = jnp.take_along_axis(piece, inner, axis=1, mode="promise_in_bounds")
        found = jnp.where(outer == q, piece, found)
    return found


def iota(shape, dim):
    return lax.broadcasted_iota(jnp.int32, shape, dim)


def column_of(row):
    size = row.shape[1]
    eye = iota((size, size), 0) == iota((size, size), 1)
    return jnp.sum(jnp.where(eye, row, jnp.zeros_like(row)), axis=1, keepdims=True)


def filter_kernel(
    groups, layers, state_hbm, tiles_hbm, weight_hbm, azimuth_hbm, value_hbm, var_hbm, tile_bin_hbm, bins_hbm,
    order_hbm, out_ref,
    tiles, weight, azimuth, values, variances, tile_bin, bins, order,
    own_sums, sums, own_obs, every_obs, own_taper, every_taper,
    held, weights, selects, value_cols, root_cols, var_rows, tile_weights, gathered,
    panel, upper, stage, scaled_all, change_all,
    load_sem, sum_send, sum_recv, obs_send, obs_recv, taper_send, taper_recv,
):
    me, layer = lax.axis_index("obs"), lax.axis_index("rows")
    feet = weight.shape[0]
    batches, per = own_obs.shape[0], own_obs.shape[1]
    count, nobs = bins.shape
    tiles_dev, half = tile_bin.shape[0], TILE // 2
    padded = var_rows.shape[0]

    pairs = [
        (order_hbm, order), (value_hbm, values), (var_hbm, variances), (azimuth_hbm, azimuth), (tiles_hbm, tiles),
        (tile_bin_hbm, tile_bin), (state_hbm, out_ref), (weight_hbm, weight), (bins_hbm, bins),
    ]
    loads = [pltpu.make_async_copy(source, target, load_sem.at[i]) for i, (source, target) in enumerate(pairs)]
    barrier = pltpu.get_barrier_semaphore()
    for k in range(1, groups):
        pl.semaphore_signal(barrier, inc=1, device_id={"obs": lax.rem(me + k, groups)}, device_id_type=MESH)
    for k in range(1, layers):
        pl.semaphore_signal(barrier, inc=1, device_id={"rows": lax.rem(layer + k, layers)}, device_id_type=MESH)
    for load in loads:
        load.start()
    for load in loads[:8]:
        load.wait()

    partial = [jnp.zeros((feet, MEMBERS), F32) for _ in range(2)]
    listed = [column_of(tiles[t : t + 1, :].astype(F32)).astype(jnp.int32) for t in range(tiles.shape[0])]
    for tile in range(tiles_dev):
        number = layer * tiles_dev + tile
        chosen = jnp.zeros((feet, TILE), F32)
        for t in range(tiles.shape[0]):
            chosen = chosen + jnp.where(listed[t] == number, weight[:, t, :], 0.0)
        for h in range(2):
            partial[h] = partial[h] + jnp.dot(
                chosen[:, h * half : (h + 1) * half],
                out_ref[pl.ds(tile * TILE + h * half, half), :],
                precision=HIGH,
                preferred_element_type=F32,
            )
    for h in range(2):
        own_sums[h] = partial[h]
    loads[8].wait()
    pl.semaphore_wait(barrier, groups + layers - 2)

    def sum_copy(k):
        return pltpu.make_async_remote_copy(
            own_sums, sums.at[k], sum_send.at[k], sum_recv.at[k],
            device_id={"rows": lax.rem(layer + k, layers)}, device_id_type=MESH,
        )

    def obs_copy(k, b):
        return pltpu.make_async_remote_copy(
            own_obs.at[b], every_obs.at[b, me], obs_send.at[b], obs_recv.at[b],
            device_id={"obs": lax.rem(me + k, groups)}, device_id_type=MESH,
        )

    def taper_copy(k, b):
        wide = pl.ds(0, b * BATCH)
        return pltpu.make_async_remote_copy(
            own_taper.at[b, :, wide], every_taper.at[b, me, :, wide], taper_send.at[b], taper_recv.at[b],
            device_id={"obs": lax.rem(me + k, groups)}, device_id_type=MESH,
        )

    def all_copies(b):
        others, right = pl.ds(0, groups - 1), {"obs": lax.rem(me + 1, groups)}
        copies = [
            pltpu.make_async_remote_copy(
                every_obs.at[b, others], every_obs.at[b, others], obs_send.at[b], obs_recv.at[b],
                device_id=right, device_id_type=MESH,
            )
        ]
        if b:
            part = every_taper.at[b, others, :, pl.ds(0, b * BATCH)]
            copies.append(
                pltpu.make_async_remote_copy(
                    part, part, taper_send.at[b], taper_recv.at[b], device_id=right, device_id_type=MESH,
                )
            )
        return copies

    def peers(action):
        def one(k, carry):
            action(k)
            return carry

        lax.fori_loop(1, groups, one, 0)

    for k in range(1, layers):
        sum_copy(k).start()

    order_rows = [order[pl.ds(BATCH * q, BATCH)].reshape(1, BATCH) for q in range(batches)]
    base = me * count
    order_wide = jnp.concatenate(order_rows, 1)
    steps = iota((count, nobs), 1).astype(F32)
    member = jnp.logical_and(order_wide >= base, order_wide < base + count).astype(F32)
    local = iota((count, 1), 0)
    at = jnp.sum(jnp.where(order_wide == base + local, steps, 0.0), axis=1, keepdims=True)
    rank = jnp.sum(jnp.where(steps < at, member, 0.0), axis=1, keepdims=True)
    square = (count, count)
    rank_row = jnp.sum(jnp.where(iota(square, 0) == iota(square, 1), rank, 0.0), axis=0, keepdims=True)
    chooser = (iota(square, 0).astype(F32) == rank_row).astype(F32)
    ranked = jnp.dot(
        chooser.astype(BF16), taper_weight(bins[...]).astype(BF16), preferred_element_type=F32
    )
    for n in range(batches - 1):
        rest = count - (n + 1) * per
        index = jnp.broadcast_to(order_rows[n], (rest, BATCH))
        block = lookup([ranked[count - rest :, q * BATCH : (q + 1) * BATCH] for q in range(batches)], index)
        for b in range(n + 1, batches):
            own_taper[b, :, n * BATCH : (n + 1) * BATCH] = block[(b - n - 1) * per : (b - n) * per, :]
    for b in range(1, batches):
        every_taper[b, me, :, : b * BATCH] = own_taper[b, :, : b * BATCH]
    early = min(4, batches)
    for b in range(1, early):
        peers(lambda k: taper_copy(k, b).start())

    foot_of = (iota((count, feet), 0) // (count // feet) == iota((count, feet), 1)).astype(F32)
    spread_feet = jnp.dot(chooser.astype(BF16), foot_of.astype(BF16), preferred_element_type=F32).astype(BF16)
    angles = azimuth[...].reshape(1, count)
    cosines = jnp.sum(chooser * jnp.cos(angles), axis=1, keepdims=True)
    sines = jnp.sum(chooser * jnp.sin(angles), axis=1, keepdims=True)

    blank = [jnp.zeros((padded - batches, BATCH), jnp.int32)] if padded > batches else []
    orders = jnp.concatenate(order_rows + blank, 0)
    value_rows = lookup([values[pl.ds(BATCH * q, BATCH)].reshape(1, BATCH) for q in range(batches)], orders)
    variance_rows = lookup([variances[pl.ds(BATCH * q, BATCH)].reshape(1, BATCH) for q in range(batches)], orders)
    var_rows[...] = variance_rows
    for tile in range(tiles_dev):
        tapers = taper_weight(tile_bin[tile : tile + 1, :])
        tile_weights[tile] = lookup([tapers[:, q * BATCH : (q + 1) * BATCH] for q in range(batches)], orders)
    before = (iota((BATCH, BATCH), 0) < iota((BATCH, BATCH), 1)).astype(F32).astype(BF16)
    places = []
    for b in range(batches):
        group = order_rows[b] // count
        same = (iota((groups, BATCH), 0) == group).astype(F32)
        earlier = jnp.dot(same.astype(BF16), before, preferred_element_type=F32)
        places.append(group.astype(F32) * per + jnp.sum(same * earlier, axis=0, keepdims=True))
    empty = [jnp.zeros((padded - batches, BATCH), F32)] if padded > batches else []
    columns = jnp.transpose(jnp.concatenate(places + empty + [value_rows, jnp.sqrt(variance_rows)], 0))
    for b in range(batches):
        place = columns[:, b : b + 1]
        selects[b] = (place == iota((BATCH, BATCH), 1).astype(F32)).astype(F32).astype(BF16)
        value_cols[b] = columns[:, padded + b : padded + b + 1]
        root_cols[b] = jnp.broadcast_to(columns[:, 2 * padded + b : 2 * padded + b + 1], (BATCH, BATCH))

    for k in range(1, layers):
        sum_copy(k).wait_recv()
    winds = [own_sums[h] for h in range(2)]
    for k in range(1, layers):
        winds = [winds[h] + sums[k, h] for h in range(2)]
    winds = pick(spread_feet, jnp.concatenate(winds, 1))
    observed = model_function(winds[:, :MEMBERS], winds[:, MEMBERS:], cosines, sines)
    for b in range(batches):
        own_obs[b] = observed[b * per : (b + 1) * per, :]
        every_obs[b, me] = observed[b * per : (b + 1) * per, :]
    for b in range(batches):
        if b >= early:
            peers(lambda k: taper_copy(k, b).start())
        peers(lambda k: obs_copy(k, b).start())

    def arrive(b):
        for copy in all_copies(b):
            copy.wait_recv()

    def prepare(b):
        rows = pl.ds(b * BATCH, BATCH)
        if per % SUB == 0:
            obs = every_obs[b].reshape(BATCH, MEMBERS)
            taper = every_taper[b].reshape(BATCH, nobs)
        else:
            for g in range(groups):
                gathered[g * per : (g + 1) * per, :MEMBERS] = every_obs[b, g]
                gathered[g * per : (g + 1) * per, MEMBERS:] = every_taper[b, g]
            obs, taper = gathered[:, :MEMBERS], gathered[:, MEMBERS:]
        select = selects[b]
        held[rows, :] = pick(select, obs)
        if b:
            known = taper[:, : b * BATCH].astype(BF16)
            weights[rows, : b * BATCH] = jnp.dot(select, known, preferred_element_type=F32)

    def members_of(place):
        kind, number = place
        return (held, number * BATCH, BATCH) if kind == "obs" else (out_ref, number * TILE, TILE)

    def weight_of(place, m):
        kind, number = place
        if kind == "obs":
            return weights[pl.ds(number * BATCH, BATCH), pl.ds(m * BATCH, BATCH)]
        return jnp.broadcast_to(tile_weights[number, pl.ds(m, 1), :], (TILE, BATCH))

    def load(places):
        values = []
        for place in places:
            ref, first, size = members_of(place)
            values.append(ref[pl.ds(first, size), :])
        return jnp.concatenate(values, 0)

    def store(places, value):
        done = 0
        for place in places:
            ref, first, size = members_of(place)
            ref[pl.ds(first, size), :] = value[done : done + size, :]
            done += size

    def measure(places, scaled, m):
        product = dot3(halves(load(places)), scaled, NT)
        return product * jnp.concatenate([weight_of(place, m) for place in places], 0)

    def lagged(places, m):
        product = []

        def first():
            scaled = (scaled_all[m, :, :MEMBERS], scaled_all[m, :, MEMBERS:])
            product.append(halves(measure(places, scaled, m)))

        def second():
            change = (change_all[m, :, :MEMBERS], change_all[m, :, MEMBERS:])
            store(places, load(places) + dot3(product[0], change, NN))

        return [first, second]

    eye = iota((BATCH, BATCH), 0) == iota((BATCH, BATCH), 1)
    states = [("state", tile) for tile in range(tiles_dev)]

    def gains(n, work, ahead):
        batch_obs = held[pl.ds(n * BATCH, BATCH), :]
        row_mean = jnp.mean(batch_obs, axis=1, keepdims=True)
        perturb = batch_obs - row_mean
        innov = value_cols[n] - row_mean
        split = halves(perturb)
        scaled = halves(perturb * (1.0 / (MEMBERS - 1)))
        panel[:, :BATCH] = dot3(split, scaled, NT) + jnp.where(eye, var_rows[pl.ds(n, 1), :], 0.0)
        panel[:, BATCH:] = eye.astype(F32)
        scaled_all[n] = jnp.concatenate(scaled, 1)
        queue, slots, products = list(work), BATCH // SUB, []
        if ahead and (n or ahead == states):
            queue.append(lambda: products.append(halves(measure(ahead, scaled, n))))

        def fill(b):
            for _ in range(-(-len(queue) // (slots - b))):
                queue.pop(0)()

        factor(panel, root_cols.at[n], upper, stage, fill)
        first = panel[:, :BATCH]
        inverses = halves(jnp.concatenate([first, -panel[:, BATCH:]], 1))
        known = halves(jnp.concatenate([jnp.broadcast_to(innov, (BATCH, MEMBERS)), perturb], 0))
        middle = halves(dot3(inverses, known, NN))
        first = halves(first)
        if n == 0 and ahead != states:
            arrive(1)
            prepare(1)
            products.append(halves(measure(ahead, scaled, n)))
        rotated = halves(dot3(products[0], first, NT))
        store(ahead, load(ahead) + dot3(rotated, middle, NN))

        def change():
            change_all[n] = jnp.concatenate(halves(dot3(first, middle, TN)), 1)

        return change

    applied = [0] * batches
    arrive(0)
    prepare(0)
    change = None
    for n in range(batches):
        work = [change] if n else []
        if n:
            for b in [2, 3] if n == 1 else [n + 2]:
                if b < batches:
                    arrive(b)
                    work.append(functools.partial(prepare, b))
            seen = [b for b in range(n + 1, min(n + 3, batches))]
            for m in range(n):
                places = [("obs", b) for b in seen if applied[b] <= m]
                if m == n - 1:
                    places = places + states
                if places:
                    work += lagged(places, m)
            for b in seen:
                applied[b] = n
        ahead = [("obs", n + 1)] if n + 1 < batches else states
        change = gains(n, work, ahead)
        if n + 1 < batches:
            applied[n + 1] = n + 1
    for k in range(1, layers):
        sum_copy(k).wait_send()
    for b in range(batches):
        for copy in all_copies(b):
            copy.wait_send()


def shards(state, foot_tiles, foot_weight, azimuth, obs_value, obs_var, tile_bin, obs_bin, order):
    groups, layers = lax.axis_size("obs"), lax.axis_size("rows")
    count, nobs = obs_bin.shape
    batches, feet, tiles_dev = nobs // BATCH, foot_tiles.shape[0], tile_bin.shape[0]
    per, padded = count // batches, (nobs // BATCH + SUB - 1) // SUB * SUB
    dma, vmem = pltpu.SemaphoreType.DMA, pltpu.VMEM
    return pl.pallas_call(
        functools.partial(filter_kernel, groups, layers),
        out_shape=jax.ShapeDtypeStruct(state.shape, F32),
        in_specs=[ANY] * 9,
        out_specs=VMEM,
        scratch_shapes=[
            vmem(foot_tiles.shape[::-1], jnp.int32), vmem(foot_weight.shape, F32), vmem((count,), F32),
            vmem((nobs,), F32), vmem((nobs,), F32), vmem(tile_bin.shape, jnp.int32), vmem(obs_bin.shape, jnp.int32),
            vmem((nobs,), jnp.int32),
            vmem((2, feet, MEMBERS), F32), vmem((layers, 2, feet, MEMBERS), F32),
            vmem((batches, per, MEMBERS), F32), vmem((batches, groups, per, MEMBERS), F32),
            vmem((batches, per, nobs), F32), vmem((batches, groups, per, nobs), F32),
            vmem((nobs, MEMBERS), F32), vmem((nobs, nobs), F32), vmem((batches, BATCH, BATCH), BF16),
            vmem((batches, BATCH, 1), F32), vmem((batches, BATCH, BATCH), F32), vmem((padded, BATCH), F32),
            vmem((tiles_dev, padded, BATCH), F32), vmem((BATCH, MEMBERS + nobs), F32),
            vmem((BATCH, 2 * BATCH), F32), vmem((SPAN, BATCH), F32), vmem((STAGES, SUB, SUB, BATCH), F32),
            vmem((batches, BATCH, 2 * MEMBERS), BF16), vmem((batches, BATCH, 2 * MEMBERS), BF16),
            dma((9,)), dma((layers,)), dma((layers,)), dma((batches,)), dma((batches,)), dma((batches,)), dma((batches,)),
        ],
        compiler_params=pltpu.CompilerParams(
            collective_id=0, has_side_effects=True, vmem_limit_bytes=48 * 1024 * 1024
        ),
    )(*(
        pltpu.with_memory_space_constraint(array, pltpu.MemorySpace.HBM)
        for array in (state, foot_tiles.T, foot_weight, azimuth, obs_value, obs_var, tile_bin, obs_bin, order)
    ))


def solution(mesh):
    return jax.shard_map(
        shards,
        mesh=mesh,
        in_specs=(
            P(("obs", "rows"), None),
            P("obs", None),
            P("obs", None, None),
            P("obs"),
            P(),
            P(),
            P(("obs", "rows"), None),
            P("obs", None),
            P(),
        ),
        out_specs=P(("obs", "rows"), None),
        check_vma=False,
    )
```

```python
import functools

import jax
import jax.numpy as jnp
from jax import lax
from jax.experimental import pallas as pl
from jax.experimental.pallas import tpu as pltpu
from jax.sharding import PartitionSpec as P

MEMBERS = 256
BATCH = 128
TILE = 256
RADIUS = 8
SUB = 8
SPAN = 16
AHEAD = 2
F32 = jnp.float32
BF16 = jnp.bfloat16


HIGH = lax.Precision.HIGHEST
MESH = pl.DeviceIdType.MESH
VMEM = pl.BlockSpec(memory_space=pltpu.VMEM)
ANY = pl.BlockSpec(memory_space=pl.ANY)


def model_function(east_wind, north_wind, cosines, sines):
    speed = jnp.sqrt(east_wind * east_wind + north_wind * north_wind + 1.0)
    cosine = (east_wind * cosines + north_wind * sines) / speed
    return jnp.exp(0.6 * jnp.log(speed)) * (0.7 + 0.4 * cosine + 0.6 * cosine * cosine)


def taper_weight(bins):
    scaled = 1.0 - bins.astype(F32) / RADIUS
    return jnp.where(bins < RADIUS, scaled * scaled, jnp.zeros_like(scaled))


def halves(value):
    high = value.astype(BF16)
    return high, (value - high.astype(F32)).astype(BF16)


def dot3(left, right, dims):
    (left_hi, left_lo), (right_hi, right_lo) = left, right
    (left_dim,), (right_dim,) = dims
    return lax.dot_general(
        jnp.concatenate([left_hi, left_lo, left_hi], left_dim),
        jnp.concatenate([right_hi, right_hi, right_lo], right_dim),
        (dims, ((), ())),
        preferred_element_type=F32,
    )


NN = ((1,), (0,))
NT = ((1,), (1,))
TN = ((0,), (0,))


def total(terms):
    while len(terms) > 1:
        terms = [a + b for a, b in zip(terms[::2], terms[1::2])]
    return terms[0]


def factor(panel, roots, innov_row, solved_innov, upper, fill):
    blocks, group = BATCH // SUB, upper.shape[0] // SUB
    lane = lax.broadcasted_iota(jnp.int32, (SUB, BATCH), 1)
    sub = lax.broadcasted_iota(jnp.int32, (SUB, BATCH), 0)
    left, right = pl.ds(0, BATCH), pl.ds(BATCH, BATCH)

    def down(value, row):
        return jnp.broadcast_to(value[row : row + 1, :], (SUB, BATCH))

    def rows(i):
        return pl.ds(SUB * i, SUB)

    def column_block(value, i):
        lanes = sub + SUB * i
        return [
            jnp.take_along_axis(down(value, k), lanes, axis=1, mode="promise_in_bounds") for k in range(SUB)
        ]

    for b in range(blocks):
        base = SUB * b
        end = (b // group + 1) * group
        border = SUB * end
        inside = jnp.logical_and(lane >= base, lane < base + SUB)
        start = panel[rows(b), left]
        given = panel[rows(b), right]
        root = roots[rows(b), :]
        cols = column_block(start, b)
        near = min(end + AHEAD, blocks)
        coefficients = [column_block(start, i) for i in range(b + 1, near)]
        solved = jnp.where(inside, (lane == sub + base).astype(F32), start)
        forward, scale, diagonal, steps = solved, None, None, []
        for k in range(0, SUB, 2):
            one, two = sub == k, sub == k + 1
            pair, below = jnp.logical_or(one, two), sub > k + 1
            u, v = cols[k], cols[k + 1]
            a, e, c = down(u, k), down(u, k + 1), down(v, k + 1)
            det = a * c - e * e
            inv_det_root, inv_root = lax.rsqrt(det), lax.rsqrt(a)
            inv = inv_det_root * inv_det_root
            p = jnp.where(one, -c, jnp.where(two, e, c * u - e * v))
            q = jnp.where(one, e, jnp.where(two, -a, a * v - e * u))
            for m in range(k + 2, SUB):
                cols[m] = jnp.where(pair, 0.0, cols[m]) - (p * down(u, m) + q * down(v, m)) * inv
            full_p, full_q = p * inv, q * inv
            solved = jnp.where(pair, 0.0, solved) - (full_p * down(solved, k) + full_q * down(solved, k + 1))
            ratio = e * (inv_root * inv_root)
            part_p = jnp.where(below, full_p, jnp.where(two, ratio, 0.0))
            part_q = jnp.where(below, full_q, 0.0)
            forward = forward - (part_p * down(forward, k) + part_q * down(forward, k + 1))
            second_scale = inv_det_root * (a * inv_root)
            diag_one, diag_two = a * inv_root, det * inv_det_root * inv_root
            if k == 0:
                scale, diagonal = jnp.where(one, inv_root, second_scale), jnp.where(one, diag_one, diag_two)
            else:
                scale = jnp.where(one, inv_root, jnp.where(two, second_scale, scale))
                diagonal = jnp.where(one, diag_one, jnp.where(two, diag_two, diagonal))
            steps.append((k, full_p, full_q, pair, u * inv_root, (v - u * ratio) * second_scale, one, two, below))
        forward = forward * scale
        lower = jnp.where(lane <= sub + base, forward, 0.0)
        panel[rows(b), left] = lower
        solved_innov[rows(b), :] = jnp.sum(lower * innov_row, axis=1, keepdims=True)
        if end < blocks:
            upper[rows(b % group), :] = jnp.where(lane < border, lower, forward)
        gain = 1.0 / (diagonal + root)
        own = given
        for k, _, _, _, low, next_low, one, two, below in steps:
            first = down(own, k) * down(gain, k)
            second = (down(own, k + 1) - down(low, k + 1) * first) * down(gain, k + 1)
            rest = own - (low * first + next_low * second)
            own = jnp.where(below, rest, jnp.where(one, first, jnp.where(two, second, own)))
        panel[rows(b), right] = own
        if b + 1 < near:
            spread = given - root * own
            for k, full_p, full_q, pair, *_ in steps:
                spread = jnp.where(pair, 0.0, spread) - (full_p * down(spread, k) + full_q * down(spread, k + 1))
            for i, columns in zip(range(b + 1, near), coefficients):
                value = jnp.where(inside, 0.0, panel[rows(i), left])
                panel[rows(i), left] = value - total([columns[k] * down(solved, k) for k in range(SUB)])
                panel[rows(i), right] = panel[rows(i), right] - total([columns[k] * down(spread, k) for k in range(SUB)])
        if b + 1 == end and near < blocks:
            inner, first = pl.ds(border - SUB * group, SUB * group), SUB * near
            far = pl.ds(first, BATCH - first)
            outer = halves(upper[...])
            wide = iota((BATCH - first, BATCH), 1)
            joined = jnp.logical_and(wide >= border - SUB * group, wide < border)
            change = dot3(outer, outer, TN)[first:, :]
            panel[far, left] = jnp.where(joined, 0.0, panel[far, left]) - change
            change = dot3(outer, halves(panel[inner, right]), TN)[first:, :]
            panel[far, right] = panel[far, right] - change

        fill(b)


def pick(select, value):
    high, rest = halves(value)
    low = (value - high.astype(F32) - rest.astype(F32)).astype(BF16)
    return jnp.dot(
        jnp.concatenate([select] * 3, 1), jnp.concatenate([high, rest, low], 0), preferred_element_type=F32
    )


def lookup(pieces, index):
    inner, outer = index % BATCH, index // BATCH
    found = jnp.zeros(index.shape, pieces[0].dtype)
    for q, piece in enumerate(pieces):
        piece = jnp.broadcast_to(piece, index.shape)
        piece = jnp.take_along_axis(piece, inner, axis=1, mode="promise_in_bounds")
        found = jnp.where(outer == q, piece, found)
    return found


def iota(shape, dim):
    return lax.broadcasted_iota(jnp.int32, shape, dim)


def column_of(row):
    size = row.shape[1]
    eye = iota((size, size), 0) == iota((size, size), 1)
    return jnp.sum(jnp.where(eye, row, jnp.zeros_like(row)), axis=1, keepdims=True)


def filter_kernel(
    groups, layers, state_hbm, tiles_hbm, weight_hbm, azimuth_hbm, value_hbm, var_hbm, tile_bin_hbm, bins_hbm,
    order_hbm, out_ref,
    tiles, weight, azimuth, values, variances, tile_bin, bins, order,
    own_sums, sums, own_obs, every_obs, own_taper, every_taper,
    held, weights, selects, value_cols, root_cols, var_rows, tile_weights, gathered,
    panel, solved_innov, upper, scaled_all, change_all,
    load_sem, sum_send, sum_recv, obs_send, obs_recv, taper_send, taper_recv,
):
    me, layer = lax.axis_index("obs"), lax.axis_index("rows")
    feet = weight.shape[0]
    batches, per = own_obs.shape[0], own_obs.shape[1]
    count, nobs = bins.shape
    tiles_dev, half = tile_bin.shape[0], TILE // 2
    padded = var_rows.shape[0]

    pairs = [
        (order_hbm, order), (value_hbm, values), (var_hbm, variances), (azimuth_hbm, azimuth), (tiles_hbm, tiles),
        (tile_bin_hbm, tile_bin), (state_hbm, out_ref), (weight_hbm, weight), (bins_hbm, bins),
    ]
    loads = [pltpu.make_async_copy(source, target, load_sem.at[i]) for i, (source, target) in enumerate(pairs)]
    barrier = pltpu.get_barrier_semaphore()
    for k in range(1, groups):
        pl.semaphore_signal(barrier, inc=1, device_id={"obs": lax.rem(me + k, groups)}, device_id_type=MESH)
    for k in range(1, layers):
        pl.semaphore_signal(barrier, inc=1, device_id={"rows": lax.rem(layer + k, layers)}, device_id_type=MESH)
    for load in loads:
        load.start()
    for load in loads[:8]:
        load.wait()

    partial = [jnp.zeros((feet, MEMBERS), F32) for _ in range(2)]
    listed = [column_of(tiles[t : t + 1, :].astype(F32)).astype(jnp.int32) for t in range(tiles.shape[0])]
    for tile in range(tiles_dev):
        number = layer * tiles_dev + tile
        chosen = jnp.zeros((feet, TILE), F32)
        for t in range(tiles.shape[0]):
            chosen = chosen + jnp.where(listed[t] == number, weight[:, t, :], 0.0)
        for h in range(2):
            partial[h] = partial[h] + jnp.dot(
                chosen[:, h * half : (h + 1) * half],
                out_ref[pl.ds(tile * TILE + h * half, half), :],
                precision=HIGH,
                preferred_element_type=F32,
            )
    for h in range(2):
        own_sums[h] = partial[h]
    loads[8].wait()
    pl.semaphore_wait(barrier, groups + layers - 2)

    def sum_copy(k):
        return pltpu.make_async_remote_copy(
            own_sums, sums.at[k], sum_send.at[k], sum_recv.at[k],
            device_id={"rows": lax.rem(layer + k, layers)}, device_id_type=MESH,
        )

    def obs_copy(k, b):
        return pltpu.make_async_remote_copy(
            own_obs.at[b], every_obs.at[b, me], obs_send.at[b], obs_recv.at[b],
            device_id={"obs": lax.rem(me + k, groups)}, device_id_type=MESH,
        )

    def taper_copy(k, b):
        wide = pl.ds(0, b * BATCH)
        return pltpu.make_async_remote_copy(
            own_taper.at[b, :, wide], every_taper.at[b, me, :, wide], taper_send.at[b], taper_recv.at[b],
            device_id={"obs": lax.rem(me + k, groups)}, device_id_type=MESH,
        )

    def all_copies(b):
        others, right = pl.ds(0, groups - 1), {"obs": lax.rem(me + 1, groups)}
        copies = [
            pltpu.make_async_remote_copy(
                every_obs.at[b, others], every_obs.at[b, others], obs_send.at[b], obs_recv.at[b],
                device_id=right, device_id_type=MESH,
            )
        ]
        if b:
            part = every_taper.at[b, others, :, pl.ds(0, b * BATCH)]
            copies.append(
                pltpu.make_async_remote_copy(
                    part, part, taper_send.at[b], taper_recv.at[b], device_id=right, device_id_type=MESH,
                )
            )
        return copies

    def peers(action):
        def one(k, carry):
            action(k)
            return carry

        lax.fori_loop(1, groups, one, 0)

    for k in range(1, layers):
        sum_copy(k).start()

    order_rows = [order[pl.ds(BATCH * q, BATCH)].reshape(1, BATCH) for q in range(batches)]
    base = me * count
    order_wide = jnp.concatenate(order_rows, 1)
    steps = iota((count, nobs), 1).astype(F32)
    member = jnp.logical_and(order_wide >= base, order_wide < base + count).astype(F32)
    local = iota((count, 1), 0)
    at = jnp.sum(jnp.where(order_wide == base + local, steps, 0.0), axis=1, keepdims=True)
    rank = jnp.sum(jnp.where(steps < at, member, 0.0), axis=1, keepdims=True)
    square = (count, count)
    rank_row = jnp.sum(jnp.where(iota(square, 0) == iota(square, 1), rank, 0.0), axis=0, keepdims=True)
    chooser = (iota(square, 0).astype(F32) == rank_row).astype(F32)
    ranked = jnp.dot(
        chooser.astype(BF16), taper_weight(bins[...]).astype(BF16), preferred_element_type=F32
    )
    for n in range(batches - 1):
        rest = count - (n + 1) * per
        index = jnp.broadcast_to(order_rows[n], (rest, BATCH))
        block = lookup([ranked[count - rest :, q * BATCH : (q + 1) * BATCH] for q in range(batches)], index)
        for b in range(n + 1, batches):
            own_taper[b, :, n * BATCH : (n + 1) * BATCH] = block[(b - n - 1) * per : (b - n) * per, :]
    for b in range(1, batches):
        every_taper[b, me, :, : b * BATCH] = own_taper[b, :, : b * BATCH]
    early = min(4, batches)
    for b in range(1, early):
        peers(lambda k: taper_copy(k, b).start())

    foot_of = (iota((count, feet), 0) // (count // feet) == iota((count, feet), 1)).astype(F32)
    spread_feet = jnp.dot(chooser.astype(BF16), foot_of.astype(BF16), preferred_element_type=F32).astype(BF16)
    angles = azimuth[...].reshape(1, count)
    cosines = jnp.sum(chooser * jnp.cos(angles), axis=1, keepdims=True)
    sines = jnp.sum(chooser * jnp.sin(angles), axis=1, keepdims=True)

    blank = [jnp.zeros((padded - batches, BATCH), jnp.int32)] if padded > batches else []
    orders = jnp.concatenate(order_rows + blank, 0)
    value_rows = lookup([values[pl.ds(BATCH * q, BATCH)].reshape(1, BATCH) for q in range(batches)], orders)
    variance_rows = lookup([variances[pl.ds(BATCH * q, BATCH)].reshape(1, BATCH) for q in range(batches)], orders)
    var_rows[...] = variance_rows
    for tile in range(tiles_dev):
        tapers = taper_weight(tile_bin[tile : tile + 1, :])
        tile_weights[tile] = lookup([tapers[:, q * BATCH : (q + 1) * BATCH] for q in range(batches)], orders)
    before = (iota((BATCH, BATCH), 0) < iota((BATCH, BATCH), 1)).astype(F32).astype(BF16)
    places = []
    for b in range(batches):
        group = order_rows[b] // count
        same = (iota((groups, BATCH), 0) == group).astype(F32)
        earlier = jnp.dot(same.astype(BF16), before, preferred_element_type=F32)
        places.append(group.astype(F32) * per + jnp.sum(same * earlier, axis=0, keepdims=True))
    empty = [jnp.zeros((padded - batches, BATCH), F32)] if padded > batches else []
    columns = jnp.transpose(jnp.concatenate(places + empty + [value_rows, jnp.sqrt(variance_rows)], 0))
    for b in range(batches):
        place = columns[:, b : b + 1]
        selects[b] = (place == iota((BATCH, BATCH), 1).astype(F32)).astype(F32).astype(BF16)
        value_cols[b] = columns[:, padded + b : padded + b + 1]
        root_cols[b] = jnp.broadcast_to(columns[:, 2 * padded + b : 2 * padded + b + 1], (BATCH, BATCH))

    for k in range(1, layers):
        sum_copy(k).wait_recv()
    winds = [own_sums[h] for h in range(2)]
    for k in range(1, layers):
        winds = [winds[h] + sums[k, h] for h in range(2)]
    winds = pick(spread_feet, jnp.concatenate(winds, 1))
    observed = model_function(winds[:, :MEMBERS], winds[:, MEMBERS:], cosines, sines)
    for b in range(batches):
        own_obs[b] = observed[b * per : (b + 1) * per, :]
        every_obs[b, me] = observed[b * per : (b + 1) * per, :]
    for b in range(batches):
        if b >= early:
            peers(lambda k: taper_copy(k, b).start())
        peers(lambda k: obs_copy(k, b).start())

    def arrive(b):
        for copy in all_copies(b):
            copy.wait_recv()

    def prepare(b):
        rows = pl.ds(b * BATCH, BATCH)
        if per % SUB == 0:
            obs = every_obs[b].reshape(BATCH, MEMBERS)
            taper = every_taper[b].reshape(BATCH, nobs)
        else:
            for g in range(groups):
                gathered[g * per : (g + 1) * per, :MEMBERS] = every_obs[b, g]
                gathered[g * per : (g + 1) * per, MEMBERS:] = every_taper[b, g]
            obs, taper = gathered[:, :MEMBERS], gathered[:, MEMBERS:]
        select = selects[b]
        held[rows, :] = pick(select, obs)
        if b:
            known = taper[:, : b * BATCH].astype(BF16)
            weights[rows, : b * BATCH] = jnp.dot(select, known, preferred_element_type=F32)

    def members_of(place):
        kind, number = place
        return (held, number * BATCH, BATCH) if kind == "obs" else (out_ref, number * TILE, TILE)

    def weight_of(place, m):
        kind, number = place
        if kind == "obs":
            return weights[pl.ds(number * BATCH, BATCH), pl.ds(m * BATCH, BATCH)]
        return jnp.broadcast_to(tile_weights[number, pl.ds(m, 1), :], (TILE, BATCH))

    def load(places):
        values = []
        for place in places:
            ref, first, size = members_of(place)
            values.append(ref[pl.ds(first, size), :])
        return jnp.concatenate(values, 0)

    def store(places, value):
        done = 0
        for place in places:
            ref, first, size = members_of(place)
            ref[pl.ds(first, size), :] = value[done : done + size, :]
            done += size

    def measure(places, scaled, m):
        product = dot3(halves(load(places)), scaled, NT)
        return product * jnp.concatenate([weight_of(place, m) for place in places], 0)

    def lagged(places, m):
        product = []

        def first():
            scaled = (scaled_all[m, :, :MEMBERS], scaled_all[m, :, MEMBERS:])
            product.append(halves(measure(places, scaled, m)))

        def second():
            change = (change_all[m, :, :MEMBERS], change_all[m, :, MEMBERS:])
            store(places, load(places) + dot3(product[0], change, NN))

        return [first, second]

    eye = iota((BATCH, BATCH), 0) == iota((BATCH, BATCH), 1)
    states = [("state", tile) for tile in range(tiles_dev)]

    def gains(n, work, ahead):
        batch_obs = held[pl.ds(n * BATCH, BATCH), :]
        row_mean = jnp.mean(batch_obs, axis=1, keepdims=True)
        perturb = batch_obs - row_mean
        innov = value_cols[n] - row_mean
        innov_row = jnp.sum(jnp.where(eye, innov, 0.0), axis=0, keepdims=True)
        split = halves(perturb)
        scaled = halves(perturb * (1.0 / (MEMBERS - 1)))
        panel[:, :BATCH] = dot3(split, scaled, NT) + jnp.where(eye, var_rows[pl.ds(n, 1), :], 0.0)
        panel[:, BATCH:] = eye.astype(F32)
        scaled_all[n] = jnp.concatenate(scaled, 1)
        queue, slots, products = list(work), BATCH // SUB, []
        if ahead and (n or ahead == states):
            queue.append(lambda: products.append(halves(measure(ahead, scaled, n))))

        def fill(b):
            left = (slots - b) // 2
            if b % 2 and left:
                for _ in range(-(-len(queue) // left)):
                    queue.pop(0)()

        factor(panel, root_cols.at[n], innov_row, solved_innov, upper, fill)
        first = panel[:, :BATCH]
        middle = halves(solved_innov[...] - dot3(halves(panel[:, BATCH:]), split, NN))
        first = halves(first)
        if n == 0 and ahead != states:
            arrive(1)
            prepare(1)
            products.append(halves(measure(ahead, scaled, n)))
        rotated = halves(dot3(products[0], first, NT))
        store(ahead, load(ahead) + dot3(rotated, middle, NN))

        def change():
            change_all[n] = jnp.concatenate(halves(dot3(first, middle, TN)), 1)

        return change

    applied = [0] * batches
    arrive(0)
    prepare(0)
    change = None
    for n in range(batches):
        work = [change] if n else []
        if n:
            for b in [2, 3] if n == 1 else [n + 2]:
                if b < batches:
                    arrive(b)
                    work.append(functools.partial(prepare, b))
            seen = [b for b in range(n + 1, min(n + 3, batches))]
            for m in range(n):
                places = [("obs", b) for b in seen if applied[b] <= m]
                if m == n - 1:
                    places = places + states
                for part in range(0, len(places), 2):
                    work += lagged(places[part : part + 2], m)
            for b in seen:
                applied[b] = n
        ahead = [("obs", n + 1)] if n + 1 < batches else states
        change = gains(n, work, ahead)
        if n + 1 < batches:
            applied[n + 1] = n + 1
    for k in range(1, layers):
        sum_copy(k).wait_send()
    for b in range(batches):
        for copy in all_copies(b):
            copy.wait_send()


def shards(state, foot_tiles, foot_weight, azimuth, obs_value, obs_var, tile_bin, obs_bin, order):
    groups, layers = lax.axis_size("obs"), lax.axis_size("rows")
    count, nobs = obs_bin.shape
    batches, feet, tiles_dev = nobs // BATCH, foot_tiles.shape[0], tile_bin.shape[0]
    per, padded = count // batches, (nobs // BATCH + SUB - 1) // SUB * SUB
    dma, vmem = pltpu.SemaphoreType.DMA, pltpu.VMEM
    return pl.pallas_call(
        functools.partial(filter_kernel, groups, layers),
        out_shape=jax.ShapeDtypeStruct(state.shape, F32),
        in_specs=[ANY] * 9,
        out_specs=VMEM,
        scratch_shapes=[
            vmem(foot_tiles.shape[::-1], jnp.int32), vmem(foot_weight.shape, F32), vmem((count,), F32),
            vmem((nobs,), F32), vmem((nobs,), F32), vmem(tile_bin.shape, jnp.int32), vmem(obs_bin.shape, jnp.int32),
            vmem((nobs,), jnp.int32),
            vmem((2, feet, MEMBERS), F32), vmem((layers, 2, feet, MEMBERS), F32),
            vmem((batches, per, MEMBERS), F32), vmem((batches, groups, per, MEMBERS), F32),
            vmem((batches, per, nobs), F32), vmem((batches, groups, per, nobs), F32),
            vmem((nobs, MEMBERS), F32), vmem((nobs, nobs), F32), vmem((batches, BATCH, BATCH), BF16),
            vmem((batches, BATCH, 1), F32), vmem((batches, BATCH, BATCH), F32), vmem((padded, BATCH), F32),
            vmem((tiles_dev, padded, BATCH), F32), vmem((BATCH, MEMBERS + nobs), F32),
            vmem((BATCH, 2 * BATCH), F32), vmem((BATCH, 1), F32), vmem((SPAN, BATCH), F32),
            vmem((batches, BATCH, 2 * MEMBERS), BF16), vmem((batches, BATCH, 2 * MEMBERS), BF16),
            dma((9,)), dma((layers,)), dma((layers,)), dma((batches,)), dma((batches,)), dma((batches,)), dma((batches,)),
        ],
        compiler_params=pltpu.CompilerParams(
            collective_id=0, has_side_effects=True, vmem_limit_bytes=48 * 1024 * 1024
        ),
    )(*(
        pltpu.with_memory_space_constraint(array, pltpu.MemorySpace.HBM)
        for array in (state, foot_tiles.T, foot_weight, azimuth, obs_value, obs_var, tile_bin, obs_bin, order)
    ))


def solution(mesh):
    return jax.shard_map(
        shards,
        mesh=mesh,
        in_specs=(
            P(("obs", "rows"), None),
            P("obs", None),
            P("obs", None, None),
            P("obs"),
            P(),
            P(),
            P(("obs", "rows"), None),
            P("obs", None),
            P(),
        ),
        out_specs=P(("obs", "rows"), None),
        check_vma=False,
    )
```

```python
import functools

import jax
import jax.numpy as jnp
from jax import lax
from jax.experimental import pallas as pl
from jax.experimental.pallas import tpu as pltpu
from jax.sharding import PartitionSpec as P

MEMBERS = 256
BATCH = 128
TILE = 256
RADIUS = 8
SUB = 8
SPAN = 16
AHEAD = 2
F32 = jnp.float32
BF16 = jnp.bfloat16


HIGH = lax.Precision.HIGHEST
MESH = pl.DeviceIdType.MESH
VMEM = pl.BlockSpec(memory_space=pltpu.VMEM)
ANY = pl.BlockSpec(memory_space=pl.ANY)


def model_function(east_wind, north_wind, cosines, sines):
    speed = jnp.sqrt(east_wind * east_wind + north_wind * north_wind + 1.0)
    cosine = (east_wind * cosines + north_wind * sines) / speed
    return jnp.exp(0.6 * jnp.log(speed)) * (0.7 + 0.4 * cosine + 0.6 * cosine * cosine)


def taper_weight(bins):
    scaled = 1.0 - bins.astype(F32) / RADIUS
    return jnp.where(bins < RADIUS, scaled * scaled, jnp.zeros_like(scaled))


def halves(value):
    high = value.astype(BF16)
    return high, (value - high.astype(F32)).astype(BF16)


def dot3(left, right, dims):
    (left_hi, left_lo), (right_hi, right_lo) = left, right
    (left_dim,), (right_dim,) = dims
    return lax.dot_general(
        jnp.concatenate([left_hi, left_lo, left_hi], left_dim),
        jnp.concatenate([right_hi, right_hi, right_lo], right_dim),
        (dims, ((), ())),
        preferred_element_type=F32,
    )


NN = ((1,), (0,))
NT = ((1,), (1,))
TN = ((0,), (0,))


def total(terms):
    while len(terms) > 1:
        terms = [a + b for a, b in zip(terms[::2], terms[1::2])]
    return terms[0]


def factor(panel, roots, innov_row, solved_innov, upper, fill):
    blocks, group = BATCH // SUB, upper.shape[0] // SUB
    lane = lax.broadcasted_iota(jnp.int32, (SUB, BATCH), 1)
    sub = lax.broadcasted_iota(jnp.int32, (SUB, BATCH), 0)
    left, right = pl.ds(0, BATCH), pl.ds(BATCH, BATCH)

    def down(value, row):
        return jnp.broadcast_to(value[row : row + 1, :], (SUB, BATCH))

    def rows(i):
        return pl.ds(SUB * i, SUB)

    def column_block(value, i):
        lanes = sub + SUB * i
        return [
            jnp.take_along_axis(down(value, k), lanes, axis=1, mode="promise_in_bounds") for k in range(SUB)
        ]

    for b in range(blocks):
        base = SUB * b
        end = (b // group + 1) * group
        border = SUB * end
        inside = jnp.logical_and(lane >= base, lane < base + SUB)
        start = panel[rows(b), left]
        given = panel[rows(b), right]
        root = roots[rows(b), :]
        cols = column_block(start, b)
        near = min(end + AHEAD, blocks)
        coefficients = [column_block(start, i) for i in range(b + 1, near)]
        solved = jnp.where(inside, (lane == sub + base).astype(F32), start)
        forward, scale, diagonal, steps = solved, None, None, []
        for k in range(0, SUB, 2):
            one, two = sub == k, sub == k + 1
            pair, below = jnp.logical_or(one, two), sub > k + 1
            u, v = cols[k], cols[k + 1]
            a, e, c = down(u, k), down(u, k + 1), down(v, k + 1)
            det = a * c - e * e
            inv_det_root, inv_root = lax.rsqrt(det), lax.rsqrt(a)
            inv = inv_det_root * inv_det_root
            p = jnp.where(one, -c, jnp.where(two, e, c * u - e * v))
            q = jnp.where(one, e, jnp.where(two, -a, a * v - e * u))
            for m in range(k + 2, SUB):
                cols[m] = jnp.where(pair, 0.0, cols[m]) - (p * down(u, m) + q * down(v, m)) * inv
            full_p, full_q = p * inv, q * inv
            solved = jnp.where(pair, 0.0, solved) - (full_p * down(solved, k) + full_q * down(solved, k + 1))
            ratio = e * (inv_root * inv_root)
            part_p = jnp.where(below, full_p, jnp.where(two, ratio, 0.0))
            part_q = jnp.where(below, full_q, 0.0)
            forward = forward - (part_p * down(forward, k) + part_q * down(forward, k + 1))
            second_scale = inv_det_root * (a * inv_root)
            diag_one, diag_two = a * inv_root, det * inv_det_root * inv_root
            if k == 0:
                scale, diagonal = jnp.where(one, inv_root, second_scale), jnp.where(one, diag_one, diag_two)
            else:
                scale = jnp.where(one, inv_root, jnp.where(two, second_scale, scale))
                diagonal = jnp.where(one, diag_one, jnp.where(two, diag_two, diagonal))
            steps.append((k, full_p, full_q, pair, u * inv_root, (v - u * ratio) * second_scale, one, two, below))
        forward = forward * scale
        lower = jnp.where(lane <= sub + base, forward, 0.0)
        panel[rows(b), left] = lower
        solved_innov[rows(b), :] = jnp.sum(lower * innov_row, axis=1, keepdims=True)
        if end < blocks:
            upper[rows(b % group), :] = jnp.where(lane < border, lower, forward)
        gain = 1.0 / (diagonal + root)
        own = given
        for k, _, _, _, low, next_low, one, two, below in steps:
            first = down(own, k) * down(gain, k)
            second = (down(own, k + 1) - down(low, k + 1) * first) * down(gain, k + 1)
            rest = own - (low * first + next_low * second)
            own = jnp.where(below, rest, jnp.where(one, first, jnp.where(two, second, own)))
        panel[rows(b), right] = own
        if b + 1 < near:
            spread = given - root * own
            for k, full_p, full_q, pair, *_ in steps:
                spread = jnp.where(pair, 0.0, spread) - (full_p * down(spread, k) + full_q * down(spread, k + 1))
            for i, columns in zip(range(b + 1, near), coefficients):
                value = jnp.where(inside, 0.0, panel[rows(i), left])
                panel[rows(i), left] = value - total([columns[k] * down(solved, k) for k in range(SUB)])
                panel[rows(i), right] = panel[rows(i), right] - total([columns[k] * down(spread, k) for k in range(SUB)])
        if b + 1 == end and near < blocks:
            inner, first = pl.ds(border - SUB * group, SUB * group), SUB * near
            far = pl.ds(first, BATCH - first)
            outer = halves(upper[...])
            wide = iota((BATCH - first, BATCH), 1)
            joined = jnp.logical_and(wide >= border - SUB * group, wide < border)
            change = dot3(outer, outer, TN)[first:, :]
            panel[far, left] = jnp.where(joined, 0.0, panel[far, left]) - change
            change = dot3(outer, halves(panel[inner, right]), TN)[first:, :]
            panel[far, right] = panel[far, right] - change

        fill(b)


def pick(select, value):
    high, rest = halves(value)
    low = (value - high.astype(F32) - rest.astype(F32)).astype(BF16)
    return jnp.dot(
        jnp.concatenate([select] * 3, 1), jnp.concatenate([high, rest, low], 0), preferred_element_type=F32
    )


def lookup(pieces, index):
    inner, outer = index % BATCH, index // BATCH
    found = jnp.zeros(index.shape, pieces[0].dtype)
    for q, piece in enumerate(pieces):
        piece = jnp.broadcast_to(piece, index.shape)
        piece = jnp.take_along_axis(piece, inner, axis=1, mode="promise_in_bounds")
        found = jnp.where(outer == q, piece, found)
    return found


def iota(shape, dim):
    return lax.broadcasted_iota(jnp.int32, shape, dim)


def column_of(row):
    size = row.shape[1]
    eye = iota((size, size), 0) == iota((size, size), 1)
    return jnp.sum(jnp.where(eye, row, jnp.zeros_like(row)), axis=1, keepdims=True)


def filter_kernel(
    groups, layers, state_hbm, tiles_hbm, weight_hbm, azimuth_hbm, value_hbm, var_hbm, tile_bin_hbm, bins_hbm,
    order_hbm, out_ref,
    tiles, weight, azimuth, values, variances, tile_bin, bins, order,
    own_sums, sums, own_obs, every_obs, own_taper, every_taper,
    held, weights, selects, value_cols, root_cols, var_rows, tile_weights, gathered,
    panel, solved_innov, upper, scaled_all, change_all,
    load_sem, sum_send, sum_recv, obs_send, obs_recv, taper_send, taper_recv, pass_send, pass_recv,
):
    me, layer = lax.axis_index("obs"), lax.axis_index("rows")
    feet = weight.shape[0]
    batches, per = own_obs.shape[0], own_obs.shape[1]
    count, nobs = bins.shape
    tiles_dev, half = tile_bin.shape[0], TILE // 2
    padded = var_rows.shape[0]

    pairs = [
        (order_hbm, order), (value_hbm, values), (var_hbm, variances), (azimuth_hbm, azimuth), (tiles_hbm, tiles),
        (tile_bin_hbm, tile_bin), (state_hbm, out_ref), (weight_hbm, weight), (bins_hbm, bins),
    ]
    loads = [pltpu.make_async_copy(source, target, load_sem.at[i]) for i, (source, target) in enumerate(pairs)]
    barrier = pltpu.get_barrier_semaphore()
    for k in range(1, groups):
        pl.semaphore_signal(barrier, inc=1, device_id={"obs": lax.rem(me + k, groups)}, device_id_type=MESH)
    for k in range(1, layers):
        pl.semaphore_signal(barrier, inc=1, device_id={"rows": lax.rem(layer + k, layers)}, device_id_type=MESH)
    for load in loads:
        load.start()
    for load in loads[:8]:
        load.wait()

    partial = [jnp.zeros((feet, MEMBERS), F32) for _ in range(2)]
    listed = [column_of(tiles[t : t + 1, :].astype(F32)).astype(jnp.int32) for t in range(tiles.shape[0])]
    for tile in range(tiles_dev):
        number = layer * tiles_dev + tile
        chosen = jnp.zeros((feet, TILE), F32)
        for t in range(tiles.shape[0]):
            chosen = chosen + jnp.where(listed[t] == number, weight[:, t, :], 0.0)
        for h in range(2):
            partial[h] = partial[h] + jnp.dot(
                chosen[:, h * half : (h + 1) * half],
                out_ref[pl.ds(tile * TILE + h * half, half), :],
                precision=HIGH,
                preferred_element_type=F32,
            )
    for h in range(2):
        own_sums[h] = partial[h]
    loads[8].wait()
    pl.semaphore_wait(barrier, groups + layers - 2)

    def sum_copy(k):
        return pltpu.make_async_remote_copy(
            own_sums, sums.at[k], sum_send.at[k], sum_recv.at[k],
            device_id={"rows": lax.rem(layer + k, layers)}, device_id_type=MESH,
        )

    def obs_copy(k, b):
        return pltpu.make_async_remote_copy(
            own_obs.at[b], every_obs.at[b, me], obs_send.at[b], obs_recv.at[b],
            device_id={"obs": lax.rem(me + k, groups)}, device_id_type=MESH,
        )

    partner = {"obs": me + 1 - 2 * (me % 2)}

    def taper_part(b, first, size):
        return every_taper.at[b, pl.ds(first, size), :, pl.ds(0, b * BATCH)]

    def taper_copy(k, b):
        wide = pl.ds(0, b * BATCH)
        return pltpu.make_async_remote_copy(
            own_taper.at[b, :, wide], every_taper.at[b, me, :, wide], taper_send.at[b], taper_recv.at[b],
            device_id={"obs": lax.rem(me + 2 * k, groups)} if k is not None else partner, device_id_type=MESH,
        )

    def pass_copy(k, b):
        part = taper_part(b, lax.rem(me + 2 * k, groups), 1)
        return pltpu.make_async_remote_copy(
            part, part, pass_send.at[b], pass_recv.at[b], device_id=partner, device_id_type=MESH,
        )

    def taper_copies(b):
        direct, passed = taper_part(b, 0, groups // 2), taper_part(b, 0, groups // 2 - 1)
        return [
            pltpu.make_async_remote_copy(part, part, send, recv, device_id=partner, device_id_type=MESH)
            for part, send, recv in (
                (direct, taper_send.at[b], taper_recv.at[b]), (passed, pass_send.at[b], pass_recv.at[b])
            )
        ]

    def all_obs(b):
        part = every_obs.at[b, pl.ds(0, groups - 1)]
        return pltpu.make_async_remote_copy(
            part, part, obs_send.at[b], obs_recv.at[b], device_id=partner, device_id_type=MESH,
        )

    def peers(action, last=groups):
        def one(k, carry):
            action(k)
            return carry

        lax.fori_loop(1, last, one, 0)

    for k in range(1, layers):
        sum_copy(k).start()

    order_rows = [order[pl.ds(BATCH * q, BATCH)].reshape(1, BATCH) for q in range(batches)]
    base = me * count
    order_wide = jnp.concatenate(order_rows, 1)
    steps = iota((count, nobs), 1).astype(F32)
    member = jnp.logical_and(order_wide >= base, order_wide < base + count).astype(F32)
    local = iota((count, 1), 0)
    at = jnp.sum(jnp.where(order_wide == base + local, steps, 0.0), axis=1, keepdims=True)
    rank = jnp.sum(jnp.where(steps < at, member, 0.0), axis=1, keepdims=True)
    square = (count, count)
    rank_row = jnp.sum(jnp.where(iota(square, 0) == iota(square, 1), rank, 0.0), axis=0, keepdims=True)
    chooser = (iota(square, 0).astype(F32) == rank_row).astype(F32)
    ranked = jnp.dot(
        chooser.astype(BF16), taper_weight(bins[...]).astype(BF16), preferred_element_type=F32
    )
    for n in range(batches - 1):
        rest = count - (n + 1) * per
        index = jnp.broadcast_to(order_rows[n], (rest, BATCH))
        block = lookup([ranked[count - rest :, q * BATCH : (q + 1) * BATCH] for q in range(batches)], index)
        for b in range(n + 1, batches):
            own_taper[b, :, n * BATCH : (n + 1) * BATCH] = block[(b - n - 1) * per : (b - n) * per, :]
    for b in range(1, batches):
        every_taper[b, me, :, : b * BATCH] = own_taper[b, :, : b * BATCH]
    for b in range(1, batches):
        taper_copy(None, b).start()
        peers(lambda k: taper_copy(k, b).start(), groups // 2)

    foot_of = (iota((count, feet), 0) // (count // feet) == iota((count, feet), 1)).astype(F32)
    spread_feet = jnp.dot(chooser.astype(BF16), foot_of.astype(BF16), preferred_element_type=F32).astype(BF16)
    angles = azimuth[...].reshape(1, count)
    cosines = jnp.sum(chooser * jnp.cos(angles), axis=1, keepdims=True)
    sines = jnp.sum(chooser * jnp.sin(angles), axis=1, keepdims=True)

    blank = [jnp.zeros((padded - batches, BATCH), jnp.int32)] if padded > batches else []
    orders = jnp.concatenate(order_rows + blank, 0)
    value_rows = lookup([values[pl.ds(BATCH * q, BATCH)].reshape(1, BATCH) for q in range(batches)], orders)
    variance_rows = lookup([variances[pl.ds(BATCH * q, BATCH)].reshape(1, BATCH) for q in range(batches)], orders)
    var_rows[...] = variance_rows
    for tile in range(tiles_dev):
        tapers = taper_weight(tile_bin[tile : tile + 1, :])
        tile_weights[tile] = lookup([tapers[:, q * BATCH : (q + 1) * BATCH] for q in range(batches)], orders)
    before = (iota((BATCH, BATCH), 0) < iota((BATCH, BATCH), 1)).astype(F32).astype(BF16)
    places = []
    for b in range(batches):
        group = order_rows[b] // count
        same = (iota((groups, BATCH), 0) == group).astype(F32)
        earlier = jnp.dot(same.astype(BF16), before, preferred_element_type=F32)
        places.append(group.astype(F32) * per + jnp.sum(same * earlier, axis=0, keepdims=True))
    empty = [jnp.zeros((padded - batches, BATCH), F32)] if padded > batches else []
    columns = jnp.transpose(jnp.concatenate(places + empty + [value_rows, jnp.sqrt(variance_rows)], 0))
    for b in range(batches):
        place = columns[:, b : b + 1]
        selects[b] = (place == iota((BATCH, BATCH), 1).astype(F32)).astype(F32).astype(BF16)
        value_cols[b] = columns[:, padded + b : padded + b + 1]
        root_cols[b] = jnp.broadcast_to(columns[:, 2 * padded + b : 2 * padded + b + 1], (BATCH, BATCH))

    for k in range(1, layers):
        sum_copy(k).wait_recv()
    winds = [own_sums[h] for h in range(2)]
    for k in range(1, layers):
        winds = [winds[h] + sums[k, h] for h in range(2)]
    winds = pick(spread_feet, jnp.concatenate(winds, 1))
    observed = model_function(winds[:, :MEMBERS], winds[:, MEMBERS:], cosines, sines)
    for b in range(batches):
        own_obs[b] = observed[b * per : (b + 1) * per, :]
        every_obs[b, me] = observed[b * per : (b + 1) * per, :]
    for b in range(batches):
        peers(lambda k: obs_copy(k, b).start())
    for b in range(1, batches):
        taper_copies(b)[0].wait_recv()
        peers(lambda k: pass_copy(k, b).start(), groups // 2)

    def arrive(b):
        all_obs(b).wait_recv()
        if b:
            taper_copies(b)[1].wait_recv()

    def prepare(b):
        rows = pl.ds(b * BATCH, BATCH)
        if per % SUB == 0:
            obs = every_obs[b].reshape(BATCH, MEMBERS)
            taper = every_taper[b].reshape(BATCH, nobs)
        else:
            for g in range(groups):
                gathered[g * per : (g + 1) * per, :MEMBERS] = every_obs[b, g]
                gathered[g * per : (g + 1) * per, MEMBERS:] = every_taper[b, g]
            obs, taper = gathered[:, :MEMBERS], gathered[:, MEMBERS:]
        select = selects[b]
        held[rows, :] = pick(select, obs)
        if b:
            known = taper[:, : b * BATCH].astype(BF16)
            weights[rows, : b * BATCH] = jnp.dot(select, known, preferred_element_type=F32)

    def members_of(place):
        kind, number = place
        return (held, number * BATCH, BATCH) if kind == "obs" else (out_ref, number * TILE, TILE)

    def weight_of(place, m):
        kind, number = place
        if kind == "obs":
            return weights[pl.ds(number * BATCH, BATCH), pl.ds(m * BATCH, BATCH)]
        return jnp.broadcast_to(tile_weights[number, pl.ds(m, 1), :], (TILE, BATCH))

    def load(places):
        values = []
        for place in places:
            ref, first, size = members_of(place)
            values.append(ref[pl.ds(first, size), :])
        return jnp.concatenate(values, 0)

    def store(places, value):
        done = 0
        for place in places:
            ref, first, size = members_of(place)
            ref[pl.ds(first, size), :] = value[done : done + size, :]
            done += size

    def measure(places, scaled, m):
        product = dot3(halves(load(places)), scaled, NT)
        return product * jnp.concatenate([weight_of(place, m) for place in places], 0)

    def lagged(places, m):
        product = []

        def first():
            scaled = (scaled_all[m, :, :MEMBERS], scaled_all[m, :, MEMBERS:])
            product.append(halves(measure(places, scaled, m)))

        def second():
            change = (change_all[m, :, :MEMBERS], change_all[m, :, MEMBERS:])
            store(places, load(places) + dot3(product[0], change, NN))

        return [first, second]

    eye = iota((BATCH, BATCH), 0) == iota((BATCH, BATCH), 1)
    states = [("state", tile) for tile in range(tiles_dev)]

    def gains(n, work, ahead):
        batch_obs = held[pl.ds(n * BATCH, BATCH), :]
        row_mean = jnp.mean(batch_obs, axis=1, keepdims=True)
        perturb = batch_obs - row_mean
        innov = value_cols[n] - row_mean
        innov_row = jnp.sum(jnp.where(eye, innov, 0.0), axis=0, keepdims=True)
        split = halves(perturb)
        scaled = halves(perturb * (1.0 / (MEMBERS - 1)))
        panel[:, :BATCH] = dot3(split, scaled, NT) + jnp.where(eye, var_rows[pl.ds(n, 1), :], 0.0)
        panel[:, BATCH:] = eye.astype(F32)
        scaled_all[n] = jnp.concatenate(scaled, 1)
        queue, slots, products = list(work), BATCH // SUB, []
        queue.append(lambda: products.append(halves(measure(ahead, scaled, n))))

        def fill(b):
            left = (slots - b) // 2
            if b % 2 and left:
                for _ in range(-(-len(queue) // left)):
                    queue.pop(0)()

        factor(panel, root_cols.at[n], innov_row, solved_innov, upper, fill)
        first = panel[:, :BATCH]
        middle = halves(solved_innov[...] - dot3(halves(panel[:, BATCH:]), split, NN))
        first = halves(first)
        rotated = halves(dot3(products[0], first, NT))
        store(ahead, load(ahead) + dot3(rotated, middle, NN))

        def change():
            change_all[n] = jnp.concatenate(halves(dot3(first, middle, TN)), 1)

        return change

    applied = [0] * batches
    arrive(0)
    prepare(0)
    change = None
    for n in range(batches):
        work = [change] if n else []
        if n == 0 and batches > 1:
            work = [lambda: None] * 3 + [functools.partial(arrive, 1), functools.partial(prepare, 1)]
        if n:
            for b in [2, 3] if n == 1 else [n + 2]:
                if b < batches:
                    arrive(b)
                    work.append(functools.partial(prepare, b))
            seen = [b for b in range(n + 1, min(n + 3, batches))]
            for m in range(n):
                places = [("obs", b) for b in seen if applied[b] <= m]
                if m == n - 1:
                    places = places + states
                for part in range(0, len(places), 2):
                    work += lagged(places[part : part + 2], m)
            for b in seen:
                applied[b] = n
        ahead = [("obs", n + 1)] if n + 1 < batches else states
        change = gains(n, work, ahead)
        if n + 1 < batches:
            applied[n + 1] = n + 1
    for k in range(1, layers):
        sum_copy(k).wait_send()
    for b in range(batches):
        all_obs(b).wait_send()
        if b:
            for copy in taper_copies(b):
                copy.wait_send()


def shards(state, foot_tiles, foot_weight, azimuth, obs_value, obs_var, tile_bin, obs_bin, order):
    groups, layers = lax.axis_size("obs"), lax.axis_size("rows")
    count, nobs = obs_bin.shape
    batches, feet, tiles_dev = nobs // BATCH, foot_tiles.shape[0], tile_bin.shape[0]
    per, padded = count // batches, (nobs // BATCH + SUB - 1) // SUB * SUB
    dma, vmem = pltpu.SemaphoreType.DMA, pltpu.VMEM
    return pl.pallas_call(
        functools.partial(filter_kernel, groups, layers),
        out_shape=jax.ShapeDtypeStruct(state.shape, F32),
        in_specs=[ANY] * 9,
        out_specs=VMEM,
        scratch_shapes=[
            vmem(foot_tiles.shape[::-1], jnp.int32), vmem(foot_weight.shape, F32), vmem((count,), F32),
            vmem((nobs,), F32), vmem((nobs,), F32), vmem(tile_bin.shape, jnp.int32), vmem(obs_bin.shape, jnp.int32),
            vmem((nobs,), jnp.int32),
            vmem((2, feet, MEMBERS), F32), vmem((layers, 2, feet, MEMBERS), F32),
            vmem((batches, per, MEMBERS), F32), vmem((batches, groups, per, MEMBERS), F32),
            vmem((batches, per, nobs), F32), vmem((batches, groups, per, nobs), F32),
            vmem((nobs, MEMBERS), F32), vmem((nobs, nobs), F32), vmem((batches, BATCH, BATCH), BF16),
            vmem((batches, BATCH, 1), F32), vmem((batches, BATCH, BATCH), F32), vmem((padded, BATCH), F32),
            vmem((tiles_dev, padded, BATCH), F32), vmem((BATCH, MEMBERS + nobs), F32),
            vmem((BATCH, 2 * BATCH), F32), vmem((BATCH, 1), F32), vmem((SPAN, BATCH), F32),
            vmem((batches, BATCH, 2 * MEMBERS), BF16), vmem((batches, BATCH, 2 * MEMBERS), BF16),
            dma((9,)), dma((layers,)), dma((layers,)), *[dma((batches,)) for _ in range(6)],
        ],
        compiler_params=pltpu.CompilerParams(
            collective_id=0, has_side_effects=True, vmem_limit_bytes=48 * 1024 * 1024
        ),
    )(*(
        pltpu.with_memory_space_constraint(array, pltpu.MemorySpace.HBM)
        for array in (state, foot_tiles.T, foot_weight, azimuth, obs_value, obs_var, tile_bin, obs_bin, order)
    ))


def solution(mesh):
    return jax.shard_map(
        shards,
        mesh=mesh,
        in_specs=(
            P(("obs", "rows"), None),
            P("obs", None),
            P("obs", None, None),
            P("obs"),
            P(),
            P(),
            P(("obs", "rows"), None),
            P("obs", None),
            P(),
        ),
        out_specs=P(("obs", "rows"), None),
        check_vma=False,
    )
```

```python
import functools

import jax
import jax.numpy as jnp
from jax import lax
from jax.experimental import pallas as pl
from jax.experimental.pallas import tpu as pltpu
from jax.sharding import PartitionSpec as P

MEMBERS = 256
BATCH = 128
TILE = 256
RADIUS = 8
SUB = 8
SPAN = 16
AHEAD = 2
F32 = jnp.float32
BF16 = jnp.bfloat16


HIGH = lax.Precision.HIGHEST
MESH = pl.DeviceIdType.MESH
VMEM = pl.BlockSpec(memory_space=pltpu.VMEM)
ANY = pl.BlockSpec(memory_space=pl.ANY)


def model_function(east_wind, north_wind, cosines, sines):
    speed = jnp.sqrt(east_wind * east_wind + north_wind * north_wind + 1.0)
    cosine = (east_wind * cosines + north_wind * sines) / speed
    return jnp.exp(0.6 * jnp.log(speed)) * (0.7 + 0.4 * cosine + 0.6 * cosine * cosine)


def taper_weight(bins):
    scaled = 1.0 - bins.astype(F32) / RADIUS
    return jnp.where(bins < RADIUS, scaled * scaled, jnp.zeros_like(scaled))


def halves(value):
    high = value.astype(BF16)
    return high, (value - high.astype(F32)).astype(BF16)


def dot3(left, right, dims):
    (left_hi, left_lo), (right_hi, right_lo) = left, right
    (left_dim,), (right_dim,) = dims
    return lax.dot_general(
        jnp.concatenate([left_hi, left_lo, left_hi], left_dim),
        jnp.concatenate([right_hi, right_hi, right_lo], right_dim),
        (dims, ((), ())),
        preferred_element_type=F32,
    )


NN = ((1,), (0,))
NT = ((1,), (1,))
TN = ((0,), (0,))


def total(terms):
    while len(terms) > 1:
        terms = [a + b for a, b in zip(terms[::2], terms[1::2])]
    return terms[0]


def factor(panel, roots, innov_row, solved_innov, upper, fill):
    blocks, group = BATCH // SUB, upper.shape[0] // SUB
    lane = lax.broadcasted_iota(jnp.int32, (SUB, BATCH), 1)
    sub = lax.broadcasted_iota(jnp.int32, (SUB, BATCH), 0)
    left, right = pl.ds(0, BATCH), pl.ds(BATCH, BATCH)

    def down(value, row):
        return jnp.broadcast_to(value[row : row + 1, :], (SUB, BATCH))

    def rows(i):
        return pl.ds(SUB * i, SUB)

    def column_block(value, i):
        lanes = sub + SUB * i
        return [
            jnp.take_along_axis(down(value, k), lanes, axis=1, mode="promise_in_bounds") for k in range(SUB)
        ]

    for b in range(blocks):
        base = SUB * b
        end = (b // group + 1) * group
        border = SUB * end
        inside = jnp.logical_and(lane >= base, lane < base + SUB)
        start = panel[rows(b), left]
        given = panel[rows(b), right]
        root = roots[rows(b), :]
        cols = column_block(start, b)
        near = min(end + AHEAD, blocks)
        coefficients = [column_block(start, i) for i in range(b + 1, near)]
        solved = jnp.where(inside, (lane == sub + base).astype(F32), start)
        forward, scale, diagonal, steps = solved, None, None, []
        for k in range(0, SUB, 2):
            one, two = sub == k, sub == k + 1
            pair, below = jnp.logical_or(one, two), sub > k + 1
            u, v = cols[k], cols[k + 1]
            a, e, c = down(u, k), down(u, k + 1), down(v, k + 1)
            det = a * c - e * e
            inv_det_root, inv_root = lax.rsqrt(det), lax.rsqrt(a)
            inv = inv_det_root * inv_det_root
            p = jnp.where(one, -c, jnp.where(two, e, c * u - e * v))
            q = jnp.where(one, e, jnp.where(two, -a, a * v - e * u))
            for m in range(k + 2, SUB):
                cols[m] = jnp.where(pair, 0.0, cols[m]) - (p * down(u, m) + q * down(v, m)) * inv
            full_p, full_q = p * inv, q * inv
            solved = jnp.where(pair, 0.0, solved) - (full_p * down(solved, k) + full_q * down(solved, k + 1))
            ratio = e * (inv_root * inv_root)
            part_p = jnp.where(below, full_p, jnp.where(two, ratio, 0.0))
            part_q = jnp.where(below, full_q, 0.0)
            forward = forward - (part_p * down(forward, k) + part_q * down(forward, k + 1))
            second_scale = inv_det_root * (a * inv_root)
            diag_one, diag_two = a * inv_root, det * inv_det_root * inv_root
            if k == 0:
                scale, diagonal = jnp.where(one, inv_root, second_scale), jnp.where(one, diag_one, diag_two)
            else:
                scale = jnp.where(one, inv_root, jnp.where(two, second_scale, scale))
                diagonal = jnp.where(one, diag_one, jnp.where(two, diag_two, diagonal))
            steps.append((k, full_p, full_q, pair, u * inv_root, (v - u * ratio) * second_scale, one, two, below))
        forward = forward * scale
        lower = jnp.where(lane <= sub + base, forward, 0.0)
        panel[rows(b), left] = lower
        solved_innov[rows(b), :] = jnp.sum(lower * innov_row, axis=1, keepdims=True)
        if end < blocks:
            upper[rows(b % group), :] = jnp.where(lane < border, lower, forward)
        gain = 1.0 / (diagonal + root)
        own = given
        for k, _, _, _, low, next_low, one, two, below in steps:
            first = down(own, k) * down(gain, k)
            second = (down(own, k + 1) - down(low, k + 1) * first) * down(gain, k + 1)
            rest = own - (low * first + next_low * second)
            own = jnp.where(below, rest, jnp.where(one, first, jnp.where(two, second, own)))
        panel[rows(b), right] = own
        if b + 1 < near:
            spread = given - root * own
            for k, full_p, full_q, pair, *_ in steps:
                spread = jnp.where(pair, 0.0, spread) - (full_p * down(spread, k) + full_q * down(spread, k + 1))
            for i, columns in zip(range(b + 1, near), coefficients):
                value = jnp.where(inside, 0.0, panel[rows(i), left])
                panel[rows(i), left] = value - total([columns[k] * down(solved, k) for k in range(SUB)])
                panel[rows(i), right] = panel[rows(i), right] - total([columns[k] * down(spread, k) for k in range(SUB)])
        if b + 1 == end and near < blocks:
            inner, first = pl.ds(border - SUB * group, SUB * group), SUB * near
            far = pl.ds(first, BATCH - first)
            outer = halves(upper[...])
            wide = iota((BATCH - first, BATCH), 1)
            joined = jnp.logical_and(wide >= border - SUB * group, wide < border)
            change = dot3(outer, outer, TN)[first:, :]
            panel[far, left] = jnp.where(joined, 0.0, panel[far, left]) - change
            change = dot3(outer, halves(panel[inner, right]), TN)[first:, :]
            panel[far, right] = panel[far, right] - change

        fill(b)


def pick(select, value):
    high, rest = halves(value)
    low = (value - high.astype(F32) - rest.astype(F32)).astype(BF16)
    return jnp.dot(
        jnp.concatenate([select] * 3, 1), jnp.concatenate([high, rest, low], 0), preferred_element_type=F32
    )


def lookup(pieces, index):
    inner, outer = index % BATCH, index // BATCH
    found = jnp.zeros(index.shape, pieces[0].dtype)
    for q, piece in enumerate(pieces):
        piece = jnp.broadcast_to(piece, index.shape)
        piece = jnp.take_along_axis(piece, inner, axis=1, mode="promise_in_bounds")
        found = jnp.where(outer == q, piece, found)
    return found


def iota(shape, dim):
    return lax.broadcasted_iota(jnp.int32, shape, dim)


def column_of(row):
    size = row.shape[1]
    eye = iota((size, size), 0) == iota((size, size), 1)
    return jnp.sum(jnp.where(eye, row, jnp.zeros_like(row)), axis=1, keepdims=True)


def filter_kernel(
    groups, layers, state_hbm, tiles_hbm, weight_hbm, azimuth_hbm, value_hbm, var_hbm, tile_bin_hbm, bins_hbm,
    order_hbm, out_ref,
    tiles, weight, azimuth, values, variances, tile_bin, bins, order,
    own_sums, sums, own_obs, every_obs, own_taper, every_taper,
    held, weights, selects, value_cols, root_cols, var_rows, tile_weights, gathered,
    panel, solved_innov, upper, scaled_all, change_all,
    load_sem, sum_send, sum_recv, obs_send, obs_recv, taper_send, taper_recv, pass_send, pass_recv,
):
    me, layer = lax.axis_index("obs"), lax.axis_index("rows")
    feet = weight.shape[0]
    batches, per = own_obs.shape[0], own_obs.shape[1]
    count, nobs = bins.shape
    tiles_dev, half = tile_bin.shape[0], TILE // 2
    padded = var_rows.shape[0]

    pairs = [
        (order_hbm, order), (value_hbm, values), (var_hbm, variances), (azimuth_hbm, azimuth), (tiles_hbm, tiles),
        (tile_bin_hbm, tile_bin), (state_hbm, out_ref), (weight_hbm, weight), (bins_hbm, bins),
    ]
    loads = [pltpu.make_async_copy(source, target, load_sem.at[i]) for i, (source, target) in enumerate(pairs)]
    barrier = pltpu.get_barrier_semaphore()
    for k in range(1, groups):
        pl.semaphore_signal(barrier, inc=1, device_id={"obs": lax.rem(me + k, groups)}, device_id_type=MESH)
    for k in range(1, layers):
        pl.semaphore_signal(barrier, inc=1, device_id={"rows": lax.rem(layer + k, layers)}, device_id_type=MESH)
    for load in loads:
        load.start()
    for load in loads[:8]:
        load.wait()

    partial = [jnp.zeros((feet, MEMBERS), F32) for _ in range(2)]
    listed = [column_of(tiles[t : t + 1, :].astype(F32)).astype(jnp.int32) for t in range(tiles.shape[0])]
    for tile in range(tiles_dev):
        number = layer * tiles_dev + tile
        chosen = jnp.zeros((feet, TILE), F32)
        for t in range(tiles.shape[0]):
            chosen = chosen + jnp.where(listed[t] == number, weight[:, t, :], 0.0)
        for h in range(2):
            partial[h] = partial[h] + jnp.dot(
                chosen[:, h * half : (h + 1) * half],
                out_ref[pl.ds(tile * TILE + h * half, half), :],
                precision=HIGH,
                preferred_element_type=F32,
            )
    for h in range(2):
        own_sums[h] = partial[h]
    loads[8].wait()
    pl.semaphore_wait(barrier, groups + layers - 2)

    def sum_copy(k):
        return pltpu.make_async_remote_copy(
            own_sums, sums.at[k], sum_send.at[0], sum_recv.at[0],
            device_id={"rows": lax.rem(layer + k, layers)}, device_id_type=MESH,
        )

    def obs_copy(k, b):
        return pltpu.make_async_remote_copy(
            own_obs.at[b], every_obs.at[b, me], obs_send.at[0], obs_recv.at[b],
            device_id={"obs": lax.rem(me + k, groups)}, device_id_type=MESH,
        )

    partner = {"obs": me + 1 - 2 * (me % 2)}

    def taper_part(b, first, size):
        return every_taper.at[b, pl.ds(first, size), :, pl.ds(0, b * BATCH)]

    def taper_copy(k, b):
        wide = pl.ds(0, b * BATCH)
        return pltpu.make_async_remote_copy(
            own_taper.at[b, :, wide], every_taper.at[b, me, :, wide], taper_send.at[0], taper_recv.at[b - 1],
            device_id={"obs": lax.rem(me + 2 * k, groups)} if k is not None else partner, device_id_type=MESH,
        )

    def pass_copy(k, b):
        part = taper_part(b, lax.rem(me + 2 * k, groups), 1)
        return pltpu.make_async_remote_copy(
            part, part, pass_send.at[0], pass_recv.at[b - 1], device_id=partner, device_id_type=MESH,
        )

    def taper_copies(b):
        direct, passed = taper_part(b, 0, groups // 2), taper_part(b, 0, groups // 2 - 1)
        return [
            pltpu.make_async_remote_copy(part, part, send, recv, device_id=partner, device_id_type=MESH)
            for part, send, recv in (
                (direct, taper_send.at[0], taper_recv.at[b - 1]), (passed, pass_send.at[0], pass_recv.at[b - 1])
            )
        ]

    def all_obs(b):
        part = every_obs.at[b, pl.ds(0, groups - 1)]
        return pltpu.make_async_remote_copy(
            part, part, obs_send.at[0], obs_recv.at[b], device_id=partner, device_id_type=MESH,
        )

    def peers(action, last=groups):
        def one(k, carry):
            action(k)
            return carry

        lax.fori_loop(1, last, one, 0)

    for k in range(1, layers):
        sum_copy(k).start()

    order_rows = [order[pl.ds(BATCH * q, BATCH)].reshape(1, BATCH) for q in range(batches)]
    base = me * count
    order_wide = jnp.concatenate(order_rows, 1)
    steps = iota((count, nobs), 1).astype(F32)
    member = jnp.logical_and(order_wide >= base, order_wide < base + count).astype(F32)
    local = iota((count, 1), 0)
    at = jnp.sum(jnp.where(order_wide == base + local, steps, 0.0), axis=1, keepdims=True)
    rank = jnp.sum(jnp.where(steps < at, member, 0.0), axis=1, keepdims=True)
    square = (count, count)
    rank_row = jnp.sum(jnp.where(iota(square, 0) == iota(square, 1), rank, 0.0), axis=0, keepdims=True)
    chooser = (iota(square, 0).astype(F32) == rank_row).astype(F32)
    ranked = jnp.dot(
        chooser.astype(BF16), taper_weight(bins[...]).astype(BF16), preferred_element_type=F32
    )
    for n in range(batches - 1):
        rest = count - (n + 1) * per
        index = jnp.broadcast_to(order_rows[n], (rest, BATCH))
        block = lookup([ranked[count - rest :, q * BATCH : (q + 1) * BATCH] for q in range(batches)], index)
        for b in range(n + 1, batches):
            own_taper[b, :, n * BATCH : (n + 1) * BATCH] = block[(b - n - 1) * per : (b - n) * per, :]
    for b in range(1, batches):
        every_taper[b, me, :, : b * BATCH] = own_taper[b, :, : b * BATCH]
    for b in range(1, batches):
        taper_copy(None, b).start()
        peers(lambda k: taper_copy(k, b).start(), groups // 2)

    foot_of = (iota((count, feet), 0) // (count // feet) == iota((count, feet), 1)).astype(F32)
    spread_feet = jnp.dot(chooser.astype(BF16), foot_of.astype(BF16), preferred_element_type=F32).astype(BF16)
    angles = azimuth[...].reshape(1, count)
    cosines = jnp.sum(chooser * jnp.cos(angles), axis=1, keepdims=True)
    sines = jnp.sum(chooser * jnp.sin(angles), axis=1, keepdims=True)

    blank = [jnp.zeros((padded - batches, BATCH), jnp.int32)] if padded > batches else []
    orders = jnp.concatenate(order_rows + blank, 0)
    value_rows = lookup([values[pl.ds(BATCH * q, BATCH)].reshape(1, BATCH) for q in range(batches)], orders)
    variance_rows = lookup([variances[pl.ds(BATCH * q, BATCH)].reshape(1, BATCH) for q in range(batches)], orders)
    var_rows[...] = variance_rows
    for tile in range(tiles_dev):
        tapers = taper_weight(tile_bin[tile : tile + 1, :])
        tile_weights[tile] = lookup([tapers[:, q * BATCH : (q + 1) * BATCH] for q in range(batches)], orders)
    before = (iota((BATCH, BATCH), 0) < iota((BATCH, BATCH), 1)).astype(F32).astype(BF16)
    places = []
    for b in range(batches):
        group = order_rows[b] // count
        same = (iota((groups, BATCH), 0) == group).astype(F32)
        earlier = jnp.dot(same.astype(BF16), before, preferred_element_type=F32)
        places.append(group.astype(F32) * per + jnp.sum(same * earlier, axis=0, keepdims=True))
    empty = [jnp.zeros((padded - batches, BATCH), F32)] if padded > batches else []
    columns = jnp.transpose(jnp.concatenate(places + empty + [value_rows, jnp.sqrt(variance_rows)], 0))
    for b in range(batches):
        place = columns[:, b : b + 1]
        selects[b] = (place == iota((BATCH, BATCH), 1).astype(F32)).astype(F32).astype(BF16)
        value_cols[b] = columns[:, padded + b : padded + b + 1]
        root_cols[b] = jnp.broadcast_to(columns[:, 2 * padded + b : 2 * padded + b + 1], (BATCH, BATCH))

    part = sums.at[pl.ds(0, layers - 1)]
    all_sums = pltpu.make_async_remote_copy(
        part, part, sum_send.at[0], sum_recv.at[0],
        device_id={"rows": lax.rem(layer + 1, layers)}, device_id_type=MESH,
    )
    all_sums.wait_recv()
    winds = [own_sums[h] for h in range(2)]
    for k in range(1, layers):
        winds = [winds[h] + sums[k, h] for h in range(2)]
    winds = pick(spread_feet, jnp.concatenate(winds, 1))
    observed = model_function(winds[:, :MEMBERS], winds[:, MEMBERS:], cosines, sines)
    for b in range(batches):
        own_obs[b] = observed[b * per : (b + 1) * per, :]
        every_obs[b, me] = observed[b * per : (b + 1) * per, :]
    for b in range(batches):
        peers(lambda k: obs_copy(k, b).start())
    for b in range(1, batches):
        taper_copies(b)[0].wait_recv()
        peers(lambda k: pass_copy(k, b).start(), groups // 2)

    def arrive(b):
        all_obs(b).wait_recv()
        if b:
            taper_copies(b)[1].wait_recv()

    def prepare(b):
        rows = pl.ds(b * BATCH, BATCH)
        if per % SUB == 0:
            obs = every_obs[b].reshape(BATCH, MEMBERS)
            taper = every_taper[b].reshape(BATCH, nobs)
        else:
            for g in range(groups):
                gathered[g * per : (g + 1) * per, :MEMBERS] = every_obs[b, g]
                gathered[g * per : (g + 1) * per, MEMBERS:] = every_taper[b, g]
            obs, taper = gathered[:, :MEMBERS], gathered[:, MEMBERS:]
        select = selects[b]
        held[rows, :] = pick(select, obs)
        if b:
            known = taper[:, : b * BATCH].astype(BF16)
            weights[rows, : b * BATCH] = jnp.dot(select, known, preferred_element_type=F32)

    def members_of(place):
        kind, number = place
        return (held, number * BATCH, BATCH) if kind == "obs" else (out_ref, number * TILE, TILE)

    def weight_of(place, m):
        kind, number = place
        if kind == "obs":
            return weights[pl.ds(number * BATCH, BATCH), pl.ds(m * BATCH, BATCH)]
        return jnp.broadcast_to(tile_weights[number, pl.ds(m, 1), :], (TILE, BATCH))

    def load(places):
        values = []
        for place in places:
            ref, first, size = members_of(place)
            values.append(ref[pl.ds(first, size), :])
        return jnp.concatenate(values, 0)

    def store(places, value):
        done = 0
        for place in places:
            ref, first, size = members_of(place)
            ref[pl.ds(first, size), :] = value[done : done + size, :]
            done += size

    def measure(places, scaled, m):
        product = dot3(halves(load(places)), scaled, NT)
        return product * jnp.concatenate([weight_of(place, m) for place in places], 0)

    def lagged(places, m):
        product = []

        def first():
            scaled = (scaled_all[m, :, :MEMBERS], scaled_all[m, :, MEMBERS:])
            product.append(halves(measure(places, scaled, m)))

        def second():
            change = (change_all[m, :, :MEMBERS], change_all[m, :, MEMBERS:])
            store(places, load(places) + dot3(product[0], change, NN))

        return [first, second]

    eye = iota((BATCH, BATCH), 0) == iota((BATCH, BATCH), 1)
    states = [("state", tile) for tile in range(tiles_dev)]

    def gains(n, work, ahead):
        batch_obs = held[pl.ds(n * BATCH, BATCH), :]
        row_mean = jnp.mean(batch_obs, axis=1, keepdims=True)
        perturb = batch_obs - row_mean
        innov = value_cols[n] - row_mean
        innov_row = jnp.sum(jnp.where(eye, innov, 0.0), axis=0, keepdims=True)
        split = halves(perturb)
        scaled = halves(perturb * (1.0 / (MEMBERS - 1)))
        panel[:, :BATCH] = dot3(split, scaled, NT) + jnp.where(eye, var_rows[pl.ds(n, 1), :], 0.0)
        panel[:, BATCH:] = eye.astype(F32)
        scaled_all[n] = jnp.concatenate(scaled, 1)
        queue, slots, products = list(work), BATCH // SUB, []
        queue.append(lambda: products.append(halves(measure(ahead, scaled, n))))

        def fill(b):
            left = (slots - b) // 2
            if b % 2 and left:
                for _ in range(-(-len(queue) // left)):
                    queue.pop(0)()

        factor(panel, root_cols.at[n], innov_row, solved_innov, upper, fill)
        first = panel[:, :BATCH]
        middle = halves(solved_innov[...] - dot3(halves(panel[:, BATCH:]), split, NN))
        first = halves(first)
        rotated = halves(dot3(products[0], first, NT))
        store(ahead, load(ahead) + dot3(rotated, middle, NN))

        def change():
            change_all[n] = jnp.concatenate(halves(dot3(first, middle, TN)), 1)

        return change

    applied = [0] * batches
    arrive(0)
    prepare(0)
    change = None
    for n in range(batches):
        work = [change] if n else []
        if n == 0 and batches > 1:
            work = [lambda: None] * 3 + [functools.partial(arrive, 1), functools.partial(prepare, 1)]
        if n:
            for b in [2, 3] if n == 1 else [n + 2]:
                if b < batches:
                    arrive(b)
                    work.append(functools.partial(prepare, b))
            seen = [b for b in range(n + 1, min(n + 3, batches))]
            for m in range(n):
                places = [("obs", b) for b in seen if applied[b] <= m]
                if m == n - 1:
                    places = places + states
                for part in range(0, len(places), 2):
                    work += lagged(places[part : part + 2], m)
            for b in seen:
                applied[b] = n
        ahead = [("obs", n + 1)] if n + 1 < batches else states
        change = gains(n, work, ahead)
        if n + 1 < batches:
            applied[n + 1] = n + 1
    all_sums.wait_send()
    rows, wide = (batches - 1, batches) if batches % 2 == 0 else (batches, batches - 1)
    sent = [(every_obs.at[:, pl.ds(0, groups - 1)], obs_send)]
    for count, semaphore in ((groups // 2, taper_send), (groups // 2 - 1, pass_send)):
        sent.append((every_taper.at[pl.ds(0, rows), pl.ds(0, count), :, pl.ds(0, wide * BATCH // 2)], semaphore))
    for part, semaphore in sent:
        pltpu.make_async_remote_copy(
            part, part, semaphore.at[0], semaphore.at[0], device_id=partner, device_id_type=MESH
        ).wait_send()


def shards(state, foot_tiles, foot_weight, azimuth, obs_value, obs_var, tile_bin, obs_bin, order):
    groups, layers = lax.axis_size("obs"), lax.axis_size("rows")
    count, nobs = obs_bin.shape
    batches, feet, tiles_dev = nobs // BATCH, foot_tiles.shape[0], tile_bin.shape[0]
    per, padded = count // batches, (nobs // BATCH + SUB - 1) // SUB * SUB
    dma, vmem = pltpu.SemaphoreType.DMA, pltpu.VMEM
    return pl.pallas_call(
        functools.partial(filter_kernel, groups, layers),
        out_shape=jax.ShapeDtypeStruct(state.shape, F32),
        in_specs=[ANY] * 9,
        out_specs=VMEM,
        scratch_shapes=[
            vmem(foot_tiles.shape[::-1], jnp.int32), vmem(foot_weight.shape, F32), vmem((count,), F32),
            vmem((nobs,), F32), vmem((nobs,), F32), vmem(tile_bin.shape, jnp.int32), vmem(obs_bin.shape, jnp.int32),
            vmem((nobs,), jnp.int32),
            vmem((2, feet, MEMBERS), F32), vmem((layers, 2, feet, MEMBERS), F32),
            vmem((batches, per, MEMBERS), F32), vmem((batches, groups, per, MEMBERS), F32),
            vmem((batches, per, nobs), F32), vmem((batches, groups, per, nobs), F32),
            vmem((nobs, MEMBERS), F32), vmem((nobs, nobs), F32), vmem((batches, BATCH, BATCH), BF16),
            vmem((batches, BATCH, 1), F32), vmem((batches, BATCH, BATCH), F32), vmem((padded, BATCH), F32),
            vmem((tiles_dev, padded, BATCH), F32), vmem((BATCH, MEMBERS + nobs), F32),
            vmem((BATCH, 2 * BATCH), F32), vmem((BATCH, 1), F32), vmem((SPAN, BATCH), F32),
            vmem((batches, BATCH, 2 * MEMBERS), BF16), vmem((batches, BATCH, 2 * MEMBERS), BF16),
            dma((9,)), dma((1,)), dma((1,)), dma((1,)), dma((batches,)), dma((1,)), dma((batches - 1,)), dma((1,)), dma((batches - 1,)),
        ],
        compiler_params=pltpu.CompilerParams(
            collective_id=0, has_side_effects=True, vmem_limit_bytes=48 * 1024 * 1024
        ),
    )(*(
        pltpu.with_memory_space_constraint(array, pltpu.MemorySpace.HBM)
        for array in (state, foot_tiles.T, foot_weight, azimuth, obs_value, obs_var, tile_bin, obs_bin, order)
    ))


def solution(mesh):
    return jax.shard_map(
        shards,
        mesh=mesh,
        in_specs=(
            P(("obs", "rows"), None),
            P("obs", None),
            P("obs", None, None),
            P("obs"),
            P(),
            P(),
            P(("obs", "rows"), None),
            P("obs", None),
            P(),
        ),
        out_specs=P(("obs", "rows"), None),
        check_vma=False,
    )
```
